128 devices in a mesh: rows: 128 (over x, y, z, core).
Axes of the slice: x: 4, y: 4, z: 4, core: 2. Of those that a mesh axis runs over, the one named last changes fastest.
Arguments:
- source: float32 [512, 2048], P('rows'), may hold values from -60 to 60
- observed: float32 [512, 2048], P('rows'), may hold values from -4 to 4
- precision: float32 [512, 2048], P('rows'), may hold values from 1 to 10
- conductivity: float32 [512, 2048], P('rows'), may hold values from 0.5 to 2
- log_field: float32 [16, 512, 2048], P(None, 'rows'), may hold values from -4 to 4
- noise_field: float32 [16, 512, 2048], P(None, 'rows'), may hold values from -6 to 6
- subspace_noise: float32 [16, 256], replicated, may hold values from -6 to 6
- eigenvalues: float32 [256], replicated, may hold values from 0.1 to 100
- basis: bfloat16 [256, 512, 2048], P(None, 'rows'), may hold values from -0.0234375 to 0.0234375
Outputs:
- proposal: float32 [16, 512, 2048], P(None, 'rows')
- new_coef: float32 [16, 256], replicated
The draws below stay inside these ranges and needn't reach their ends.
All inputs are finite; a program needn't handle non-finite values.
Results may differ from the reference program's by a relative error of at most 0.0003.
The reference program's roundings to bfloat16 on the way (of `correction`) count: a program that leaves them out, or rounds other values in their place, can miss the bound.
Values sent between devices are 32-bit elements; how exact they have to be, the bound alone decides.
A program may use at most 64 MiB of HBM per device.

```python
import math
import jax
import jax.numpy as jnp
from jax import lax

ROWS_DEV = 4
NY = 2048
CHAINS = 16
RANK = 256
ITERS = 4
NX = 512
N_ROWS = 128


def draw_source(key, part):
    positions = jnp.arange(NX, dtype=jnp.float32)[:, None]
    fraction = positions / float(max(NX - 1, 1))
    base = jnp.clip(jax.random.normal(key, (NX, NY), jnp.float32), -6.0, 6.0)
    growth = jnp.exp(jnp.log(5.0) * fraction)
    return base * growth


def raised(entries, own_key, source, target, blocks, factor):
    owner, partner = [(jnp.arange(entries.shape[axis_at]) // (entries.shape[axis_at] // blocks)).reshape([-1 if axis == axis_at else 1 for axis in range(entries.ndim)]) for axis_at in (source, target)]
    chosen = jax.random.permutation(own_key, blocks)[partner]
    strong = (owner == chosen) | (owner == (partner + blocks // 2) % blocks)
    return jnp.where(strong, factor * entries, entries)


def steps_of(own_key, extent, cuts, smallest, high):
    def one(axis_at, parts):
        draws = jax.random.uniform(jax.random.fold_in(jax.random.fold_in(own_key, 6), axis_at), (parts,), jnp.float32, smallest / len(cuts), high / len(cuts))
        return jnp.repeat(jnp.exp(draws), extent[axis_at] // parts).reshape((-1,) + (1,) * (len(extent) - axis_at - 1))

    factor_of = one(*cuts[0])
    for cut in cuts[1:]:
        factor_of = factor_of * one(*cut)
    return factor_of


def noise(key, extent, width, most, cuts=(), held_as=jnp.bfloat16):
    drawn = jax.random.normal(key, extent, jnp.float32) * width
    if len(cuts) > 0:
        drawn = steps_of(key, extent, cuts, -0.22, 0.18) * drawn
    return jnp.clip(drawn, min=-most, max=most).astype(held_as)


def noise_with(own_key, extent, scale, limit, split, heavy, held_as=jnp.bfloat16):
    values = scale * jax.random.normal(own_key, extent, jnp.float32)
    if split:
        values = values * steps_of(own_key, extent, split, -0.22, 0.18)
    return jnp.clip(raised(values, jax.random.fold_in(own_key, 3), *heavy), -limit, limit).astype(held_as)


def setup_inputs(seed: int = 0) -> dict:
    streams_of = jax.random.split(jax.random.key(seed), 10)
    source = draw_source(jax.random.fold_in(streams_of[9], 71), 0)
    observed = noise(streams_of[1], (NX, NY), 0.3, 4.0, ((0, 128),), jnp.float32)
    precision = jnp.clip(jnp.exp(math.log(10.0) - 2.3025851 * jax.random.uniform(streams_of[2], (NX, NY), jnp.float32) ** steps_of(streams_of[2], (NX, NY), ((0, 128),), -0.2, 0.2)), 1.0, 10.0)
    conductivity = jnp.clip(jnp.exp(math.log(2.0) - 1.3862944 * jax.random.uniform(streams_of[3], (NX, NY), jnp.float32) ** steps_of(streams_of[3], (NX, NY), ((0, 128),), -0.2, 0.2)), 0.5, 2.0)
    log_field = noise(streams_of[4], (CHAINS, NX, NY), 0.7, 4.0, ((1, 128),), jnp.float32)
    noise_field = noise(streams_of[5], (CHAINS, NX, NY), 1.0, 6.0, ((1, 128),), jnp.float32)
    subspace_noise = noise(streams_of[6], (CHAINS, RANK), 1.0, 6.0, (), jnp.float32)
    eigenvalues = jnp.clip(jnp.exp(jax.random.uniform(streams_of[7], (RANK,), jnp.float32, math.log(0.1), math.log(100.0))), 0.1, 100.0)
    basis = noise_with(streams_of[8], (RANK, NX, NY), (NX * NY) ** -0.5, 0.0234375, ((1, 128),), (1, 0, 128, 5.5))
    return {"source": source, "observed": observed, "precision": precision, "conductivity": conductivity, "log_field": log_field, "noise_field": noise_field, "subspace_noise": subspace_noise, "eigenvalues": eigenvalues, "basis": basis}


def edge_weights(conductivity):
    padded = jnp.pad(conductivity, 1, mode='edge')
    return (0.5 * (conductivity + padded[:-2, 1:-1]), 0.5 * (conductivity + padded[2:, 1:-1]), 0.5 * (conductivity + padded[1:-1, :-2]), 0.5 * (conductivity + padded[1:-1, 2:]))

def apply_operator(field, weights, diagonal):
    padded = jnp.pad(field, ((0, 0), (1, 1), (1, 1)))
    beside_all = weights[0] * padded[:, :-2, 1:-1] + weights[1] * padded[:, 2:, 1:-1]
    beside_all = beside_all + weights[2] * padded[:, 1:-1, :-2] + weights[3] * padded[:, 1:-1, 2:]
    return diagonal * field - beside_all

def chain_dot(left, right):
    return lax.optimization_barrier(jnp.sum(left * right, axis=(1, 2)))

def broadcast_chain(values):
    return values[:, None, None]

def solve(right_side, weights, diagonal):
    solution = jnp.zeros_like(right_side)
    residual = right_side
    scaled = residual / diagonal
    direction = scaled
    current = chain_dot(residual, scaled)
    for iteration in range(ITERS):
        applied = apply_operator(direction, weights, diagonal)
        step_length = current / chain_dot(direction, applied)
        solution = solution + broadcast_chain(step_length) * direction
        residual = residual - broadcast_chain(step_length) * applied
        scaled = residual / diagonal
        following = chain_dot(residual, scaled)
        direction = scaled + broadcast_chain(following / current) * direction
        current = following
    return solution

def project(fields, basis):
    rounded = fields.astype(jnp.bfloat16)

    def accumulate(block, total):
        start = (block * ROWS_DEV).astype(jnp.int32)
        piece = lax.dynamic_slice_in_dim(rounded, start, ROWS_DEV, 1).astype(jnp.float32)
        basis_rows = lax.dynamic_slice_in_dim(basis, start, ROWS_DEV, 1).astype(jnp.float32)
        return total + jnp.einsum('cxy,rxy->cr', piece, basis_rows, precision=lax.Precision.HIGHEST)
    return lax.fori_loop(jnp.int32(0), jnp.int32(N_ROWS), accumulate, jnp.zeros((fields.shape[0], basis.shape[0]), jnp.float32))

def rebuild(correction, basis):
    weights_f = correction.astype(jnp.float32)

    def one_block(block):
        start = (block * ROWS_DEV).astype(jnp.int32)
        basis_rows = lax.dynamic_slice_in_dim(basis, start, ROWS_DEV, 1).astype(jnp.float32)
        return jnp.einsum('cr,rxy->cxy', weights_f, basis_rows, precision=lax.Precision.HIGHEST)
    blocks = lax.map(one_block, jnp.arange(N_ROWS, dtype=jnp.int32))
    return jnp.transpose(blocks, (1, 0, 2, 3)).reshape(correction.shape[0], NX, NY)

def reference(source, observed, precision, conductivity, log_field, noise_field, subspace_noise, eigenvalues, basis):
    weights = edge_weights(conductivity)
    reaction = jnp.exp(log_field)
    diagonal = weights[0] + weights[1] + weights[2] + weights[3] + reaction
    forward_side = jnp.broadcast_to(source, log_field.shape)
    state = solve(forward_side, weights, diagonal)
    adjoint = solve(precision * (state - observed), weights, diagonal)
    gradient = -reaction * adjoint * state
    chains = log_field.shape[0]
    coefs = project(jnp.concatenate([log_field, noise_field, gradient], 0), basis)
    state_coef = coefs[:chains]
    noise_coef = coefs[chains:2 * chains]
    grad_coef = coefs[2 * chains:]
    variance = 1.0 / (1.0 + eigenvalues)
    keep_factor = (2.0 - 0.8 * variance) / (2.0 + 0.8 * variance)
    drift_factor = 1.6 * variance / (2.0 + 0.8 * variance)
    noise_factor = jnp.sqrt(6.4 * variance) / (2.0 + 0.8 * variance)
    new_coef = keep_factor * state_coef - drift_factor * grad_coef + noise_factor * subspace_noise
    correction = (new_coef - 0.6 * state_coef - 0.8 * noise_coef).astype(jnp.bfloat16)
    proposal = 0.6 * log_field + 0.8 * noise_field + rebuild(correction, basis)
    return (proposal, new_coef)
```

```python
import functools

import jax
import jax.numpy as jnp
from jax import lax
from jax.experimental import pallas as pl
from jax.experimental.pallas import tpu as pltpu
from jax.sharding import PartitionSpec as P

ITERS = 4
AXIS = "rows"
N = 128
RD = 4
NY = 2048
CH = 16
EXT = 12
TILES = NY // 128
MESH_ID = pl.DeviceIdType.MESH
F32 = jnp.float32


def greet_all(me):
    barrier = pltpu.get_barrier_semaphore()

    def signal(step, carry):
        pl.semaphore_signal(barrier, inc=1, device_id=(lax.rem(me + step, N),), device_id_type=MESH_ID)
        return carry

    lax.fori_loop(1, N, signal, 0)
    return barrier


def send_row_to_all(me, buf, send_sem, recv_sem):
    def send(step, carry):
        pltpu.make_async_remote_copy(
            src_ref=buf.at[me], dst_ref=buf.at[me], send_sem=send_sem, recv_sem=recv_sem,
            device_id=(lax.rem(me + step, N),), device_id_type=MESH_ID,
        ).start()
        return carry

    lax.fori_loop(1, N, send, 0, unroll=8)


def wait_rows(buf, sem):
    part = buf.at[pl.ds(0, N - 1)]
    pltpu.make_async_copy(part, part, sem).wait()


def pack(accs):
    lane = lax.broadcasted_iota(jnp.int32, (8, 128), 1)
    sub = lax.broadcasted_iota(jnp.int32, (8, 128), 0)
    row = jnp.zeros((8, 128), F32)
    for k in range(8):
        for g in range(2):
            total = jnp.sum(accs[k][g], axis=1, keepdims=True)
            row = row + jnp.where(lane == (g * 8 + k) * 8 + sub, total, 0.0)
    return jnp.sum(row, axis=0, keepdims=True)


def unpack(row):
    lane = lax.broadcasted_iota(jnp.int32, (8, 128), 1)
    sub = lax.broadcasted_iota(jnp.int32, (8, 128), 0)
    wide = jnp.broadcast_to(row, (8, 128))
    moments = []
    for k in range(8):
        halves = [
            jnp.sum(jnp.where(lane == (g * 8 + k) * 8 + sub, wide, 0.0), axis=1, keepdims=True)
            for g in range(2)
        ]
        moments.append(jnp.concatenate(halves, axis=0))
    return moments


def square(poly):
    out = [None] * (2 * len(poly) - 1)
    for i, a in enumerate(poly):
        for j, b in enumerate(poly):
            term = a * b
            out[i + j] = term if out[i + j] is None else out[i + j] + term
    return out


def krylov_weights(m):
    one = jnp.ones_like(m[0])
    rho, pi = [one], [one]
    y = [jnp.zeros_like(one)] * ITERS
    g = m[0]
    spread = g
    gain, noise = None, None
    for step in range(ITERS):
        s = square(pi)
        c = functools.reduce(lambda a, b: a + b, [s[l] * (m[l] - m[l + 1]) for l in range(len(s))])
        size = functools.reduce(
            lambda a, b: a + b, [jnp.abs(s[l]) * (jnp.abs(m[l]) + jnp.abs(m[l + 1])) for l in range(len(s))]
        )
        alpha = g / c
        part = alpha * g
        err = part * ((size / c) * (size / c) + (spread / g) * (spread / g))
        gain = part if gain is None else gain + part
        noise = err if noise is None else noise + err
        for k in range(len(pi)):
            y[k] = y[k] + alpha * pi[k]
        if step == ITERS - 1:
            break
        new = []
        for k in range(len(pi) + 1):
            value = rho[k] if k < len(rho) else None
            if k < len(pi):
                value = value - alpha * pi[k]
            if k > 0:
                moved = alpha * pi[k - 1]
                value = moved if value is None else value + moved
            new.append(value)
        rho = new
        s = square(rho)
        following = functools.reduce(lambda a, b: a + b, [s[l] * m[l] for l in range(len(s))])
        spread = functools.reduce(lambda a, b: a + b, [jnp.abs(s[l]) * jnp.abs(m[l]) for l in range(len(s))])
        beta = following / g
        g = following
        pi = [rho[k] + beta * pi[k] if k < len(pi) else rho[k] for k in range(len(rho))]
    return y, noise / gain


def apply_row(vk, vn, wu, wl, dinv, e, g, lane, accs, store):
    gs = pl.ds(8 * g, 8)

    def tile(ref, row, j, rows=gs):
        return ref[row, rows, pl.ds(128 * j, 128)]

    whole = pl.ds(0, 8)
    v_at = {}
    q_at = {}
    r_at = {}
    rq_at = {}

    def prepare(j):
        v = tile(vk, e, j)
        w = tile(wl, e, j, whole)
        v_at[j] = v
        q_at[j] = w
        r_at[j] = pltpu.roll(v, 1, 1)
        rq_at[j] = pltpu.roll(w * v, 127, 1)

    prepare(0)
    for j in range(TILES):
        if j + 1 < TILES:
            prepare(j + 1)
        left = r_at[j] if j == 0 else jnp.where(lane == 0, r_at[j - 1], r_at[j])
        right = jnp.where(lane == 127, rq_at[j + 1] if j + 1 < TILES else 0.0, rq_at[j])
        t = tile(wu, e, j, whole) * tile(vk, e - 1, j) + tile(wu, e + 1, j, whole) * tile(vk, e + 1, j)
        t = t + (q_at[j] * left + right)
        v = v_at[j]
        if accs is not None:
            accs = (accs[0] + t * v, accs[1])
        if store:
            new = t * tile(dinv, e, j)
            vn[e, gs, pl.ds(128 * j, 128)] = new
            if accs is not None:
                accs = (accs[0], accs[1] + t * new)
    return accs


def powers_own(v, k, wu, wl, dinv, lane):
    zero = jnp.zeros((8, 128), F32)
    store = k < ITERS - 1
    vk = v.at[k]
    vn = v.at[k + 1] if store else None

    def row(e, carry):
        return tuple(apply_row(vk, vn, wu, wl, dinv, e, g, lane, carry[g], store) for g in range(2))

    got = lax.fori_loop(RD, 2 * RD, row, ((zero, zero), (zero, zero)))
    return [got[0][0], got[1][0]], [got[0][1], got[1][1]]


def powers_halo(v, k, wu, wl, dinv, lane, lo, hi):
    vk, vn = v.at[k], v.at[k + 1]

    def row(i, carry):
        for e in (i, EXT - 1 - i):
            for g in range(2):
                apply_row(vk, vn, wu, wl, dinv, e, g, lane, None, True)
        return carry

    lax.fori_loop(lo, hi, row, 0)


def field_kernel(
    source, observed, precision, conductivity, log_rows, grad_ref, info_ref,
    lf, dinv, v, wu, wl, ws, sx, ox, px, state, cb, sb, ob, pb, mom_a, mom_b,
    local_sem, send_sem, recv_sem, all_sem,
):
    me = lax.axis_index(AXIS)
    own = [
        pltpu.make_async_copy(log_rows, lf.at[pl.ds(RD, RD)], local_sem.at[0]),
        pltpu.make_async_copy(conductivity, cb.at[2], local_sem.at[1]),
        pltpu.make_async_copy(source, sb.at[1], local_sem.at[2]),
        pltpu.make_async_copy(observed, ob.at[1], local_sem.at[3]),
        pltpu.make_async_copy(precision, pb.at[1], local_sem.at[4]),
    ]
    for copy in own:
        copy.start()
    barrier = greet_all(me)
    for copy in own:
        copy.wait()
    pl.semaphore_wait(barrier, N - 1)

    count = [0]

    def remote(src, dst, shift):
        index = count[0]
        count[0] += 1
        copy = pltpu.make_async_remote_copy(
            src_ref=src, dst_ref=dst, send_sem=send_sem.at[index], recv_sem=recv_sem.at[index],
            device_id=(lax.rem(me + shift + N, N),), device_id_type=MESH_ID,
        )
        copy.start()
        return copy

    early = []
    for block, src, centre in ((cb, 2, 2), (sb, 1, 1)):
        early.append(remote(block.at[src], block.at[centre - 1], 1))
        early.append(remote(block.at[src], block.at[centre + 1], -1))
    early.append(remote(cb.at[2], cb.at[0], 2))
    early.append(remote(cb.at[2], cb.at[4], -2))
    rows = []
    for i in range(RD):
        rows.append(
            (
                remote(lf.at[2 * RD - 1 - i], lf.at[RD - 1 - i], 1),
                remote(lf.at[RD + i], lf.at[2 * RD + i], -1),
            )
        )
    late = []
    for block in (ob, pb):
        late.append(remote(block.at[1], block.at[0], 1))
        late.append(remote(block.at[1], block.at[2], -1))

    for copy in early:
        copy.wait()

    lane = lax.broadcasted_iota(jnp.int32, (8, 128), 1)
    first = jnp.where(me == 0, 0.0, 1.0).astype(F32)
    last = jnp.where(me == N - 1, 0.0, 1.0).astype(F32)
    col = lax.broadcasted_iota(jnp.int32, (1, NY), 1)

    def crow(e):
        return cb[e // RD + 1, pl.ds(e % RD, 1), :]

    def edge(e):
        a, b = crow(e - 1), crow(e)
        if e == RD:
            a = first * a + (1.0 - first) * b
        if e == 2 * RD:
            b = last * b + (1.0 - last) * a
        return 0.5 * (a + b)

    for e in range(EXT + 1):
        wu[e] = jnp.broadcast_to(edge(e), (8, NY))
    for e in range(EXT):
        c = crow(e)
        before = jnp.where(col == 0, c, pltpu.roll(c, 1, 1))
        after = jnp.where(col == NY - 1, c, pltpu.roll(c, NY - 1, 1))
        left = 0.5 * (c + before)
        right = 0.5 * (c + after)
        wl[e] = jnp.broadcast_to(jnp.where(col == 0, 0.0, left), (8, NY))
        ws[e] = jnp.broadcast_to(left + right, (8, NY)) + wu[e] + wu[e + 1]
        sx[e] = jnp.broadcast_to(sb[e // RD, pl.ds(e % RD, 1), :], (8, NY))

    def start_row(e, keep):
        for g in range(2):
            gs = pl.ds(8 * g, 8)
            d = keep / (ws[e] + jnp.exp(lf[e, gs, :]))
            dinv[e, gs, :] = d
            v[0, e, gs, :] = sx[e] * d

    def own_start(e, carry):
        start_row(e, jnp.float32(1.0))
        return carry

    lax.fori_loop(RD, 2 * RD, own_start, 0)
    for i, (above, below) in enumerate(rows):
        above.wait()
        below.wait()
        start_row(RD - 1 - i, first)
        start_row(2 * RD + i, last)

    def moments_zero(side):
        zero = jnp.zeros((8, 128), F32)

        def row(e, carry):
            out = []
            for g in range(2):
                acc = carry[g]
                for j in range(TILES):
                    sl = pl.ds(128 * j, 128)
                    acc = acc + side(e, g, sl) * v[0, e, pl.ds(8 * g, 8), sl]
                out.append(acc)
            return tuple(out)

        return list(lax.fori_loop(RD, 2 * RD, row, (zero, zero)))

    accs = [moments_zero(lambda e, g, sl: sx[e, :, sl])]
    moved = []
    for k in range(ITERS):
        one, two = powers_own(v, k, wu, wl, dinv, lane)
        accs.append(one)
        if k < ITERS - 1:
            accs.append(two)
            moved.append(remote(v.at[k + 1, RD], v.at[k + 1, 0], 1))
            moved.append(remote(v.at[k + 1, 2 * RD - 1], v.at[k + 1, EXT - 1], -1))
            powers_halo(v, k, wu, wl, dinv, lane, k + 1, RD)
    mom_a[me] = pack(accs)
    send_row_to_all(me, mom_a, all_sem.at[0], all_sem.at[1])

    for copy in late:
        copy.wait()
    for e in range(EXT):
        ox[e] = jnp.broadcast_to(ob[e // RD, pl.ds(e % RD, 1), :], (8, NY))
        px[e] = jnp.broadcast_to(pb[e // RD, pl.ds(e % RD, 1), :], (8, NY))
    moved[0].wait()
    moved[1].wait()
    powers_halo(v, 1, wu, wl, dinv, lane, 1, 2)
    moved[2].wait()
    moved[3].wait()
    powers_halo(v, 2, wu, wl, dinv, lane, 1, 3)
    moved[4].wait()
    moved[5].wait()

    wait_rows(mom_a, all_sem.at[1])
    y, info = krylov_weights(unpack(jnp.sum(mom_a[...], axis=0)))
    info_ref[0] = jnp.broadcast_to(info, (CH, 128))

    def adjoint_start(e, carry):
        out = []
        for g in range(2):
            acc = carry[g]
            gs = pl.ds(8 * g, 8)
            yg = [jnp.broadcast_to(y[k][8 * g:8 * g + 8], (8, 128)) for k in range(ITERS)]
            for j in range(TILES):
                sl = pl.ds(128 * j, 128)
                x = yg[0] * v[0, e, gs, sl]
                for k in range(1, ITERS):
                    x = x + yg[k] * v[k, e, gs, sl]
                side = px[e, :, sl] * (x - ox[e, :, sl])
                new = side * dinv[e, gs, sl]
                state[e, gs, sl] = x
                v[0, e, gs, sl] = new
                acc = acc + side * new
            out.append(acc)
        return tuple(out)

    zero = jnp.zeros((8, 128), F32)
    lax.fori_loop(0, RD, adjoint_start, (zero, zero))
    lax.fori_loop(2 * RD, EXT, adjoint_start, (zero, zero))
    accs = [list(lax.fori_loop(RD, 2 * RD, adjoint_start, (zero, zero)))]
    for k in range(ITERS):
        one, two = powers_own(v, k, wu, wl, dinv, lane)
        accs.append(one)
        if k < ITERS - 1:
            accs.append(two)
            powers_halo(v, k, wu, wl, dinv, lane, k + 1, RD)
    mom_b[me] = pack(accs)
    send_row_to_all(me, mom_b, all_sem.at[2], all_sem.at[3])
    wait_rows(mom_b, all_sem.at[3])
    y, info = krylov_weights(unpack(jnp.sum(mom_b[...], axis=0)))
    info_ref[1] = jnp.broadcast_to(info, (CH, 128))

    def gradient(r, carry):
        for h in range(4):
            sl = pl.ds(512 * h, 512)
            adj = y[0] * v[0, r + RD, :, sl]
            for k in range(1, ITERS):
                adj = adj + y[k] * v[k, r + RD, :, sl]
            value = -jnp.exp(lf[r + RD, :, sl]) * adj * state[r + RD, :, sl]
            grad_ref[r, :, sl] = value.astype(jnp.bfloat16)
        return carry

    lax.fori_loop(0, RD, gradient, 0)
    wait_rows(mom_a, all_sem.at[0])
    wait_rows(mom_b, all_sem.at[2])


def solve_fields(source, observed, precision, conductivity, log_rows):
    any_space = pl.BlockSpec(memory_space=pl.ANY)
    vmem = pl.BlockSpec(memory_space=pltpu.VMEM)
    wide = pltpu.VMEM((EXT, CH, NY), F32)
    row8 = pltpu.VMEM((EXT, 8, NY), F32)
    small = pltpu.VMEM((3, RD, NY), F32)
    return pl.pallas_call(
        field_kernel,
        out_shape=(
            jax.ShapeDtypeStruct((RD, CH, NY), jnp.bfloat16),
            jax.ShapeDtypeStruct((2, CH, 128), F32),
        ),
        in_specs=[any_space] * 5,
        out_specs=(vmem, vmem),
        scratch_shapes=[
            wide, wide, pltpu.VMEM((ITERS, EXT, CH, NY), F32),
            pltpu.VMEM((EXT + 1, 8, NY), F32), row8, row8, row8, row8, row8, wide,
            pltpu.VMEM((5, RD, NY), F32), small, small, small,
            pltpu.VMEM((N, 1, 128), F32), pltpu.VMEM((N, 1, 128), F32),
            pltpu.SemaphoreType.DMA((5,)),
            pltpu.SemaphoreType.DMA((24,)),
            pltpu.SemaphoreType.DMA((24,)),
            pltpu.SemaphoreType.DMA((4,)),
        ],
        compiler_params=pltpu.CompilerParams(
            collective_id=0, has_side_effects=True, vmem_limit_bytes=40 << 20
        ),
    )(source, observed, precision, conductivity, log_rows)


def sum_kernel(part, total, got, mine, sems):
    me = lax.axis_index(AXIS)
    barrier = greet_all(me)
    pl.semaphore_wait(barrier, N - 1)

    def send(step, carry):
        to = lax.rem(me + step, N)
        pltpu.make_async_remote_copy(
            src_ref=part.at[to], dst_ref=got.at[me], send_sem=sems.at[0], recv_sem=sems.at[1],
            device_id=(to,), device_id_type=MESH_ID,
        ).start()
        return carry

    lax.fori_loop(1, N, send, 0, unroll=8)
    got[me] = part[me]
    wait_rows(got, sems.at[1])
    mine[me] = jnp.sum(got[...], axis=0)
    send_row_to_all(me, mine, sems.at[2], sems.at[3])
    wait_rows(mine, sems.at[3])
    total[...] = mine[...]
    wait_rows(got, sems.at[0])
    wait_rows(mine, sems.at[2])


def sum_all(coefs):
    flat = jnp.pad(coefs.reshape(N, 1, -1), ((0, 0), (0, 0), (0, 32)))
    vmem = pl.BlockSpec(memory_space=pltpu.VMEM)
    total = pl.pallas_call(
        sum_kernel,
        out_shape=jax.ShapeDtypeStruct((N, 1, 128), F32),
        in_specs=[vmem],
        out_specs=vmem,
        scratch_shapes=[
            pltpu.VMEM((N, 1, 128), F32), pltpu.VMEM((N, 1, 128), F32), pltpu.SemaphoreType.DMA((4,)),
        ],
        compiler_params=pltpu.CompilerParams(collective_id=1, has_side_effects=True),
    )(flat)
    return total[:, :, :96].reshape(coefs.shape)


def per_device(
    source, observed, precision, conductivity, log_field, noise_field, subspace_noise, eigenvalues, basis,
):
    log_rows = jnp.transpose(log_field, (1, 0, 2))
    gradient, info = solve_fields(source, observed, precision, conductivity, log_rows)
    gradient = jnp.transpose(gradient, (1, 0, 2))
    stacked = jnp.concatenate(
        [log_field.astype(jnp.bfloat16), noise_field.astype(jnp.bfloat16), gradient], 0
    )
    part = jnp.einsum("cxy,rxy->cr", stacked, basis, preferred_element_type=F32)
    coefs = sum_all(part)
    state_coef, noise_coef, grad_coef = coefs[:CH], coefs[CH : 2 * CH], coefs[2 * CH :]
    variance = 1.0 / (1.0 + eigenvalues)
    keep_factor = (2.0 - 0.8 * variance) / (2.0 + 0.8 * variance)
    drift_factor = 1.6 * variance / (2.0 + 0.8 * variance)
    noise_factor = jnp.sqrt(6.4 * variance) / (2.0 + 0.8 * variance)
    new_coef = keep_factor * state_coef - drift_factor * grad_coef + noise_factor * subspace_noise
    correction = (new_coef - 0.6 * state_coef - 0.8 * noise_coef).astype(jnp.bfloat16)
    rebuilt = jnp.einsum("cr,rxy->cxy", correction, basis, preferred_element_type=F32)
    proposal = 0.6 * log_field + 0.8 * noise_field + rebuilt
    return (proposal, new_coef)


def solution(mesh):
    return jax.shard_map(
        per_device,
        mesh=mesh,
        in_specs=(
            P(AXIS, None), P(AXIS, None), P(AXIS, None), P(AXIS, None),
            P(None, AXIS, None), P(None, AXIS, None), P(), P(), P(None, AXIS, None),
        ),
        out_specs=(P(None, AXIS, None), P()),
        check_vma=False,
    )
```

```python
import functools

import jax
import jax.numpy as jnp
from jax import lax
from jax.experimental import pallas as pl
from jax.experimental.pallas import tpu as pltpu
from jax.sharding import PartitionSpec as P

ITERS = 4
AXIS = "rows"
N = 128
RD = 4
NY = 2048
CH = 16
EXT = 12
TILES = NY // 128
MESH_ID = pl.DeviceIdType.MESH
F32 = jnp.float32


def greet_all(me):
    barrier = pltpu.get_barrier_semaphore()

    def signal(step, carry):
        pl.semaphore_signal(barrier, inc=1, device_id=(lax.rem(me + step, N),), device_id_type=MESH_ID)
        return carry

    lax.fori_loop(1, N, signal, 0)
    return barrier


def send_row_to_all(me, buf, send_sem, recv_sem):
    def send(step, carry):
        pltpu.make_async_remote_copy(
            src_ref=buf.at[me], dst_ref=buf.at[me], send_sem=send_sem, recv_sem=recv_sem,
            device_id=(lax.rem(me + step, N),), device_id_type=MESH_ID,
        ).start()
        return carry

    lax.fori_loop(1, N, send, 0, unroll=8)


def wait_rows(buf, sem):
    part = buf.at[pl.ds(0, N - 1)]
    pltpu.make_async_copy(part, part, sem).wait()


def pack(accs):
    lane = lax.broadcasted_iota(jnp.int32, (8, 128), 1)
    sub = lax.broadcasted_iota(jnp.int32, (8, 128), 0)
    row = jnp.zeros((8, 128), F32)
    for k in range(8):
        for g in range(2):
            total = jnp.sum(accs[k][g], axis=1, keepdims=True)
            row = row + jnp.where(lane == (g * 8 + k) * 8 + sub, total, 0.0)
    return jnp.sum(row, axis=0, keepdims=True)


def unpack(row):
    lane = lax.broadcasted_iota(jnp.int32, (8, 128), 1)
    sub = lax.broadcasted_iota(jnp.int32, (8, 128), 0)
    wide = jnp.broadcast_to(row, (8, 128))
    moments = []
    for k in range(8):
        halves = [
            jnp.sum(jnp.where(lane == (g * 8 + k) * 8 + sub, wide, 0.0), axis=1, keepdims=True)
            for g in range(2)
        ]
        moments.append(jnp.concatenate(halves, axis=0))
    return moments


def square(poly):
    out = [None] * (2 * len(poly) - 1)
    for i, a in enumerate(poly):
        for j, b in enumerate(poly):
            term = a * b
            out[i + j] = term if out[i + j] is None else out[i + j] + term
    return out


def krylov_weights(m):
    one = jnp.ones_like(m[0])
    rho, pi = [one], [one]
    y = [jnp.zeros_like(one)] * ITERS
    g = m[0]
    spread = g
    gain, noise = None, None
    for step in range(ITERS):
        s = square(pi)
        c = functools.reduce(lambda a, b: a + b, [s[l] * (m[l] - m[l + 1]) for l in range(len(s))])
        size = functools.reduce(
            lambda a, b: a + b, [jnp.abs(s[l]) * (jnp.abs(m[l]) + jnp.abs(m[l + 1])) for l in range(len(s))]
        )
        alpha = g / c
        part = alpha * g
        err = part * ((size / c) * (size / c) + (spread / g) * (spread / g))
        gain = part if gain is None else gain + part
        noise = err if noise is None else noise + err
        for k in range(len(pi)):
            y[k] = y[k] + alpha * pi[k]
        if step == ITERS - 1:
            break
        new = []
        for k in range(len(pi) + 1):
            value = rho[k] if k < len(rho) else None
            if k < len(pi):
                value = value - alpha * pi[k]
            if k > 0:
                moved = alpha * pi[k - 1]
                value = moved if value is None else value + moved
            new.append(value)
        rho = new
        s = square(rho)
        following = functools.reduce(lambda a, b: a + b, [s[l] * m[l] for l in range(len(s))])
        spread = functools.reduce(lambda a, b: a + b, [jnp.abs(s[l]) * jnp.abs(m[l]) for l in range(len(s))])
        beta = following / g
        g = following
        pi = [rho[k] + beta * pi[k] if k < len(pi) else rho[k] for k in range(len(rho))]
    return y, noise / gain


def apply_row(vk, vn, wu, wl, dinv, e, g, lane, accs, store):
    gs = pl.ds(8 * g, 8)

    def tile(ref, row, j, rows=gs):
        return ref[row, rows, pl.ds(128 * j, 128)]

    whole = pl.ds(0, 8)
    v_at = {}
    q_at = {}
    r_at = {}
    rq_at = {}

    def prepare(j):
        v = tile(vk, e, j)
        w = tile(wl, e, j, whole)
        v_at[j] = v
        q_at[j] = w
        r_at[j] = pltpu.roll(v, 1, 1)
        rq_at[j] = pltpu.roll(w * v, 127, 1)

    prepare(0)
    for j in range(TILES):
        if j + 1 < TILES:
            prepare(j + 1)
        left = r_at[j] if j == 0 else jnp.where(lane == 0, r_at[j - 1], r_at[j])
        right = jnp.where(lane == 127, rq_at[j + 1] if j + 1 < TILES else 0.0, rq_at[j])
        t = tile(wu, e, j, whole) * tile(vk, e - 1, j) + tile(wu, e + 1, j, whole) * tile(vk, e + 1, j)
        t = t + (q_at[j] * left + right)
        v = v_at[j]
        if accs is not None:
            accs = (accs[0] + t * v, accs[1])
        if store:
            new = t * tile(dinv, e, j)
            vn[e, gs, pl.ds(128 * j, 128)] = new
            if accs is not None:
                accs = (accs[0], accs[1] + t * new)
    return accs


def powers_own(v, k, wu, wl, dinv, lane):
    zero = jnp.zeros((8, 128), F32)
    store = k < ITERS - 1
    vk = v.at[k]
    vn = v.at[k + 1] if store else None

    def row(e, carry):
        return tuple(apply_row(vk, vn, wu, wl, dinv, e, g, lane, carry[g], store) for g in range(2))

    got = lax.fori_loop(RD, 2 * RD, row, ((zero, zero), (zero, zero)))
    return [got[0][0], got[1][0]], [got[0][1], got[1][1]]


def powers_halo(v, k, wu, wl, dinv, lane, lo, hi):
    vk, vn = v.at[k], v.at[k + 1]

    def row(i, carry):
        for e in (i, EXT - 1 - i):
            for g in range(2):
                apply_row(vk, vn, wu, wl, dinv, e, g, lane, None, True)
        return carry

    lax.fori_loop(lo, hi, row, 0)


def project(fields, basis_rows, out):
    count = fields.shape[0] // (RD * CH)
    lane = lax.broadcasted_iota(jnp.int32, (CH, 256), 1) % RD
    for q in range(4):
        full = lax.dot_general(
            fields[...], basis_rows[pl.ds(256 * q, 256), :], (((1,), (1,)), ((), ())),
            preferred_element_type=F32,
        )
        for f in range(count):
            rows = full[64 * f : 64 * f + 64]
            part = rows[48:64]
            for x in range(RD - 1):
                part = jnp.where(lane == x, rows[16 * x : 16 * x + 16], part)
            for h in range(2):
                piece = part[:, 128 * h : 128 * h + 128]
                if count == 1:
                    out[2 * q + h] = piece
                else:
                    out[pl.ds(16 * (2 * q + h), 16), f, :] = piece


def over_rows(value):
    lane = lax.broadcasted_iota(jnp.int32, value.shape, 1)
    pair = value + jnp.where(lane % 2 == 0, pltpu.roll(value, 127, 1), pltpu.roll(value, 1, 1))
    return pair + jnp.where(lane % 4 < 2, pltpu.roll(pair, 126, 1), pltpu.roll(pair, 2, 1))


def in_three(value):
    high = value.astype(jnp.bfloat16)
    rest = value - high.astype(F32)
    middle = rest.astype(jnp.bfloat16)
    low = (rest - middle.astype(F32)).astype(jnp.bfloat16)
    return jnp.concatenate([high, middle, low], axis=0)


def join_three(value, count):
    return value[:count] + value[count : 2 * count] + value[2 * count : 3 * count]


def step_kernel(
    source, observed, precision, conductivity, log_field, noise_field, subspace, eigen, basis,
    proposal, coef_ref, info_ref,
    lf, dinv, v, wu, wl, ws, sx, ox, px, state, cb, sb, ob, pb, mom_a, mom_b,
    nf, bm, f2, fg, ps2, got2, sum2, ps, got, sums, wide_f, pick, em, pr,
    local_sem, send_sem, recv_sem, all_sem, field_sem, out_sem,
):
    me = lax.axis_index(AXIS)
    own = [
        pltpu.make_async_copy(conductivity, cb.at[2], local_sem.at[1]),
        pltpu.make_async_copy(source, sb.at[1], local_sem.at[2]),
        pltpu.make_async_copy(observed, ob.at[1], local_sem.at[3]),
        pltpu.make_async_copy(precision, pb.at[1], local_sem.at[4]),
    ]
    logs = [
        pltpu.make_async_copy(log_field.at[:, x, :], lf.at[RD + x], field_sem.at[x]) for x in range(RD)
    ]
    noises = [
        pltpu.make_async_copy(noise_field.at[:, x, :], nf.at[x], field_sem.at[RD + x]) for x in range(RD)
    ]
    barrier = greet_all(me)
    for copy in own + logs + noises:
        copy.start()

    def fetch(r, carry):
        pltpu.make_async_copy(
            basis.at[r], bm.at[pl.ds(pl.multiple_of(RD * r, RD), RD)], local_sem.at[0]
        ).start()
        return carry

    lax.fori_loop(0, basis.shape[0], fetch, 0, unroll=8)
    for copy in own + logs:
        copy.wait()
    pl.semaphore_wait(barrier, N - 1)

    count = [0]

    def remote(src, dst, shift):
        index = count[0]
        count[0] += 1
        copy = pltpu.make_async_remote_copy(
            src_ref=src, dst_ref=dst, send_sem=send_sem.at[index], recv_sem=recv_sem.at[index],
            device_id=(lax.rem(me + shift + N, N),), device_id_type=MESH_ID,
        )
        copy.start()
        return copy

    early = []
    for block, src, centre in ((cb, 2, 2), (sb, 1, 1)):
        early.append(remote(block.at[src], block.at[centre - 1], 1))
        early.append(remote(block.at[src], block.at[centre + 1], -1))
    early.append(remote(cb.at[2], cb.at[0], 2))
    early.append(remote(cb.at[2], cb.at[4], -2))
    rows = []
    for i in range(RD):
        rows.append(
            (
                remote(lf.at[2 * RD - 1 - i], lf.at[RD - 1 - i], 1),
                remote(lf.at[RD + i], lf.at[2 * RD + i], -1),
            )
        )
    late = []
    for block in (ob, pb):
        late.append(remote(block.at[1], block.at[0], 1))
        late.append(remote(block.at[1], block.at[2], -1))

    for x in range(RD):
        f2[pl.ds(16 * x, 16), :] = lf[RD + x].astype(jnp.bfloat16)
    for copy in noises:
        copy.wait()
    for x in range(RD):
        f2[pl.ds(64 + 16 * x, 16), :] = nf[x].astype(jnp.bfloat16)
    pltpu.make_async_copy(bm, bm, local_sem.at[0]).wait()
    project(f2, bm, ps2)

    for copy in early:
        copy.wait()

    lane = lax.broadcasted_iota(jnp.int32, (8, 128), 1)
    first = jnp.where(me == 0, 0.0, 1.0).astype(F32)
    last = jnp.where(me == N - 1, 0.0, 1.0).astype(F32)
    col = lax.broadcasted_iota(jnp.int32, (1, NY), 1)

    def crow(e):
        return cb[e // RD + 1, pl.ds(e % RD, 1), :]

    def edge(e):
        a, b = crow(e - 1), crow(e)
        if e == RD:
            a = first * a + (1.0 - first) * b
        if e == 2 * RD:
            b = last * b + (1.0 - last) * a
        return 0.5 * (a + b)

    for e in range(EXT + 1):
        wu[e] = jnp.broadcast_to(edge(e), (8, NY))
    for e in range(EXT):
        c = crow(e)
        before = jnp.where(col == 0, c, pltpu.roll(c, 1, 1))
        after = jnp.where(col == NY - 1, c, pltpu.roll(c, NY - 1, 1))
        left = 0.5 * (c + before)
        right = 0.5 * (c + after)
        wl[e] = jnp.broadcast_to(jnp.where(col == 0, 0.0, left), (8, NY))
        ws[e] = jnp.broadcast_to(left + right, (8, NY)) + wu[e] + wu[e + 1]
        sx[e] = jnp.broadcast_to(sb[e // RD, pl.ds(e % RD, 1), :], (8, NY))

    def start_row(e, keep):
        for g in range(2):
            gs = pl.ds(8 * g, 8)
            d = keep / (ws[e] + jnp.exp(lf[e, gs, :]))
            dinv[e, gs, :] = d
            v[0, e, gs, :] = sx[e] * d

    def own_start(e, carry):
        start_row(e, jnp.float32(1.0))
        return carry

    lax.fori_loop(RD, 2 * RD, own_start, 0)
    for i, (above, below) in enumerate(rows):
        above.wait()
        below.wait()
        start_row(RD - 1 - i, first)
        start_row(2 * RD + i, last)

    def spread2(step, carry):
        to = lax.rem(me + step, N)
        pltpu.make_async_remote_copy(
            src_ref=ps2.at[to], dst_ref=got2.at[me], send_sem=all_sem.at[4], recv_sem=all_sem.at[5],
            device_id=(to,), device_id_type=MESH_ID,
        ).start()
        return carry

    lax.fori_loop(1, N, spread2, 0, unroll=8)
    got2[me] = ps2[me]

    def moments_zero(side):
        zero = jnp.zeros((8, 128), F32)

        def row(e, carry):
            out = []
            for g in range(2):
                acc = carry[g]
                for j in range(TILES):
                    sl = pl.ds(128 * j, 128)
                    acc = acc + side(e, g, sl) * v[0, e, pl.ds(8 * g, 8), sl]
                out.append(acc)
            return tuple(out)

        return list(lax.fori_loop(RD, 2 * RD, row, (zero, zero)))

    accs = [moments_zero(lambda e, g, sl: sx[e, :, sl])]
    moved = []
    for k in range(ITERS):
        one, two = powers_own(v, k, wu, wl, dinv, lane)
        accs.append(one)
        if k < ITERS - 1:
            accs.append(two)
            moved.append(remote(v.at[k + 1, RD], v.at[k + 1, 0], 1))
            moved.append(remote(v.at[k + 1, 2 * RD - 1], v.at[k + 1, EXT - 1], -1))
            powers_halo(v, k, wu, wl, dinv, lane, k + 1, RD)
    mom_a[me] = pack(accs)
    send_row_to_all(me, mom_a, all_sem.at[0], all_sem.at[1])

    variance = 1.0 / (1.0 + eigen[...])
    below = 2.0 + 0.8 * variance
    factors = jnp.concatenate(
        [
            (2.0 - 0.8 * variance) / below,
            1.6 * variance / below,
            jnp.sqrt(6.4 * variance) / below,
            jnp.zeros((5, variance.shape[1]), F32),
            subspace[...],
        ],
        axis=0,
    )
    rank = factors.shape[1]
    row_id = lax.broadcasted_iota(jnp.int32, (rank, RD * rank), 0)
    lane_id = lax.broadcasted_iota(jnp.int32, (rank, RD * rank), 1)
    widen = jnp.where(lane_id // RD == row_id, 1.0, 0.0).astype(jnp.bfloat16)
    wide_f[...] = join_three(
        jnp.dot(in_three(factors), widen, preferred_element_type=F32), 8 + CH
    )
    row_id = lax.broadcasted_iota(jnp.int32, (RD * rank, rank), 0)
    lane_id = lax.broadcasted_iota(jnp.int32, (RD * rank, rank), 1)
    pick[...] = jnp.where(row_id == RD * lane_id, 1.0, 0.0).astype(jnp.bfloat16)

    for copy in late:
        copy.wait()
    for e in range(EXT):
        ox[e] = jnp.broadcast_to(ob[e // RD, pl.ds(e % RD, 1), :], (8, NY))
        px[e] = jnp.broadcast_to(pb[e // RD, pl.ds(e % RD, 1), :], (8, NY))
    moved[0].wait()
    moved[1].wait()
    powers_halo(v, 1, wu, wl, dinv, lane, 1, 2)
    moved[2].wait()
    moved[3].wait()
    powers_halo(v, 2, wu, wl, dinv, lane, 1, 3)
    moved[4].wait()
    moved[5].wait()

    wait_rows(mom_a, all_sem.at[1])
    y, info = krylov_weights(unpack(jnp.sum(mom_a[...], axis=0)))
    info_ref[0] = jnp.broadcast_to(info, (CH, 128))

    wait_rows(got2, all_sem.at[5])
    sum2[me] = over_rows(jnp.sum(got2[...], axis=0))
    send_row_to_all(me, sum2, all_sem.at[6], all_sem.at[7])

    def adjoint_start(e, carry):
        out = []
        for g in range(2):
            acc = carry[g]
            gs = pl.ds(8 * g, 8)
            yg = [jnp.broadcast_to(y[k][8 * g:8 * g + 8], (8, 128)) for k in range(ITERS)]
            for j in range(TILES):
                sl = pl.ds(128 * j, 128)
                x = yg[0] * v[0, e, gs, sl]
                for k in range(1, ITERS):
                    x = x + yg[k] * v[k, e, gs, sl]
                side = px[e, :, sl] * (x - ox[e, :, sl])
                new = side * dinv[e, gs, sl]
                state[e, gs, sl] = x
                v[0, e, gs, sl] = new
                acc = acc + side * new
            out.append(acc)
        return tuple(out)

    zero = jnp.zeros((8, 128), F32)
    lax.fori_loop(0, RD, adjoint_start, (zero, zero))
    lax.fori_loop(2 * RD, EXT, adjoint_start, (zero, zero))
    accs = [list(lax.fori_loop(RD, 2 * RD, adjoint_start, (zero, zero)))]
    for k in range(ITERS):
        one, two = powers_own(v, k, wu, wl, dinv, lane)
        accs.append(one)
        if k < ITERS - 1:
            accs.append(two)
            powers_halo(v, k, wu, wl, dinv, lane, k + 1, RD)
    mom_b[me] = pack(accs)
    send_row_to_all(me, mom_b, all_sem.at[2], all_sem.at[3])
    wait_rows(mom_b, all_sem.at[3])
    y, info = krylov_weights(unpack(jnp.sum(mom_b[...], axis=0)))
    info_ref[1] = jnp.broadcast_to(info, (CH, 128))

    for r in range(RD):
        for h in range(4):
            sl = pl.ds(512 * h, 512)
            adj = y[0] * v[0, r + RD, :, sl]
            for k in range(1, ITERS):
                adj = adj + y[k] * v[k, r + RD, :, sl]
            value = -jnp.exp(lf[r + RD, :, sl]) * adj * state[r + RD, :, sl]
            fg[pl.ds(16 * r, 16), sl] = value.astype(jnp.bfloat16)
    project(fg, bm, ps)

    def spread(step, carry):
        to = lax.rem(me + step, N)
        pltpu.make_async_remote_copy(
            src_ref=ps.at[to // CH, pl.ds(to % CH, 1)], dst_ref=got.at[me],
            send_sem=all_sem.at[8], recv_sem=all_sem.at[9],
            device_id=(to,), device_id_type=MESH_ID,
        ).start()
        return carry

    lax.fori_loop(1, N, spread, 0, unroll=8)
    got[me] = ps[me // CH, pl.ds(me % CH, 1), :]
    wait_rows(got, all_sem.at[9])
    sums[me] = over_rows(jnp.sum(got[...], axis=0))
    send_row_to_all(me, sums, all_sem.at[10], all_sem.at[11])
    wait_rows(sum2, all_sem.at[7])
    wait_rows(sums, all_sem.at[11])

    lane = lax.broadcasted_iota(jnp.int32, (CH, 128), 1) % RD
    pieces = []
    for b in range(8):
        rows = pl.ds(16 * b, 16)
        cols = pl.ds(128 * b, 128)
        state_coef, noise_coef = sum2[rows, 0, :], sum2[rows, 1, :]
        new = wide_f[0:1, cols] * state_coef - wide_f[1:2, cols] * sums[rows, 0, :]
        new = new + wide_f[2:3, cols] * wide_f[8 : 8 + CH, cols]
        correction = new - 0.6 * state_coef - 0.8 * noise_coef
        for x in range(RD):
            em[pl.ds(16 * x, 16), cols] = jnp.where(lane == x, correction, 0.0).astype(jnp.bfloat16)
        pieces.append(new)
    for h in range(4):
        sl = pl.ds(512 * h, 512)
        rebuilt = jnp.dot(em[...], bm[:, sl], preferred_element_type=F32)
        for x in range(RD):
            pr[x, :, sl] = 0.6 * lf[RD + x, :, sl] + 0.8 * nf[x, :, sl] + rebuilt[16 * x : 16 * x + 16]
    results = [pltpu.make_async_copy(pr.at[x], proposal.at[:, x, :], out_sem.at[x]) for x in range(RD)]
    for copy in results:
        copy.start()
    coef_ref[...] = join_three(
        jnp.dot(in_three(jnp.concatenate(pieces, axis=1)), pick[...], preferred_element_type=F32), CH
    )
    for buf, sem in ((mom_a, 0), (mom_b, 2), (got2, 4), (sum2, 6), (got, 8), (sums, 10)):
        wait_rows(buf, all_sem.at[sem])
    for copy in results:
        copy.wait()


def per_device(
    source, observed, precision, conductivity, log_field, noise_field, subspace_noise, eigenvalues, basis,
):
    any_space = pl.BlockSpec(memory_space=pl.ANY)
    vmem = pl.BlockSpec(memory_space=pltpu.VMEM)
    rank = eigenvalues.shape[0]
    wide = pltpu.VMEM((EXT, CH, NY), F32)
    row8 = pltpu.VMEM((EXT, 8, NY), F32)
    small = pltpu.VMEM((3, RD, NY), F32)
    one = pltpu.VMEM((N, 1, 128), F32)
    two = pltpu.VMEM((N, 2, 128), F32)
    half = jnp.bfloat16
    proposal, new_coef, info = pl.pallas_call(
        step_kernel,
        out_shape=(
            jax.ShapeDtypeStruct(log_field.shape, F32),
            jax.ShapeDtypeStruct((CH, rank), F32),
            jax.ShapeDtypeStruct((2, CH, 128), F32),
        ),
        in_specs=[any_space] * 6 + [vmem] * 2 + [any_space],
        out_specs=(any_space, vmem, vmem),
        scratch_shapes=[
            wide, wide, pltpu.VMEM((ITERS, EXT, CH, NY), F32),
            pltpu.VMEM((EXT + 1, 8, NY), F32), row8, row8, row8, row8, row8, wide,
            pltpu.VMEM((5, RD, NY), F32), small, small, small, one, one,
            pltpu.VMEM((RD, CH, NY), F32),
            pltpu.VMEM((RD * rank, NY), half),
            pltpu.VMEM((2 * RD * CH, NY), half),
            pltpu.VMEM((RD * CH, NY), half),
            two, two, two,
            pltpu.VMEM((8, CH, 128), F32), one, one,
            pltpu.VMEM((8 + CH, RD * rank), F32),
            pltpu.VMEM((RD * rank, rank), half),
            pltpu.VMEM((RD * CH, RD * rank), half),
            pltpu.VMEM((RD, CH, NY), F32),
            pltpu.SemaphoreType.DMA((5,)),
            pltpu.SemaphoreType.DMA((24,)),
            pltpu.SemaphoreType.DMA((24,)),
            pltpu.SemaphoreType.DMA((12,)),
            pltpu.SemaphoreType.DMA((8,)),
            pltpu.SemaphoreType.DMA((4,)),
        ],
        compiler_params=pltpu.CompilerParams(
            collective_id=0, has_side_effects=True, vmem_limit_bytes=48 << 20
        ),
    )(
        source, observed, precision, conductivity, log_field, noise_field,
        subspace_noise, eigenvalues.reshape(1, rank), basis,
    )
    return (proposal, new_coef)


def solution(mesh):
    return jax.shard_map(
        per_device,
        mesh=mesh,
        in_specs=(
            P(AXIS, None), P(AXIS, None), P(AXIS, None), P(AXIS, None),
            P(None, AXIS, None), P(None, AXIS, None), P(), P(), P(None, AXIS, None),
        ),
        out_specs=(P(None, AXIS, None), P()),
        check_vma=False,
    )
```

```python
import functools

import jax
import jax.numpy as jnp
from jax import lax
from jax.experimental import pallas as pl
from jax.experimental.pallas import tpu as pltpu
from jax.sharding import PartitionSpec as P

ITERS = 4
AXIS = "rows"
N = 128
RD = 4
NY = 2048
CH = 16
EXT = 12
TILES = NY // 128
MESH_ID = pl.DeviceIdType.MESH
F32 = jnp.float32


def greet_all(me):
    barrier = pltpu.get_barrier_semaphore()

    def signal(step, carry):
        pl.semaphore_signal(barrier, inc=1, device_id=(lax.rem(me + step, N),), device_id_type=MESH_ID)
        return carry

    lax.fori_loop(1, N, signal, 0)
    return barrier


def send_row_to_all(me, buf, send_sem, recv_sem):
    def send(step, carry):
        pltpu.make_async_remote_copy(
            src_ref=buf.at[me], dst_ref=buf.at[me], send_sem=send_sem, recv_sem=recv_sem,
            device_id=(lax.rem(me + step, N),), device_id_type=MESH_ID,
        ).start()
        return carry

    lax.fori_loop(1, N, send, 0, unroll=8)


def wait_rows(buf, sem):
    part = buf.at[pl.ds(0, N - 1)]
    pltpu.make_async_copy(part, part, sem).wait()


def pack(accs):
    lane = lax.broadcasted_iota(jnp.int32, (8, 128), 1)
    sub = lax.broadcasted_iota(jnp.int32, (8, 128), 0)
    row = jnp.zeros((8, 128), F32)
    for k in range(8):
        for g in range(2):
            total = jnp.sum(accs[k][g], axis=1, keepdims=True)
            row = row + jnp.where(lane == (g * 8 + k) * 8 + sub, total, 0.0)
    return jnp.sum(row, axis=0, keepdims=True)


def unpack(row):
    lane = lax.broadcasted_iota(jnp.int32, (8, 128), 1)
    sub = lax.broadcasted_iota(jnp.int32, (8, 128), 0)
    wide = jnp.broadcast_to(row, (8, 128))
    moments = []
    for k in range(8):
        halves = [
            jnp.sum(jnp.where(lane == (g * 8 + k) * 8 + sub, wide, 0.0), axis=1, keepdims=True)
            for g in range(2)
        ]
        moments.append(jnp.concatenate(halves, axis=0))
    return moments


def square(poly):
    out = [None] * (2 * len(poly) - 1)
    for i, a in enumerate(poly):
        for j, b in enumerate(poly):
            term = a * b
            out[i + j] = term if out[i + j] is None else out[i + j] + term
    return out


def krylov_weights(m):
    one = jnp.ones_like(m[0])
    rho, pi = [one], [one]
    y = [jnp.zeros_like(one)] * ITERS
    g = m[0]
    spread = g
    gain, noise = None, None
    for step in range(ITERS):
        s = square(pi)
        c = functools.reduce(lambda a, b: a + b, [s[l] * (m[l] - m[l + 1]) for l in range(len(s))])
        size = functools.reduce(
            lambda a, b: a + b, [jnp.abs(s[l]) * (jnp.abs(m[l]) + jnp.abs(m[l + 1])) for l in range(len(s))]
        )
        alpha = g / c
        part = alpha * g
        err = part * ((size / c) * (size / c) + (spread / g) * (spread / g))
        gain = part if gain is None else gain + part
        noise = err if noise is None else noise + err
        for k in range(len(pi)):
            y[k] = y[k] + alpha * pi[k]
        if step == ITERS - 1:
            break
        new = []
        for k in range(len(pi) + 1):
            value = rho[k] if k < len(rho) else None
            if k < len(pi):
                value = value - alpha * pi[k]
            if k > 0:
                moved = alpha * pi[k - 1]
                value = moved if value is None else value + moved
            new.append(value)
        rho = new
        s = square(rho)
        following = functools.reduce(lambda a, b: a + b, [s[l] * m[l] for l in range(len(s))])
        spread = functools.reduce(lambda a, b: a + b, [jnp.abs(s[l]) * jnp.abs(m[l]) for l in range(len(s))])
        beta = following / g
        g = following
        pi = [rho[k] + beta * pi[k] if k < len(pi) else rho[k] for k in range(len(rho))]
    return y, noise / gain


def apply_row(vk, vn, wu, wl, dinv, e, g, lane, accs, store):
    gs = pl.ds(8 * g, 8)

    def tile(ref, row, j, rows=gs):
        return ref[row, rows, pl.ds(128 * j, 128)]

    whole = pl.ds(0, 8)
    v_at = {}
    q_at = {}
    r_at = {}
    rq_at = {}

    def prepare(j):
        v = tile(vk, e, j)
        w = tile(wl, e, j, whole)
        v_at[j] = v
        q_at[j] = w
        r_at[j] = pltpu.roll(v, 1, 1)
        rq_at[j] = pltpu.roll(w * v, 127, 1)

    prepare(0)
    for j in range(TILES):
        if j + 1 < TILES:
            prepare(j + 1)
        left = r_at[j] if j == 0 else jnp.where(lane == 0, r_at[j - 1], r_at[j])
        right = jnp.where(lane == 127, rq_at[j + 1] if j + 1 < TILES else 0.0, rq_at[j])
        t = tile(wu, e, j, whole) * tile(vk, e - 1, j) + tile(wu, e + 1, j, whole) * tile(vk, e + 1, j)
        t = t + (q_at[j] * left + right)
        v = v_at[j]
        if accs is not None:
            accs = (accs[0] + t * v, accs[1])
        if store:
            new = t * tile(dinv, e, j)
            vn[e, gs, pl.ds(128 * j, 128)] = new
            if accs is not None:
                accs = (accs[0], accs[1] + t * new)
    return accs


def powers_own(v, k, wu, wl, dinv, lane):
    zero = jnp.zeros((8, 128), F32)
    store = k < ITERS - 1
    vk = v.at[k]
    vn = v.at[k + 1] if store else None

    def row(e, carry):
        return tuple(apply_row(vk, vn, wu, wl, dinv, e, g, lane, carry[g], store) for g in range(2))

    got = lax.fori_loop(RD, 2 * RD, row, ((zero, zero), (zero, zero)))
    return [got[0][0], got[1][0]], [got[0][1], got[1][1]]


def powers_halo(v, k, wu, wl, dinv, lane, lo, hi):
    vk, vn = v.at[k], v.at[k + 1]

    def row(i, carry):
        for e in (i, EXT - 1 - i):
            for g in range(2):
                apply_row(vk, vn, wu, wl, dinv, e, g, lane, None, True)
        return carry

    lax.fori_loop(lo, hi, row, 0)


def project(fields, basis_rows, out):
    count = fields.shape[0] // (RD * CH)
    lane = lax.broadcasted_iota(jnp.int32, (CH, 256), 1) % RD
    for q in range(4):
        full = lax.dot_general(
            fields[...], basis_rows[pl.ds(256 * q, 256), :], (((1,), (1,)), ((), ())),
            preferred_element_type=F32,
        )
        for f in range(count):
            rows = full[64 * f : 64 * f + 64]
            part = rows[48:64]
            for x in range(RD - 1):
                part = jnp.where(lane == x, rows[16 * x : 16 * x + 16], part)
            for h in range(2):
                piece = part[:, 128 * h : 128 * h + 128]
                if count == 1:
                    out[2 * q + h] = piece
                else:
                    out[pl.ds(16 * (2 * q + h), 16), f, :] = piece


def over_rows(value):
    lane = lax.broadcasted_iota(jnp.int32, value.shape, 1)
    pair = value + jnp.where(lane % 2 == 0, pltpu.roll(value, 127, 1), pltpu.roll(value, 1, 1))
    return pair + jnp.where(lane % 4 < 2, pltpu.roll(pair, 126, 1), pltpu.roll(pair, 2, 1))


def in_three(value):
    high = value.astype(jnp.bfloat16)
    rest = value - high.astype(F32)
    middle = rest.astype(jnp.bfloat16)
    low = (rest - middle.astype(F32)).astype(jnp.bfloat16)
    return jnp.concatenate([high, middle, low], axis=0)


def join_three(value, count):
    return value[:count] + value[count : 2 * count] + value[2 * count : 3 * count]


def step_kernel(
    source, observed, precision, conductivity, log_field, noise_field, subspace_hbm, eigen_hbm, basis,
    proposal, coef_ref, info_ref,
    lf, dinv, v, wu, wl, ws, sx, ox, px, state, cb, sb, ob, pb, mom_a, mom_b,
    nf, bm, f2, fg, ps2, got2, sum2, ps, got, sums, wide_f, pick, em, pr,
    subspace, eigen,
    local_sem, send_sem, recv_sem, all_sem, field_sem, out_sem,
):
    me = lax.axis_index(AXIS)
    own = [
        pltpu.make_async_copy(conductivity, cb.at[2], local_sem.at[1]),
        pltpu.make_async_copy(source, sb.at[1], local_sem.at[2]),
        pltpu.make_async_copy(observed, ob.at[1], local_sem.at[3]),
        pltpu.make_async_copy(precision, pb.at[1], local_sem.at[4]),
        pltpu.make_async_copy(subspace_hbm, subspace, local_sem.at[5]),
        pltpu.make_async_copy(eigen_hbm, eigen, local_sem.at[6]),
    ]
    logs = [
        pltpu.make_async_copy(log_field.at[:, x, :], lf.at[RD + x], field_sem.at[x]) for x in range(RD)
    ]
    noises = [
        pltpu.make_async_copy(noise_field.at[:, x, :], nf.at[x], field_sem.at[RD + x]) for x in range(RD)
    ]
    barrier = greet_all(me)
    for copy in own + logs + noises:
        copy.start()

    def fetch(r, carry):
        pltpu.make_async_copy(
            basis.at[r], bm.at[pl.ds(pl.multiple_of(RD * r, RD), RD)], local_sem.at[0]
        ).start()
        return carry

    lax.fori_loop(0, basis.shape[0], fetch, 0, unroll=8)
    for copy in own + logs:
        copy.wait()
    pl.semaphore_wait(barrier, N - 1)

    count = [0]

    def remote(src, dst, shift):
        index = count[0]
        count[0] += 1
        copy = pltpu.make_async_remote_copy(
            src_ref=src, dst_ref=dst, send_sem=send_sem.at[index], recv_sem=recv_sem.at[index],
            device_id=(lax.rem(me + shift + N, N),), device_id_type=MESH_ID,
        )
        copy.start()
        return copy

    early = []
    for block, src, centre in ((cb, 2, 2), (sb, 1, 1)):
        early.append(remote(block.at[src], block.at[centre - 1], 1))
        early.append(remote(block.at[src], block.at[centre + 1], -1))
    early.append(remote(cb.at[2], cb.at[0], 2))
    early.append(remote(cb.at[2], cb.at[4], -2))
    rows = []
    for i in range(RD):
        rows.append(
            (
                remote(lf.at[2 * RD - 1 - i], lf.at[RD - 1 - i], 1),
                remote(lf.at[RD + i], lf.at[2 * RD + i], -1),
            )
        )
    late = []
    for block in (ob, pb):
        late.append(remote(block.at[1], block.at[0], 1))
        late.append(remote(block.at[1], block.at[2], -1))

    for x in range(RD):
        f2[pl.ds(16 * x, 16), :] = lf[RD + x].astype(jnp.bfloat16)
    for copy in noises:
        copy.wait()
    for x in range(RD):
        f2[pl.ds(64 + 16 * x, 16), :] = nf[x].astype(jnp.bfloat16)
    pltpu.make_async_copy(bm, bm, local_sem.at[0]).wait()
    project(f2, bm, ps2)

    for copy in early:
        copy.wait()

    lane = lax.broadcasted_iota(jnp.int32, (8, 128), 1)
    first = jnp.where(me == 0, 0.0, 1.0).astype(F32)
    last = jnp.where(me == N - 1, 0.0, 1.0).astype(F32)
    col = lax.broadcasted_iota(jnp.int32, (1, NY), 1)

    def crow(e):
        return cb[e // RD + 1, pl.ds(e % RD, 1), :]

    def edge(e):
        a, b = crow(e - 1), crow(e)
        if e == RD:
            a = first * a + (1.0 - first) * b
        if e == 2 * RD:
            b = last * b + (1.0 - last) * a
        return 0.5 * (a + b)

    for e in range(EXT + 1):
        wu[e] = jnp.broadcast_to(edge(e), (8, NY))
    for e in range(EXT):
        c = crow(e)
        before = jnp.where(col == 0, c, pltpu.roll(c, 1, 1))
        after = jnp.where(col == NY - 1, c, pltpu.roll(c, NY - 1, 1))
        left = 0.5 * (c + before)
        right = 0.5 * (c + after)
        wl[e] = jnp.broadcast_to(jnp.where(col == 0, 0.0, left), (8, NY))
        ws[e] = jnp.broadcast_to(left + right, (8, NY)) + wu[e] + wu[e + 1]
        sx[e] = jnp.broadcast_to(sb[e // RD, pl.ds(e % RD, 1), :], (8, NY))

    def start_row(e, keep):
        for g in range(2):
            gs = pl.ds(8 * g, 8)
            d = keep / (ws[e] + jnp.exp(lf[e, gs, :]))
            dinv[e, gs, :] = d
            v[0, e, gs, :] = sx[e] * d

    def own_start(e, carry):
        start_row(e, jnp.float32(1.0))
        return carry

    lax.fori_loop(RD, 2 * RD, own_start, 0)
    for i, (above, below) in enumerate(rows):
        above.wait()
        below.wait()
        start_row(RD - 1 - i, first)
        start_row(2 * RD + i, last)

    def spread2(step, carry):
        to = lax.rem(me + step, N)
        pltpu.make_async_remote_copy(
            src_ref=ps2.at[to], dst_ref=got2.at[me], send_sem=all_sem.at[4], recv_sem=all_sem.at[5],
            device_id=(to,), device_id_type=MESH_ID,
        ).start()
        return carry

    lax.fori_loop(1, N, spread2, 0, unroll=8)
    got2[me] = ps2[me]

    def moments_zero(side):
        zero = jnp.zeros((8, 128), F32)

        def row(e, carry):
            out = []
            for g in range(2):
                acc = carry[g]
                for j in range(TILES):
                    sl = pl.ds(128 * j, 128)
                    acc = acc + side(e, g, sl) * v[0, e, pl.ds(8 * g, 8), sl]
                out.append(acc)
            return tuple(out)

        return list(lax.fori_loop(RD, 2 * RD, row, (zero, zero)))

    accs = [moments_zero(lambda e, g, sl: sx[e, :, sl])]
    moved = []
    for k in range(ITERS):
        one, two = powers_own(v, k, wu, wl, dinv, lane)
        accs.append(one)
        if k < ITERS - 1:
            accs.append(two)
            moved.append(remote(v.at[k + 1, RD], v.at[k + 1, 0], 1))
            moved.append(remote(v.at[k + 1, 2 * RD - 1], v.at[k + 1, EXT - 1], -1))
            powers_halo(v, k, wu, wl, dinv, lane, k + 1, RD)
    mom_a[me] = pack(accs)
    send_row_to_all(me, mom_a, all_sem.at[0], all_sem.at[1])

    variance = 1.0 / (1.0 + eigen[...])
    below = 2.0 + 0.8 * variance
    factors = jnp.concatenate(
        [
            (2.0 - 0.8 * variance) / below,
            1.6 * variance / below,
            jnp.sqrt(6.4 * variance) / below,
            jnp.zeros((5, variance.shape[1]), F32),
            subspace[...],
        ],
        axis=0,
    )
    rank = factors.shape[1]
    row_id = lax.broadcasted_iota(jnp.int32, (rank, RD * rank), 0)
    lane_id = lax.broadcasted_iota(jnp.int32, (rank, RD * rank), 1)
    widen = jnp.where(lane_id // RD == row_id, 1.0, 0.0).astype(jnp.bfloat16)
    wide_f[...] = join_three(
        jnp.dot(in_three(factors), widen, preferred_element_type=F32), 8 + CH
    )
    row_id = lax.broadcasted_iota(jnp.int32, (RD * rank, rank), 0)
    lane_id = lax.broadcasted_iota(jnp.int32, (RD * rank, rank), 1)
    pick[...] = jnp.where(row_id == RD * lane_id, 1.0, 0.0).astype(jnp.bfloat16)

    for copy in late:
        copy.wait()
    for e in range(EXT):
        ox[e] = jnp.broadcast_to(ob[e // RD, pl.ds(e % RD, 1), :], (8, NY))
        px[e] = jnp.broadcast_to(pb[e // RD, pl.ds(e % RD, 1), :], (8, NY))
    moved[0].wait()
    moved[1].wait()
    powers_halo(v, 1, wu, wl, dinv, lane, 1, 2)
    moved[2].wait()
    moved[3].wait()
    powers_halo(v, 2, wu, wl, dinv, lane, 1, 3)
    moved[4].wait()
    moved[5].wait()

    wait_rows(mom_a, all_sem.at[1])
    y, info = krylov_weights(unpack(jnp.sum(mom_a[...], axis=0)))
    info_ref[0] = jnp.broadcast_to(info, (CH, 128))

    wait_rows(got2, all_sem.at[5])
    sum2[me] = over_rows(jnp.sum(got2[...], axis=0))
    send_row_to_all(me, sum2, all_sem.at[6], all_sem.at[7])

    def adjoint_start(e, carry):
        out = []
        for g in range(2):
            acc = carry[g]
            gs = pl.ds(8 * g, 8)
            yg = [jnp.broadcast_to(y[k][8 * g:8 * g + 8], (8, 128)) for k in range(ITERS)]
            for j in range(TILES):
                sl = pl.ds(128 * j, 128)
                x = yg[0] * v[0, e, gs, sl]
                for k in range(1, ITERS):
                    x = x + yg[k] * v[k, e, gs, sl]
                side = px[e, :, sl] * (x - ox[e, :, sl])
                new = side * dinv[e, gs, sl]
                state[e, gs, sl] = x
                v[0, e, gs, sl] = new
                acc = acc + side * new
            out.append(acc)
        return tuple(out)

    zero = jnp.zeros((8, 128), F32)
    lax.fori_loop(0, RD, adjoint_start, (zero, zero))
    lax.fori_loop(2 * RD, EXT, adjoint_start, (zero, zero))
    accs = [list(lax.fori_loop(RD, 2 * RD, adjoint_start, (zero, zero)))]
    for k in range(ITERS):
        one, two = powers_own(v, k, wu, wl, dinv, lane)
        accs.append(one)
        if k < ITERS - 1:
            accs.append(two)
            powers_halo(v, k, wu, wl, dinv, lane, k + 1, RD)
    mom_b[me] = pack(accs)
    send_row_to_all(me, mom_b, all_sem.at[2], all_sem.at[3])
    wait_rows(mom_b, all_sem.at[3])
    y, info = krylov_weights(unpack(jnp.sum(mom_b[...], axis=0)))
    info_ref[1] = jnp.broadcast_to(info, (CH, 128))

    for r in range(RD):
        for h in range(4):
            sl = pl.ds(512 * h, 512)
            adj = y[0] * v[0, r + RD, :, sl]
            for k in range(1, ITERS):
                adj = adj + y[k] * v[k, r + RD, :, sl]
            value = -jnp.exp(lf[r + RD, :, sl]) * adj * state[r + RD, :, sl]
            fg[pl.ds(16 * r, 16), sl] = value.astype(jnp.bfloat16)
    project(fg, bm, ps)

    def spread(step, carry):
        to = lax.rem(me + step, N)
        pltpu.make_async_remote_copy(
            src_ref=ps.at[to // CH, pl.ds(to % CH, 1)], dst_ref=got.at[me],
            send_sem=all_sem.at[8], recv_sem=all_sem.at[9],
            device_id=(to,), device_id_type=MESH_ID,
        ).start()
        return carry

    lax.fori_loop(1, N, spread, 0, unroll=8)
    got[me] = ps[me // CH, pl.ds(me % CH, 1), :]
    wait_rows(got, all_sem.at[9])
    sums[me] = over_rows(jnp.sum(got[...], axis=0))
    send_row_to_all(me, sums, all_sem.at[10], all_sem.at[11])
    wait_rows(sum2, all_sem.at[7])
    wait_rows(sums, all_sem.at[11])

    lane = lax.broadcasted_iota(jnp.int32, (CH, 128), 1) % RD
    pieces = []
    for b in range(8):
        rows = pl.ds(16 * b, 16)
        cols = pl.ds(128 * b, 128)
        state_coef, noise_coef = sum2[rows, 0, :], sum2[rows, 1, :]
        new = wide_f[0:1, cols] * state_coef - wide_f[1:2, cols] * sums[rows, 0, :]
        new = new + wide_f[2:3, cols] * wide_f[8 : 8 + CH, cols]
        correction = new - 0.6 * state_coef - 0.8 * noise_coef
        for x in range(RD):
            em[pl.ds(16 * x, 16), cols] = jnp.where(lane == x, correction, 0.0).astype(jnp.bfloat16)
        pieces.append(new)
    for h in range(4):
        sl = pl.ds(512 * h, 512)
        rebuilt = jnp.dot(em[...], bm[:, sl], preferred_element_type=F32)
        for x in range(RD):
            pr[x, :, sl] = 0.6 * lf[RD + x, :, sl] + 0.8 * nf[x, :, sl] + rebuilt[16 * x : 16 * x + 16]
    results = [pltpu.make_async_copy(pr.at[x], proposal.at[:, x, :], out_sem.at[x]) for x in range(RD)]
    for copy in results:
        copy.start()
    coef_ref[...] = join_three(
        jnp.dot(in_three(jnp.concatenate(pieces, axis=1)), pick[...], preferred_element_type=F32), CH
    )
    for buf, sem in ((mom_a, 0), (mom_b, 2), (got2, 4), (sum2, 6), (got, 8), (sums, 10)):
        wait_rows(buf, all_sem.at[sem])
    for copy in results:
        copy.wait()


def per_device(
    source, observed, precision, conductivity, log_field, noise_field, subspace_noise, eigenvalues, basis,
):
    any_space = pl.BlockSpec(memory_space=pltpu.HBM)
    vmem = pl.BlockSpec(memory_space=pltpu.VMEM)
    rank = eigenvalues.shape[0]
    wide = pltpu.VMEM((EXT, CH, NY), F32)
    row8 = pltpu.VMEM((EXT, 8, NY), F32)
    small = pltpu.VMEM((3, RD, NY), F32)
    one = pltpu.VMEM((N, 1, 128), F32)
    two = pltpu.VMEM((N, 2, 128), F32)
    half = jnp.bfloat16
    proposal, new_coef, info = pl.pallas_call(
        step_kernel,
        out_shape=(
            jax.ShapeDtypeStruct(log_field.shape, F32),
            jax.ShapeDtypeStruct((CH, rank), F32),
            jax.ShapeDtypeStruct((2, CH, 128), F32),
        ),
        in_specs=[any_space] * 9,
        out_specs=(any_space, vmem, vmem),
        scratch_shapes=[
            wide, wide, pltpu.VMEM((ITERS, EXT, CH, NY), F32),
            pltpu.VMEM((EXT + 1, 8, NY), F32), row8, row8, row8, row8, row8, wide,
            pltpu.VMEM((5, RD, NY), F32), small, small, small, one, one,
            pltpu.VMEM((RD, CH, NY), F32),
            pltpu.VMEM((RD * rank, NY), half),
            pltpu.VMEM((2 * RD * CH, NY), half),
            pltpu.VMEM((RD * CH, NY), half),
            two, two, two,
            pltpu.VMEM((8, CH, 128), F32), one, one,
            pltpu.VMEM((8 + CH, RD * rank), F32),
            pltpu.VMEM((RD * rank, rank), half),
            pltpu.VMEM((RD * CH, RD * rank), half),
            pltpu.VMEM((RD, CH, NY), F32),
            pltpu.VMEM((CH, rank), F32), pltpu.VMEM((1, rank), F32),
            pltpu.SemaphoreType.DMA((7,)),
            pltpu.SemaphoreType.DMA((24,)),
            pltpu.SemaphoreType.DMA((24,)),
            pltpu.SemaphoreType.DMA((12,)),
            pltpu.SemaphoreType.DMA((8,)),
            pltpu.SemaphoreType.DMA((4,)),
        ],
        compiler_params=pltpu.CompilerParams(
            collective_id=0, has_side_effects=True, vmem_limit_bytes=66_900_000
        ),
    )(
        source, observed, precision, conductivity, log_field, noise_field,
        subspace_noise, eigenvalues.reshape(1, rank), basis,
    )
    return (proposal, new_coef)


def solution(mesh):
    return jax.shard_map(
        per_device,
        mesh=mesh,
        in_specs=(
            P(AXIS, None), P(AXIS, None), P(AXIS, None), P(AXIS, None),
            P(None, AXIS, None), P(None, AXIS, None), P(), P(), P(None, AXIS, None),
        ),
        out_specs=(P(None, AXIS, None), P()),
        check_vma=False,
    )
```

```python
import functools

import jax
import jax.numpy as jnp
from jax import lax
from jax.experimental import pallas as pl
from jax.experimental.pallas import tpu as pltpu
from jax.sharding import PartitionSpec as P

ITERS = 4
AXIS = "rows"
N = 128
RD = 4
NY = 2048
CH = 16
EXT = 12
TILES = NY // 128
MESH_ID = pl.DeviceIdType.MESH
F32 = jnp.float32


def far_first(turn):
    return lax.rem(2 + 3 * turn + 3 * (turn * (turn - 1) // 2), 4)


def for_peers(me, act):
    near = []
    for z in (2, 1, 3, 0):
        for c in (1, 0):
            near.append(lax.rem(me + c, 2) + 2 * lax.rem(me // 2 + z, 4))

    def plane(turn, carry):
        y = lax.rem(me // 8 + far_first(lax.rem(turn, 4)), 4)
        x = lax.rem(me // 32 + far_first(turn // 4), 4)
        for at in near:
            act(8 * y + 32 * x + at)
        return carry

    lax.fori_loop(0, 15, plane, 0)
    for at in near[:-1]:
        act(8 * (me // 8) + at)


def greet_all(me):
    barrier = pltpu.get_barrier_semaphore()
    for_peers(
        me, lambda to: pl.semaphore_signal(barrier, inc=1, device_id=(to,), device_id_type=MESH_ID)
    )
    return barrier


def send_row_to_all(me, buf, send_sem, recv_sem):
    def send(to):
        pltpu.make_async_remote_copy(
            src_ref=buf.at[me], dst_ref=buf.at[me], send_sem=send_sem, recv_sem=recv_sem,
            device_id=(to,), device_id_type=MESH_ID,
        ).start()

    for_peers(me, send)


def wait_rows(buf, sem):
    part = buf.at[pl.ds(0, N - 1)]
    pltpu.make_async_copy(part, part, sem).wait()


def pack(accs):
    lane = lax.broadcasted_iota(jnp.int32, (8, 128), 1)
    sub = lax.broadcasted_iota(jnp.int32, (8, 128), 0)
    row = jnp.zeros((8, 128), F32)
    for k in range(8):
        for g in range(2):
            total = jnp.sum(accs[k][g], axis=1, keepdims=True)
            row = row + jnp.where(lane == (g * 8 + k) * 8 + sub, total, 0.0)
    return jnp.sum(row, axis=0, keepdims=True)


def unpack(row):
    lane = lax.broadcasted_iota(jnp.int32, (8, 128), 1)
    sub = lax.broadcasted_iota(jnp.int32, (8, 128), 0)
    wide = jnp.broadcast_to(row, (8, 128))
    moments = []
    for k in range(8):
        halves = [
            jnp.sum(jnp.where(lane == (g * 8 + k) * 8 + sub, wide, 0.0), axis=1, keepdims=True)
            for g in range(2)
        ]
        moments.append(jnp.concatenate(halves, axis=0))
    return moments


def square(poly):
    out = [None] * (2 * len(poly) - 1)
    for i, a in enumerate(poly):
        for j, b in enumerate(poly):
            term = a * b
            out[i + j] = term if out[i + j] is None else out[i + j] + term
    return out


def krylov_weights(m):
    one = jnp.ones_like(m[0])
    rho, pi = [one], [one]
    y = [jnp.zeros_like(one)] * ITERS
    g = m[0]
    spread = g
    gain, noise = None, None
    for step in range(ITERS):
        s = square(pi)
        c = functools.reduce(lambda a, b: a + b, [s[l] * (m[l] - m[l + 1]) for l in range(len(s))])
        size = functools.reduce(
            lambda a, b: a + b, [jnp.abs(s[l]) * (jnp.abs(m[l]) + jnp.abs(m[l + 1])) for l in range(len(s))]
        )
        alpha = g / c
        part = alpha * g
        err = part * ((size / c) * (size / c) + (spread / g) * (spread / g))
        gain = part if gain is None else gain + part
        noise = err if noise is None else noise + err
        for k in range(len(pi)):
            y[k] = y[k] + alpha * pi[k]
        if step == ITERS - 1:
            break
        new = []
        for k in range(len(pi) + 1):
            value = rho[k] if k < len(rho) else None
            if k < len(pi):
                value = value - alpha * pi[k]
            if k > 0:
                moved = alpha * pi[k - 1]
                value = moved if value is None else value + moved
            new.append(value)
        rho = new
        s = square(rho)
        following = functools.reduce(lambda a, b: a + b, [s[l] * m[l] for l in range(len(s))])
        spread = functools.reduce(lambda a, b: a + b, [jnp.abs(s[l]) * jnp.abs(m[l]) for l in range(len(s))])
        beta = following / g
        g = following
        pi = [rho[k] + beta * pi[k] if k < len(pi) else rho[k] for k in range(len(rho))]
    return y, noise / gain


def apply_row(vk, vn, wu, wl, dinv, e, lane, accs):
    whole = pl.ds(0, 8)
    groups = (pl.ds(0, 8), pl.ds(8, 8))
    kept = {}

    def prepare(j):
        cols = pl.ds(128 * j, 128)
        w = wl[e, whole, cols]
        out = []
        for gs in groups:
            v = vk[e, gs, cols]
            out.append((v, pltpu.roll(v, 1, 1), pltpu.roll(w * v, 127, 1)))
        kept[j] = (w, out)

    prepare(0)
    for j in range(TILES):
        cols = pl.ds(128 * j, 128)
        if j + 1 < TILES:
            prepare(j + 1)
        w, here = kept[j]
        above, below = wu[e, whole, cols], wu[e + 1, whole, cols]
        for g, gs in enumerate(groups):
            v, moved, moved_back = here[g]
            left = moved if j == 0 else jnp.where(lane == 0, kept[j - 1][1][g][1], moved)
            right = jnp.where(lane == 127, kept[j + 1][1][g][2] if j + 1 < TILES else 0.0, moved_back)
            t = above * vk[e - 1, gs, cols] + below * vk[e + 1, gs, cols]
            t = t + (w * left + right)
            if accs is not None:
                accs[0][g] = accs[0][g] + t * v
            if vn is not None:
                new = t * dinv[e, gs, cols]
                vn[e, gs, cols] = new
                if accs is not None:
                    accs[1][g] = accs[1][g] + t * new


def powers_own(v, k, wu, wl, dinv, lane):
    zero = jnp.zeros((8, 128), F32)

    def rows(i, carry):
        accs = [list(carry[0]), list(carry[1])]
        for h in range(2):
            e = RD + 2 * i + h
            apply_row(v.at[k], v.at[k + 1] if k < ITERS - 1 else None, wu, wl, dinv, e, lane, accs)
        return tuple(accs[0]), tuple(accs[1])

    got = lax.fori_loop(0, RD // 2, rows, ((zero, zero), (zero, zero)))
    return list(got[0]), list(got[1])


def powers_pairs(v, wu, wl, dinv, lane, count, which):
    def rows(step, carry):
        k, i = which(step)
        for e in (RD - i, 2 * RD - 1 + i):
            apply_row(v.at[k], v.at[k + 1], wu, wl, dinv, e, lane, None)
        return carry

    if count == 1:
        rows(0, 0)
    else:
        lax.fori_loop(0, count, rows, 0)


def project(fields, basis_rows, out):
    count = fields.shape[0] // (RD * CH)
    lane = lax.broadcasted_iota(jnp.int32, (CH, 256), 1) % RD
    for q in range(4):
        full = lax.dot_general(
            fields[...], basis_rows[pl.ds(256 * q, 256), :], (((1,), (1,)), ((), ())),
            preferred_element_type=F32,
        )
        for f in range(count):
            rows = full[64 * f : 64 * f + 64]
            part = rows[48:64]
            for x in range(RD - 1):
                part = jnp.where(lane == x, rows[16 * x : 16 * x + 16], part)
            for h in range(2):
                piece = part[:, 128 * h : 128 * h + 128]
                if count == 1:
                    out[2 * q + h] = piece
                else:
                    out[pl.ds(16 * (2 * q + h), 16), f, :] = piece


def over_rows(value):
    lane = lax.broadcasted_iota(jnp.int32, value.shape, 1)
    pair = value + jnp.where(lane % 2 == 0, pltpu.roll(value, 127, 1), pltpu.roll(value, 1, 1))
    return pair + jnp.where(lane % 4 < 2, pltpu.roll(pair, 126, 1), pltpu.roll(pair, 2, 1))


def in_three(value):
    high = value.astype(jnp.bfloat16)
    rest = value - high.astype(F32)
    middle = rest.astype(jnp.bfloat16)
    low = (rest - middle.astype(F32)).astype(jnp.bfloat16)
    return jnp.concatenate([high, middle, low], axis=0)


def join_three(value, count):
    return value[:count] + value[count : 2 * count] + value[2 * count : 3 * count]


def step_kernel(
    source, observed, precision, conductivity, log_field, noise_field, subspace_hbm, eigen_hbm, basis,
    proposal, coef_ref, info_ref,
    lf, dinv, v, wu, wl, ws, sx, ox, px, state, cb, sb, ob, pb, mom_a, mom_b,
    nf, bm, f2, fg, ps2, got2, sum2, ps, got, sums, wide_f, pick, em, pr,
    subspace, eigen,
    local_sem, send_sem, recv_sem, all_sem, field_sem, out_sem,
):
    me = lax.axis_index(AXIS)
    own = [
        pltpu.make_async_copy(conductivity, cb.at[2], local_sem.at[1]),
        pltpu.make_async_copy(source, sb.at[1], local_sem.at[2]),
        pltpu.make_async_copy(observed, ob.at[1], local_sem.at[3]),
        pltpu.make_async_copy(precision, pb.at[1], local_sem.at[4]),
        pltpu.make_async_copy(subspace_hbm, subspace, local_sem.at[5]),
        pltpu.make_async_copy(eigen_hbm, eigen, local_sem.at[6]),
    ]
    logs = [
        pltpu.make_async_copy(log_field.at[:, x, :], lf.at[RD + x], field_sem.at[x]) for x in range(RD)
    ]
    noises = [
        pltpu.make_async_copy(noise_field.at[:, x, :], nf.at[x], field_sem.at[RD + x]) for x in range(RD)
    ]
    barrier = greet_all(me)
    for copy in own + logs + noises:
        copy.start()

    def fetch(r, carry):
        pltpu.make_async_copy(
            basis.at[r], bm.at[pl.ds(pl.multiple_of(RD * r, RD), RD)], local_sem.at[0]
        ).start()
        return carry

    lax.fori_loop(0, basis.shape[0], fetch, 0, unroll=8)
    for copy in own + logs:
        copy.wait()
    pl.semaphore_wait(barrier, N - 1)

    count = [0]

    def remote(src, dst, shift):
        index = count[0]
        count[0] += 1
        copy = pltpu.make_async_remote_copy(
            src_ref=src, dst_ref=dst, send_sem=send_sem.at[index], recv_sem=recv_sem.at[index],
            device_id=(lax.rem(me + shift + N, N),), device_id_type=MESH_ID,
        )
        copy.start()
        return copy

    early = []
    for block, src, centre in ((cb, 2, 2), (sb, 1, 1)):
        early.append(remote(block.at[src], block.at[centre - 1], 1))
        early.append(remote(block.at[src], block.at[centre + 1], -1))
    early.append(remote(cb.at[2], cb.at[0], 2))
    early.append(remote(cb.at[2], cb.at[4], -2))
    rows = []
    for i in range(RD):
        rows.append(
            (
                remote(lf.at[2 * RD - 1 - i], lf.at[RD - 1 - i], 1),
                remote(lf.at[RD + i], lf.at[2 * RD + i], -1),
            )
        )
    late = []
    for block in (ob, pb):
        late.append(remote(block.at[1], block.at[0], 1))
        late.append(remote(block.at[1], block.at[2], -1))

    for x in range(RD):
        f2[pl.ds(16 * x, 16), :] = lf[RD + x].astype(jnp.bfloat16)
    for copy in noises:
        copy.wait()
    for x in range(RD):
        f2[pl.ds(64 + 16 * x, 16), :] = nf[x].astype(jnp.bfloat16)
    pltpu.make_async_copy(bm, bm, local_sem.at[0]).wait()
    project(f2, bm, ps2)

    for copy in early:
        copy.wait()

    lane = lax.broadcasted_iota(jnp.int32, (8, 128), 1)
    first = jnp.where(me == 0, 0.0, 1.0).astype(F32)
    last = jnp.where(me == N - 1, 0.0, 1.0).astype(F32)
    col = lax.broadcasted_iota(jnp.int32, (1, NY), 1)

    def crow(e):
        return cb[e // RD + 1, pl.ds(e % RD, 1), :]

    def edge(e):
        a, b = crow(e - 1), crow(e)
        if e == RD:
            a = first * a + (1.0 - first) * b
        if e == 2 * RD:
            b = last * b + (1.0 - last) * a
        return 0.5 * (a + b)

    for e in range(EXT + 1):
        wu[e] = jnp.broadcast_to(edge(e), (8, NY))
    for e in range(EXT):
        c = crow(e)
        before = jnp.where(col == 0, c, pltpu.roll(c, 1, 1))
        after = jnp.where(col == NY - 1, c, pltpu.roll(c, NY - 1, 1))
        left = 0.5 * (c + before)
        right = 0.5 * (c + after)
        wl[e] = jnp.broadcast_to(jnp.where(col == 0, 0.0, left), (8, NY))
        ws[e] = jnp.broadcast_to(left + right, (8, NY)) + wu[e] + wu[e + 1]
        sx[e] = jnp.broadcast_to(sb[e // RD, pl.ds(e % RD, 1), :], (8, NY))

    def start_row(e, keep):
        for g in range(2):
            gs = pl.ds(8 * g, 8)
            d = keep / (ws[e] + jnp.exp(lf[e, gs, :]))
            dinv[e, gs, :] = d
            v[0, e, gs, :] = sx[e] * d

    def own_start(e, carry):
        start_row(e, jnp.float32(1.0))
        return carry

    lax.fori_loop(RD, 2 * RD, own_start, 0)

    def moments_zero(side):
        zero = jnp.zeros((8, 128), F32)

        def row(e, carry):
            out = []
            for g in range(2):
                acc = carry[g]
                for j in range(TILES):
                    sl = pl.ds(128 * j, 128)
                    acc = acc + side(e, g, sl) * v[0, e, pl.ds(8 * g, 8), sl]
                out.append(acc)
            return tuple(out)

        return list(lax.fori_loop(RD, 2 * RD, row, (zero, zero)))

    accs = [moments_zero(lambda e, g, sl: sx[e, :, sl])]
    moved = []
    for i, (above, below) in enumerate(rows):
        above.wait()
        below.wait()
        start_row(RD - 1 - i, first)
        start_row(2 * RD + i, last)
        if i > 0:
            powers_pairs(v, wu, wl, dinv, lane, i, lambda k: (k, i - k))
        one, two = powers_own(v, i, wu, wl, dinv, lane)
        accs.append(one)
        if i < ITERS - 1:
            accs.append(two)
            moved.append(remote(v.at[i + 1, RD], v.at[i + 1, 0], 1))
            moved.append(remote(v.at[i + 1, 2 * RD - 1], v.at[i + 1, EXT - 1], -1))
    mom_a[me] = pack(accs)
    send_row_to_all(me, mom_a, all_sem.at[0], all_sem.at[1])

    def spread2(to):
        pltpu.make_async_remote_copy(
            src_ref=ps2.at[to], dst_ref=got2.at[me], send_sem=all_sem.at[4], recv_sem=all_sem.at[5],
            device_id=(to,), device_id_type=MESH_ID,
        ).start()
    for_peers(me, spread2)
    got2[me] = ps2[me]


    variance = 1.0 / (1.0 + eigen[...])
    below = 2.0 + 0.8 * variance
    factors = jnp.concatenate(
        [
            (2.0 - 0.8 * variance) / below,
            1.6 * variance / below,
            jnp.sqrt(6.4 * variance) / below,
            jnp.zeros((5, variance.shape[1]), F32),
            subspace[...],
        ],
        axis=0,
    )
    rank = factors.shape[1]
    row_id = lax.broadcasted_iota(jnp.int32, (rank, RD * rank), 0)
    lane_id = lax.broadcasted_iota(jnp.int32, (rank, RD * rank), 1)
    widen = jnp.where(lane_id // RD == row_id, 1.0, 0.0).astype(jnp.bfloat16)
    wide_f[...] = join_three(
        jnp.dot(in_three(factors), widen, preferred_element_type=F32), 8 + CH
    )
    row_id = lax.broadcasted_iota(jnp.int32, (RD * rank, rank), 0)
    lane_id = lax.broadcasted_iota(jnp.int32, (RD * rank, rank), 1)
    pick[...] = jnp.where(row_id == RD * lane_id, 1.0, 0.0).astype(jnp.bfloat16)

    for copy in late:
        copy.wait()
    for e in range(EXT):
        ox[e] = jnp.broadcast_to(ob[e // RD, pl.ds(e % RD, 1), :], (8, NY))
        px[e] = jnp.broadcast_to(pb[e // RD, pl.ds(e % RD, 1), :], (8, NY))
    moved[0].wait()
    moved[1].wait()
    powers_pairs(v, wu, wl, dinv, lane, 1, lambda step: (1, 3))
    moved[2].wait()
    moved[3].wait()
    powers_pairs(v, wu, wl, dinv, lane, 2, lambda step: (2, 2 + step))
    moved[4].wait()
    moved[5].wait()

    wait_rows(mom_a, all_sem.at[1])
    y, info = krylov_weights(unpack(jnp.sum(mom_a[...], axis=0)))
    info_ref[0] = jnp.broadcast_to(info, (CH, 128))

    wait_rows(got2, all_sem.at[5])
    sum2[me] = over_rows(jnp.sum(got2[...], axis=0))
    send_row_to_all(me, sum2, all_sem.at[6], all_sem.at[7])

    def adjoint_start(e, carry):
        out = []
        for g in range(2):
            acc = carry[g]
            gs = pl.ds(8 * g, 8)
            yg = [jnp.broadcast_to(y[k][8 * g:8 * g + 8], (8, 128)) for k in range(ITERS)]
            for j in range(TILES):
                sl = pl.ds(128 * j, 128)
                x = yg[0] * v[0, e, gs, sl]
                for k in range(1, ITERS):
                    x = x + yg[k] * v[k, e, gs, sl]
                side = px[e, :, sl] * (x - ox[e, :, sl])
                new = side * dinv[e, gs, sl]
                state[e, gs, sl] = x
                v[0, e, gs, sl] = new
                acc = acc + side * new
            out.append(acc)
        return tuple(out)

    zero = jnp.zeros((8, 128), F32)
    lax.fori_loop(0, RD, adjoint_start, (zero, zero))
    lax.fori_loop(2 * RD, EXT, adjoint_start, (zero, zero))
    accs = [list(lax.fori_loop(RD, 2 * RD, adjoint_start, (zero, zero)))]
    for k in range(ITERS):
        one, two = powers_own(v, k, wu, wl, dinv, lane)
        accs.append(one)
        if k < ITERS - 1:
            accs.append(two)
            powers_pairs(v, wu, wl, dinv, lane, RD - 1 - k, lambda step: (k, 1 + step))
    mom_b[me] = pack(accs)
    send_row_to_all(me, mom_b, all_sem.at[2], all_sem.at[3])
    wait_rows(mom_b, all_sem.at[3])
    y, info = krylov_weights(unpack(jnp.sum(mom_b[...], axis=0)))
    info_ref[1] = jnp.broadcast_to(info, (CH, 128))

    for r in range(RD):
        for h in range(4):
            sl = pl.ds(512 * h, 512)
            adj = y[0] * v[0, r + RD, :, sl]
            for k in range(1, ITERS):
                adj = adj + y[k] * v[k, r + RD, :, sl]
            value = -jnp.exp(lf[r + RD, :, sl]) * adj * state[r + RD, :, sl]
            fg[pl.ds(16 * r, 16), sl] = value.astype(jnp.bfloat16)
    project(fg, bm, ps)

    def spread(to):
        pltpu.make_async_remote_copy(
            src_ref=ps.at[to // CH, pl.ds(to % CH, 1)], dst_ref=got.at[me],
            send_sem=all_sem.at[8], recv_sem=all_sem.at[9],
            device_id=(to,), device_id_type=MESH_ID,
        ).start()
    for_peers(me, spread)
    got[me] = ps[me // CH, pl.ds(me % CH, 1), :]
    wait_rows(got, all_sem.at[9])
    sums[me] = over_rows(jnp.sum(got[...], axis=0))
    send_row_to_all(me, sums, all_sem.at[10], all_sem.at[11])
    wait_rows(sum2, all_sem.at[7])
    wait_rows(sums, all_sem.at[11])

    lane = lax.broadcasted_iota(jnp.int32, (CH, 128), 1) % RD
    pieces = []
    for b in range(8):
        rows = pl.ds(16 * b, 16)
        cols = pl.ds(128 * b, 128)
        state_coef, noise_coef = sum2[rows, 0, :], sum2[rows, 1, :]
        new = wide_f[0:1, cols] * state_coef - wide_f[1:2, cols] * sums[rows, 0, :]
        new = new + wide_f[2:3, cols] * wide_f[8 : 8 + CH, cols]
        correction = new - 0.6 * state_coef - 0.8 * noise_coef
        for x in range(RD):
            em[pl.ds(16 * x, 16), cols] = jnp.where(lane == x, correction, 0.0).astype(jnp.bfloat16)
        pieces.append(new)
    for h in range(4):
        sl = pl.ds(512 * h, 512)
        rebuilt = jnp.dot(em[...], bm[:, sl], preferred_element_type=F32)
        for x in range(RD):
            pr[x, :, sl] = 0.6 * lf[RD + x, :, sl] + 0.8 * nf[x, :, sl] + rebuilt[16 * x : 16 * x + 16]
    results = [pltpu.make_async_copy(pr.at[x], proposal.at[:, x, :], out_sem.at[x]) for x in range(RD)]
    for copy in results:
        copy.start()
    coef_ref[...] = join_three(
        jnp.dot(in_three(jnp.concatenate(pieces, axis=1)), pick[...], preferred_element_type=F32), CH
    )
    for buf, sem in ((mom_a, 0), (mom_b, 2), (got2, 4), (sum2, 6), (got, 8), (sums, 10)):
        wait_rows(buf, all_sem.at[sem])
    for copy in results:
        copy.wait()


def per_device(
    source, observed, precision, conductivity, log_field, noise_field, subspace_noise, eigenvalues, basis,
):
    any_space = pl.BlockSpec(memory_space=pltpu.HBM)
    vmem = pl.BlockSpec(memory_space=pltpu.VMEM)
    rank = eigenvalues.shape[0]
    wide = pltpu.VMEM((EXT, CH, NY), F32)
    row8 = pltpu.VMEM((EXT, 8, NY), F32)
    small = pltpu.VMEM((3, RD, NY), F32)
    one = pltpu.VMEM((N, 1, 128), F32)
    two = pltpu.VMEM((N, 2, 128), F32)
    half = jnp.bfloat16
    proposal, new_coef, info = pl.pallas_call(
        step_kernel,
        out_shape=(
            jax.ShapeDtypeStruct(log_field.shape, F32),
            jax.ShapeDtypeStruct((CH, rank), F32),
            jax.ShapeDtypeStruct((2, CH, 128), F32),
        ),
        in_specs=[any_space] * 9,
        out_specs=(any_space, vmem, vmem),
        scratch_shapes=[
            wide, wide, pltpu.VMEM((ITERS, EXT, CH, NY), F32),
            pltpu.VMEM((EXT + 1, 8, NY), F32), row8, row8, row8, row8, row8, wide,
            pltpu.VMEM((5, RD, NY), F32), small, small, small, one, one,
            pltpu.VMEM((RD, CH, NY), F32),
            pltpu.VMEM((RD * rank, NY), half),
            pltpu.VMEM((2 * RD * CH, NY), half),
            pltpu.VMEM((RD * CH, NY), half),
            two, two, two,
            pltpu.VMEM((8, CH, 128), F32), one, one,
            pltpu.VMEM((8 + CH, RD * rank), F32),
            pltpu.VMEM((RD * rank, rank), half),
            pltpu.VMEM((RD * CH, RD * rank), half),
            pltpu.VMEM((RD, CH, NY), F32),
            pltpu.VMEM((CH, rank), F32), pltpu.VMEM((1, rank), F32),
            pltpu.SemaphoreType.DMA((7,)),
            pltpu.SemaphoreType.DMA((24,)),
            pltpu.SemaphoreType.DMA((24,)),
            pltpu.SemaphoreType.DMA((12,)),
            pltpu.SemaphoreType.DMA((8,)),
            pltpu.SemaphoreType.DMA((4,)),
        ],
        compiler_params=pltpu.CompilerParams(
            collective_id=0, has_side_effects=True, vmem_limit_bytes=66_900_000
        ),
    )(
        source, observed, precision, conductivity, log_field, noise_field,
        subspace_noise, eigenvalues.reshape(1, rank), basis,
    )
    return (proposal, new_coef)


def solution(mesh):
    return jax.shard_map(
        per_device,
        mesh=mesh,
        in_specs=(
            P(AXIS, None), P(AXIS, None), P(AXIS, None), P(AXIS, None),
            P(None, AXIS, None), P(None, AXIS, None), P(), P(), P(None, AXIS, None),
        ),
        out_specs=(P(None, AXIS, None), P()),
        check_vma=False,
    )
```

```python
import functools

import jax
import jax.numpy as jnp
from jax import lax
from jax.experimental import pallas as pl
from jax.experimental.pallas import tpu as pltpu
from jax.sharding import PartitionSpec as P

ITERS = 4
AXIS = "rows"
N = 128
RD = 4
NY = 2048
CH = 16
EXT = 12
TILES = NY // 128
MESH_ID = pl.DeviceIdType.MESH
F32 = jnp.float32


def far_first(turn):
    return lax.rem(2 + 3 * turn + 3 * (turn * (turn - 1) // 2), 4)


def for_peers(me, act):
    near = []
    for z in (2, 1, 3, 0):
        for c in (1, 0):
            near.append(lax.rem(me + c, 2) + 2 * lax.rem(me // 2 + z, 4))

    def plane(turn, carry):
        y = lax.rem(me // 8 + far_first(lax.rem(turn, 4)), 4)
        x = lax.rem(me // 32 + far_first(turn // 4), 4)
        for at in near:
            act(8 * y + 32 * x + at)
        return carry

    lax.fori_loop(0, 15, plane, 0)
    for at in near[:-1]:
        act(8 * (me // 8) + at)


def ring_peers(me, stride):
    at = lax.rem(me // stride, 4)
    return [me + stride * (lax.rem(at + d, 4) - at) for d in (2, 1, 3)]


def greet_near(me):
    column = 8 * (me // 8)
    near = [column + lax.rem(me + d, 8) for d in range(1, 8)]
    near += ring_peers(me, 8) + ring_peers(me, 32)
    near += [lax.rem(me + d + N, N) for d in (-2, 2, -1, 1)]
    barrier = pltpu.get_barrier_semaphore()
    for to in near:
        pl.semaphore_signal(barrier, inc=1, device_id=(to,), device_id_type=MESH_ID)
    return barrier, len(near)


def pass_on(me, sem, stride):
    for to in ring_peers(me, stride):
        pl.semaphore_signal(sem, inc=1, device_id=(to,), device_id_type=MESH_ID)


def send_row_to_all(me, buf, send_sem, recv_sem):
    def send(to):
        pltpu.make_async_remote_copy(
            src_ref=buf.at[me], dst_ref=buf.at[me], send_sem=send_sem, recv_sem=recv_sem,
            device_id=(to,), device_id_type=MESH_ID,
        ).start()

    for_peers(me, send)


def wait_rows(buf, sem):
    part = buf.at[pl.ds(0, N - 1)]
    pltpu.make_async_copy(part, part, sem).wait()


def pack(accs):
    lane = lax.broadcasted_iota(jnp.int32, (8, 128), 1)
    sub = lax.broadcasted_iota(jnp.int32, (8, 128), 0)
    row = jnp.zeros((8, 128), F32)
    for k in range(8):
        for g in range(2):
            total = jnp.sum(accs[k][g], axis=1, keepdims=True)
            row = row + jnp.where(lane == (g * 8 + k) * 8 + sub, total, 0.0)
    return jnp.sum(row, axis=0, keepdims=True)


def unpack(row):
    lane = lax.broadcasted_iota(jnp.int32, (8, 128), 1)
    sub = lax.broadcasted_iota(jnp.int32, (8, 128), 0)
    wide = jnp.broadcast_to(row, (8, 128))
    moments = []
    for k in range(8):
        halves = [
            jnp.sum(jnp.where(lane == (g * 8 + k) * 8 + sub, wide, 0.0), axis=1, keepdims=True)
            for g in range(2)
        ]
        moments.append(jnp.concatenate(halves, axis=0))
    return moments


def square(poly):
    out = [None] * (2 * len(poly) - 1)
    for i, a in enumerate(poly):
        for j, b in enumerate(poly):
            term = a * b
            out[i + j] = term if out[i + j] is None else out[i + j] + term
    return out


def krylov_weights(m):
    one = jnp.ones_like(m[0])
    rho, pi = [one], [one]
    y = [jnp.zeros_like(one)] * ITERS
    g = m[0]
    spread = g
    gain, noise = None, None
    for step in range(ITERS):
        s = square(pi)
        c = functools.reduce(lambda a, b: a + b, [s[l] * (m[l] - m[l + 1]) for l in range(len(s))])
        size = functools.reduce(
            lambda a, b: a + b, [jnp.abs(s[l]) * (jnp.abs(m[l]) + jnp.abs(m[l + 1])) for l in range(len(s))]
        )
        alpha = g / c
        part = alpha * g
        err = part * ((size / c) * (size / c) + (spread / g) * (spread / g))
        gain = part if gain is None else gain + part
        noise = err if noise is None else noise + err
        for k in range(len(pi)):
            y[k] = y[k] + alpha * pi[k]
        if step == ITERS - 1:
            break
        new = []
        for k in range(len(pi) + 1):
            value = rho[k] if k < len(rho) else None
            if k < len(pi):
                value = value - alpha * pi[k]
            if k > 0:
                moved = alpha * pi[k - 1]
                value = moved if value is None else value + moved
            new.append(value)
        rho = new
        s = square(rho)
        following = functools.reduce(lambda a, b: a + b, [s[l] * m[l] for l in range(len(s))])
        spread = functools.reduce(lambda a, b: a + b, [jnp.abs(s[l]) * jnp.abs(m[l]) for l in range(len(s))])
        beta = following / g
        g = following
        pi = [rho[k] + beta * pi[k] if k < len(pi) else rho[k] for k in range(len(rho))]
    return y, noise / gain


def apply_row(vk, vn, wu, wl, dinv, e, lane, accs):
    whole = pl.ds(0, 8)
    groups = (pl.ds(0, 8), pl.ds(8, 8))
    kept = {}

    def prepare(j):
        cols = pl.ds(128 * j, 128)
        w = wl[e, whole, cols]
        out = []
        for gs in groups:
            v = vk[e, gs, cols]
            out.append((v, pltpu.roll(v, 1, 1), pltpu.roll(w * v, 127, 1)))
        kept[j] = (w, out)

    prepare(0)
    for j in range(TILES):
        cols = pl.ds(128 * j, 128)
        if j + 1 < TILES:
            prepare(j + 1)
        w, here = kept[j]
        above, below = wu[e, whole, cols], wu[e + 1, whole, cols]
        for g, gs in enumerate(groups):
            v, moved, moved_back = here[g]
            left = moved if j == 0 else jnp.where(lane == 0, kept[j - 1][1][g][1], moved)
            right = jnp.where(lane == 127, kept[j + 1][1][g][2] if j + 1 < TILES else 0.0, moved_back)
            t = above * vk[e - 1, gs, cols] + below * vk[e + 1, gs, cols]
            t = t + (w * left + right)
            if accs is not None:
                accs[0][g] = accs[0][g] + t * v
            if vn is not None:
                new = t * dinv[e, gs, cols]
                vn[e, gs, cols] = new
                if accs is not None:
                    accs[1][g] = accs[1][g] + t * new


def powers_own(v, k, wu, wl, dinv, lane):
    zero = jnp.zeros((8, 128), F32)

    def rows(i, carry):
        accs = [list(carry[0]), list(carry[1])]
        for h in range(2):
            e = RD + 2 * i + h
            apply_row(v[k], v[k + 1] if k < ITERS - 1 else None, wu, wl, dinv, e, lane, accs)
        return tuple(accs[0]), tuple(accs[1])

    got = lax.fori_loop(0, RD // 2, rows, ((zero, zero), (zero, zero)))
    return list(got[0]), list(got[1])


def powers_pair(v, k, wu, wl, dinv, lane, i):
    for e in (RD - i, 2 * RD - 1 + i):
        apply_row(v[k], v[k + 1], wu, wl, dinv, e, lane, None)


def project(fields, basis_rows, out):
    count = fields.shape[0] // (RD * CH)
    lane = lax.broadcasted_iota(jnp.int32, (CH, 256), 1) % RD
    for q in range(4):
        full = lax.dot_general(
            fields[...], basis_rows[pl.ds(256 * q, 256), :], (((1,), (1,)), ((), ())),
            preferred_element_type=F32,
        )
        for f in range(count):
            rows = full[64 * f : 64 * f + 64]
            part = rows[48:64]
            for x in range(RD - 1):
                part = jnp.where(lane == x, rows[16 * x : 16 * x + 16], part)
            for h in range(2):
                piece = part[:, 128 * h : 128 * h + 128]
                if count == 1:
                    out[2 * q + h] = piece
                else:
                    out[pl.ds(16 * (2 * q + h), 16), f, :] = piece


def over_rows(value):
    lane = lax.broadcasted_iota(jnp.int32, value.shape, 1)
    pair = value + jnp.where(lane % 2 == 0, pltpu.roll(value, 127, 1), pltpu.roll(value, 1, 1))
    return pair + jnp.where(lane % 4 < 2, pltpu.roll(pair, 126, 1), pltpu.roll(pair, 2, 1))


def in_three(value):
    high = value.astype(jnp.bfloat16)
    rest = value - high.astype(F32)
    middle = rest.astype(jnp.bfloat16)
    low = (rest - middle.astype(F32)).astype(jnp.bfloat16)
    return jnp.concatenate([high, middle, low], axis=0)


def join_three(value, count):
    return value[:count] + value[count : 2 * count] + value[2 * count : 3 * count]


def step_kernel(
    source, observed, precision, conductivity, log_field, noise_field, subspace_hbm, eigen_hbm, basis,
    proposal, coef_ref, info_ref,
    lf, dinv, v0, v1, v2, v3, wu, wl, ws, sx, ox, px, state, cb, sb, ob, pb, mom_a, mom_b,
    nf, bm, f2, fg, ps2, got2, sum2, ps, got, sums, wide_f, pick, em, pr,
    subspace, eigen,
    local_sem, send_sem, recv_sem, all_sem, field_sem, out_sem, ring_sem,
):
    me = lax.axis_index(AXIS)
    v = (v0, v1, v2, v3)
    own = [
        pltpu.make_async_copy(conductivity, cb.at[2], local_sem.at[1]),
        pltpu.make_async_copy(source, sb.at[1], local_sem.at[2]),
        pltpu.make_async_copy(observed, ob.at[1], local_sem.at[3]),
        pltpu.make_async_copy(precision, pb.at[1], local_sem.at[4]),
        pltpu.make_async_copy(subspace_hbm, subspace, local_sem.at[5]),
        pltpu.make_async_copy(eigen_hbm, eigen, local_sem.at[6]),
    ]
    logs = [
        pltpu.make_async_copy(log_field.at[:, x, :], lf.at[RD + x], field_sem.at[x]) for x in range(RD)
    ]
    noises = [
        pltpu.make_async_copy(noise_field.at[:, x, :], nf.at[x], field_sem.at[RD + x]) for x in range(RD)
    ]
    barrier, greeted = greet_near(me)
    for copy in own + logs + noises:
        copy.start()

    def fetch(r, carry):
        pltpu.make_async_copy(
            basis.at[r], bm.at[pl.ds(pl.multiple_of(RD * r, RD), RD)], local_sem.at[0]
        ).start()
        return carry

    lax.fori_loop(0, basis.shape[0], fetch, 0, unroll=8)
    for copy in own + logs:
        copy.wait()
    pl.semaphore_wait(barrier, greeted)
    pass_on(me, ring_sem.at[0], 8)

    count = [0]

    def remote(src, dst, shift):
        index = count[0]
        count[0] += 1
        copy = pltpu.make_async_remote_copy(
            src_ref=src, dst_ref=dst, send_sem=send_sem.at[index], recv_sem=recv_sem.at[index],
            device_id=(lax.rem(me + shift + N, N),), device_id_type=MESH_ID,
        )
        copy.start()
        return copy

    early = []
    for block, src, centre in ((cb, 2, 2), (sb, 1, 1)):
        early.append(remote(block.at[src], block.at[centre - 1], 1))
        early.append(remote(block.at[src], block.at[centre + 1], -1))
    early.append(remote(cb.at[2], cb.at[0], 2))
    early.append(remote(cb.at[2], cb.at[4], -2))
    rows = []
    for i in range(RD):
        rows.append(
            (
                remote(lf.at[2 * RD - 1 - i], lf.at[RD - 1 - i], 1),
                remote(lf.at[RD + i], lf.at[2 * RD + i], -1),
            )
        )
    late = []
    for block in (ob, pb):
        late.append(remote(block.at[1], block.at[0], 1))
        late.append(remote(block.at[1], block.at[2], -1))

    for x in range(RD):
        f2[pl.ds(16 * x, 16), :] = lf[RD + x].astype(jnp.bfloat16)
    for copy in noises:
        copy.wait()
    for x in range(RD):
        f2[pl.ds(64 + 16 * x, 16), :] = nf[x].astype(jnp.bfloat16)
    pltpu.make_async_copy(bm, bm, local_sem.at[0]).wait()
    project(f2, bm, ps2)
    pl.semaphore_wait(ring_sem.at[0], 3)
    pass_on(me, ring_sem.at[1], 32)

    for copy in early:
        copy.wait()

    lane = lax.broadcasted_iota(jnp.int32, (8, 128), 1)
    first = jnp.where(me == 0, 0.0, 1.0).astype(F32)
    last = jnp.where(me == N - 1, 0.0, 1.0).astype(F32)
    col = lax.broadcasted_iota(jnp.int32, (1, NY), 1)

    def crow(e):
        return cb[e // RD + 1, pl.ds(e % RD, 1), :]

    def edge(e):
        a, b = crow(e - 1), crow(e)
        if e == RD:
            a = first * a + (1.0 - first) * b
        if e == 2 * RD:
            b = last * b + (1.0 - last) * a
        return 0.5 * (a + b)

    for e in range(EXT + 1):
        wu[e] = jnp.broadcast_to(edge(e), (8, NY))
    for e in range(EXT):
        c = crow(e)
        before = jnp.where(col == 0, c, pltpu.roll(c, 1, 1))
        after = jnp.where(col == NY - 1, c, pltpu.roll(c, NY - 1, 1))
        left = 0.5 * (c + before)
        right = 0.5 * (c + after)
        wl[e] = jnp.broadcast_to(jnp.where(col == 0, 0.0, left), (8, NY))
        ws[e] = jnp.broadcast_to(left + right, (8, NY)) + wu[e] + wu[e + 1]
        sx[e] = jnp.broadcast_to(sb[e // RD, pl.ds(e % RD, 1), :], (8, NY))

    def start_row(e, keep):
        for g in range(2):
            gs = pl.ds(8 * g, 8)
            d = keep / (ws[e] + jnp.exp(lf[e, gs, :]))
            dinv[e, gs, :] = d
            v0[e, gs, :] = sx[e] * d

    def own_start(e, carry):
        start_row(e, jnp.float32(1.0))
        return carry

    lax.fori_loop(RD, 2 * RD, own_start, 0)

    def moments_zero(side):
        zero = jnp.zeros((8, 128), F32)

        def row(e, carry):
            out = []
            for g in range(2):
                acc = carry[g]
                for j in range(TILES):
                    sl = pl.ds(128 * j, 128)
                    acc = acc + side(e, g, sl) * v0[e, pl.ds(8 * g, 8), sl]
                out.append(acc)
            return tuple(out)

        return list(lax.fori_loop(RD, 2 * RD, row, (zero, zero)))

    accs = [moments_zero(lambda e, g, sl: sx[e, :, sl])]
    moved = []
    for i, (above, below) in enumerate(rows):
        above.wait()
        below.wait()
        start_row(RD - 1 - i, first)
        start_row(2 * RD + i, last)
        for k in range(i):
            powers_pair(v, k, wu, wl, dinv, lane, i - k)
        one, two = powers_own(v, i, wu, wl, dinv, lane)
        accs.append(one)
        if i < ITERS - 1:
            accs.append(two)
            moved.append(remote(v[i + 1].at[RD], v[i + 1].at[0], 1))
            moved.append(remote(v[i + 1].at[2 * RD - 1], v[i + 1].at[EXT - 1], -1))
    mom_a[me] = pack(accs)
    pl.semaphore_wait(ring_sem.at[1], 3)
    send_row_to_all(me, mom_a, all_sem.at[0], all_sem.at[1])

    for copy in late:
        copy.wait()
    for e in range(EXT):
        ox[e] = jnp.broadcast_to(ob[e // RD, pl.ds(e % RD, 1), :], (8, NY))
        px[e] = jnp.broadcast_to(pb[e // RD, pl.ds(e % RD, 1), :], (8, NY))
    moved[0].wait()
    moved[1].wait()
    powers_pair(v, 1, wu, wl, dinv, lane, 3)
    moved[2].wait()
    moved[3].wait()
    powers_pair(v, 2, wu, wl, dinv, lane, 2)
    powers_pair(v, 2, wu, wl, dinv, lane, 3)
    moved[4].wait()
    moved[5].wait()

    wait_rows(mom_a, all_sem.at[1])
    y, info = krylov_weights(unpack(jnp.sum(mom_a[...], axis=0)))
    info_ref[0] = jnp.broadcast_to(info, (CH, 128))

    def adjoint_start(e, carry):
        out = []
        for g in range(2):
            acc = carry[g]
            gs = pl.ds(8 * g, 8)
            yg = [jnp.broadcast_to(y[k][8 * g:8 * g + 8], (8, 128)) for k in range(ITERS)]
            for j in range(TILES):
                sl = pl.ds(128 * j, 128)
                x = yg[0] * v0[e, gs, sl]
                for k in range(1, ITERS):
                    x = x + yg[k] * v[k][e, gs, sl]
                side = px[e, :, sl] * (x - ox[e, :, sl])
                new = side * dinv[e, gs, sl]
                state[e, gs, sl] = x
                v0[e, gs, sl] = new
                acc = acc + side * new
            out.append(acc)
        return tuple(out)

    zero = jnp.zeros((8, 128), F32)
    lax.fori_loop(0, RD, adjoint_start, (zero, zero))
    lax.fori_loop(2 * RD, EXT, adjoint_start, (zero, zero))
    accs = [list(lax.fori_loop(RD, 2 * RD, adjoint_start, (zero, zero)))]
    for k in range(ITERS):
        one, two = powers_own(v, k, wu, wl, dinv, lane)
        accs.append(one)
        if k < ITERS - 1:
            accs.append(two)
            for i in range(1, RD - k):
                powers_pair(v, k, wu, wl, dinv, lane, i)
    mom_b[me] = pack(accs)
    send_row_to_all(me, mom_b, all_sem.at[2], all_sem.at[3])

    def spread2(to):
        pltpu.make_async_remote_copy(
            src_ref=ps2.at[to], dst_ref=got2.at[me], send_sem=all_sem.at[4], recv_sem=all_sem.at[5],
            device_id=(to,), device_id_type=MESH_ID,
        ).start()
    for_peers(me, spread2)
    got2[me] = ps2[me]


    variance = 1.0 / (1.0 + eigen[...])
    below = 2.0 + 0.8 * variance
    factors = jnp.concatenate(
        [
            (2.0 - 0.8 * variance) / below,
            1.6 * variance / below,
            jnp.sqrt(6.4 * variance) / below,
            jnp.zeros((5, variance.shape[1]), F32),
            subspace[...],
        ],
        axis=0,
    )
    rank = factors.shape[1]
    row_id = lax.broadcasted_iota(jnp.int32, (rank, RD * rank), 0)
    lane_id = lax.broadcasted_iota(jnp.int32, (rank, RD * rank), 1)
    widen = jnp.where(lane_id // RD == row_id, 1.0, 0.0).astype(jnp.bfloat16)
    wide_f[...] = join_three(
        jnp.dot(in_three(factors), widen, preferred_element_type=F32), 8 + CH
    )
    row_id = lax.broadcasted_iota(jnp.int32, (RD * rank, rank), 0)
    lane_id = lax.broadcasted_iota(jnp.int32, (RD * rank, rank), 1)
    pick[...] = jnp.where(row_id == RD * lane_id, 1.0, 0.0).astype(jnp.bfloat16)

    wait_rows(mom_b, all_sem.at[3])
    y, info = krylov_weights(unpack(jnp.sum(mom_b[...], axis=0)))
    info_ref[1] = jnp.broadcast_to(info, (CH, 128))

    for r in range(RD):
        for h in range(4):
            sl = pl.ds(512 * h, 512)
            adj = y[0] * v0[r + RD, :, sl]
            for k in range(1, ITERS):
                adj = adj + y[k] * v[k][r + RD, :, sl]
            value = -jnp.exp(lf[r + RD, :, sl]) * adj * state[r + RD, :, sl]
            fg[pl.ds(16 * r, 16), sl] = value.astype(jnp.bfloat16)
    project(fg, bm, ps)

    def spread(to):
        pltpu.make_async_remote_copy(
            src_ref=ps.at[to // CH, pl.ds(to % CH, 1)], dst_ref=got.at[me],
            send_sem=all_sem.at[8], recv_sem=all_sem.at[9],
            device_id=(to,), device_id_type=MESH_ID,
        ).start()
    for_peers(me, spread)
    got[me] = ps[me // CH, pl.ds(me % CH, 1), :]
    wait_rows(got2, all_sem.at[5])
    sum2[me] = over_rows(jnp.sum(got2[...], axis=0))
    send_row_to_all(me, sum2, all_sem.at[6], all_sem.at[7])

    wait_rows(got, all_sem.at[9])
    sums[me] = over_rows(jnp.sum(got[...], axis=0))
    send_row_to_all(me, sums, all_sem.at[10], all_sem.at[11])
    wait_rows(sum2, all_sem.at[7])
    wait_rows(sums, all_sem.at[11])

    lane = lax.broadcasted_iota(jnp.int32, (CH, 128), 1) % RD
    pieces = []
    for b in range(8):
        rows = pl.ds(16 * b, 16)
        cols = pl.ds(128 * b, 128)
        state_coef, noise_coef = sum2[rows, 0, :], sum2[rows, 1, :]
        new = wide_f[0:1, cols] * state_coef - wide_f[1:2, cols] * sums[rows, 0, :]
        new = new + wide_f[2:3, cols] * wide_f[8 : 8 + CH, cols]
        correction = new - 0.6 * state_coef - 0.8 * noise_coef
        for x in range(RD):
            em[pl.ds(16 * x, 16), cols] = jnp.where(lane == x, correction, 0.0).astype(jnp.bfloat16)
        pieces.append(new)
    for h in range(4):
        sl = pl.ds(512 * h, 512)
        rebuilt = jnp.dot(em[...], bm[:, sl], preferred_element_type=F32)
        for x in range(RD):
            pr[x, :, sl] = 0.6 * lf[RD + x, :, sl] + 0.8 * nf[x, :, sl] + rebuilt[16 * x : 16 * x + 16]
    results = [pltpu.make_async_copy(pr.at[x], proposal.at[:, x, :], out_sem.at[x]) for x in range(RD)]
    for copy in results:
        copy.start()
    coef_ref[...] = join_three(
        jnp.dot(in_three(jnp.concatenate(pieces, axis=1)), pick[...], preferred_element_type=F32), CH
    )
    for buf, sem in ((mom_a, 0), (mom_b, 2), (got2, 4), (sum2, 6), (got, 8), (sums, 10)):
        wait_rows(buf, all_sem.at[sem])
    for copy in results:
        copy.wait()


def per_device(
    source, observed, precision, conductivity, log_field, noise_field, subspace_noise, eigenvalues, basis,
):
    any_space = pl.BlockSpec(memory_space=pltpu.HBM)
    vmem = pl.BlockSpec(memory_space=pltpu.VMEM)
    rank = eigenvalues.shape[0]
    wide = pltpu.VMEM((EXT, CH, NY), F32)
    row8 = pltpu.VMEM((EXT, 8, NY), F32)
    small = pltpu.VMEM((3, RD, NY), F32)
    one = pltpu.VMEM((N, 1, 128), F32)
    two = pltpu.VMEM((N, 2, 128), F32)
    half = jnp.bfloat16
    proposal, new_coef, info = pl.pallas_call(
        step_kernel,
        out_shape=(
            jax.ShapeDtypeStruct(log_field.shape, F32),
            jax.ShapeDtypeStruct((CH, rank), F32),
            jax.ShapeDtypeStruct((2, CH, 128), F32),
        ),
        in_specs=[any_space] * 9,
        out_specs=(any_space, vmem, vmem),
        scratch_shapes=[
            wide, wide, wide, wide, wide, wide,
            pltpu.VMEM((EXT + 1, 8, NY), F32), row8, row8, row8, row8, row8, wide,
            pltpu.VMEM((5, RD, NY), F32), small, small, small, one, one,
            pltpu.VMEM((RD, CH, NY), F32),
            pltpu.VMEM((RD * rank, NY), half),
            pltpu.VMEM((2 * RD * CH, NY), half),
            pltpu.VMEM((RD * CH, NY), half),
            two, two, two,
            pltpu.VMEM((8, CH, 128), F32), one, one,
            pltpu.VMEM((8 + CH, RD * rank), F32),
            pltpu.VMEM((RD * rank, rank), half),
            pltpu.VMEM((RD * CH, RD * rank), half),
            pltpu.VMEM((RD, CH, NY), F32),
            pltpu.VMEM((CH, rank), F32), pltpu.VMEM((1, rank), F32),
            pltpu.SemaphoreType.DMA((7,)),
            pltpu.SemaphoreType.DMA((24,)),
            pltpu.SemaphoreType.DMA((24,)),
            pltpu.SemaphoreType.DMA((12,)),
            pltpu.SemaphoreType.DMA((8,)),
            pltpu.SemaphoreType.DMA((4,)),
            pltpu.SemaphoreType.REGULAR((2,)),
        ],
        compiler_params=pltpu.CompilerParams(
            collective_id=0, has_side_effects=True, vmem_limit_bytes=66_900_000
        ),
    )(
        source, observed, precision, conductivity, log_field, noise_field,
        subspace_noise, eigenvalues.reshape(1, rank), basis,
    )
    return (proposal, new_coef)


def solution(mesh):
    return jax.shard_map(
        per_device,
        mesh=mesh,
        in_specs=(
            P(AXIS, None), P(AXIS, None), P(AXIS, None), P(AXIS, None),
            P(None, AXIS, None), P(None, AXIS, None), P(), P(), P(None, AXIS, None),
        ),
        out_specs=(P(None, AXIS, None), P()),
        check_vma=False,
    )
```

```python
import functools

import jax
import jax.numpy as jnp
from jax import lax
from jax.experimental import pallas as pl
from jax.experimental.pallas import tpu as pltpu
from jax.sharding import PartitionSpec as P

ITERS = 4
AXIS = "rows"
N = 128
RD = 4
NY = 2048
CH = 16
EXT = 12
TILES = NY // 128
MESH_ID = pl.DeviceIdType.MESH
F32 = jnp.float32


def far_first(turn):
    return lax.rem(2 + 3 * turn + 3 * (turn * (turn - 1) // 2), 4)


def for_peers(me, act):
    near = []
    for z in (2, 1, 3, 0):
        for c in (1, 0):
            near.append(lax.rem(me + c, 2) + 2 * lax.rem(me // 2 + z, 4))

    def plane(turn, carry):
        y = lax.rem(me // 8 + far_first(lax.rem(turn, 4)), 4)
        x = lax.rem(me // 32 + far_first(turn // 4), 4)
        for at in near:
            act(8 * y + 32 * x + at)
        return carry

    lax.fori_loop(0, 15, plane, 0)
    for at in near[:-1]:
        act(8 * (me // 8) + at)


def ring_peers(me, stride):
    at = lax.rem(me // stride, 4)
    return [me + stride * (lax.rem(at + d, 4) - at) for d in (2, 1, 3)]


def greet_near(me):
    column = 8 * (me // 8)
    near = [column + lax.rem(me + d, 8) for d in range(1, 8)]
    near += ring_peers(me, 8) + ring_peers(me, 32)
    near += [lax.rem(me + d + N, N) for d in (-2, 2, -1, 1)]
    barrier = pltpu.get_barrier_semaphore()
    for to in near:
        pl.semaphore_signal(barrier, inc=1, device_id=(to,), device_id_type=MESH_ID)
    return barrier, len(near)


def pass_on(me, sem, stride):
    for to in ring_peers(me, stride):
        pl.semaphore_signal(sem, inc=1, device_id=(to,), device_id_type=MESH_ID)


def send_row_to_all(me, buf, send_sem, recv_sem):
    def send(to):
        pltpu.make_async_remote_copy(
            src_ref=buf.at[me], dst_ref=buf.at[me], send_sem=send_sem, recv_sem=recv_sem,
            device_id=(to,), device_id_type=MESH_ID,
        ).start()

    for_peers(me, send)


def wait_rows(buf, sem):
    part = buf.at[pl.ds(0, N - 1)]
    pltpu.make_async_copy(part, part, sem).wait()


def pack(accs):
    lane = lax.broadcasted_iota(jnp.int32, (8, 128), 1)
    sub = lax.broadcasted_iota(jnp.int32, (8, 128), 0)
    row = jnp.zeros((8, 128), F32)
    for k in range(8):
        for g in range(2):
            total = jnp.sum(accs[k][g], axis=1, keepdims=True)
            row = row + jnp.where(lane == (g * 8 + k) * 8 + sub, total, 0.0)
    return jnp.sum(row, axis=0, keepdims=True)


def unpack(row):
    lane = lax.broadcasted_iota(jnp.int32, (8, 128), 1)
    sub = lax.broadcasted_iota(jnp.int32, (8, 128), 0)
    wide = jnp.broadcast_to(row, (8, 128))
    moments = []
    for k in range(8):
        halves = [
            jnp.sum(jnp.where(lane == (g * 8 + k) * 8 + sub, wide, 0.0), axis=1, keepdims=True)
            for g in range(2)
        ]
        moments.append(jnp.concatenate(halves, axis=0))
    return moments


def square(poly):
    out = [None] * (2 * len(poly) - 1)
    for i, a in enumerate(poly):
        for j, b in enumerate(poly):
            term = a * b
            out[i + j] = term if out[i + j] is None else out[i + j] + term
    return out


def krylov_weights(m):
    one = jnp.ones_like(m[0])
    rho, pi = [one], [one]
    y = [jnp.zeros_like(one)] * ITERS
    g = m[0]
    spread = g
    gain, noise = None, None
    for step in range(ITERS):
        s = square(pi)
        c = functools.reduce(lambda a, b: a + b, [s[l] * (m[l] - m[l + 1]) for l in range(len(s))])
        size = functools.reduce(
            lambda a, b: a + b, [jnp.abs(s[l]) * (jnp.abs(m[l]) + jnp.abs(m[l + 1])) for l in range(len(s))]
        )
        alpha = g / c
        part = alpha * g
        err = part * ((size / c) * (size / c) + (spread / g) * (spread / g))
        gain = part if gain is None else gain + part
        noise = err if noise is None else noise + err
        for k in range(len(pi)):
            y[k] = y[k] + alpha * pi[k]
        if step == ITERS - 1:
            break
        new = []
        for k in range(len(pi) + 1):
            value = rho[k] if k < len(rho) else None
            if k < len(pi):
                value = value - alpha * pi[k]
            if k > 0:
                moved = alpha * pi[k - 1]
                value = moved if value is None else value + moved
            new.append(value)
        rho = new
        s = square(rho)
        following = functools.reduce(lambda a, b: a + b, [s[l] * m[l] for l in range(len(s))])
        spread = functools.reduce(lambda a, b: a + b, [jnp.abs(s[l]) * jnp.abs(m[l]) for l in range(len(s))])
        beta = following / g
        g = following
        pi = [rho[k] + beta * pi[k] if k < len(pi) else rho[k] for k in range(len(rho))]
    return y, noise / gain


def apply_row(vk, vn, wu, wl, dinv, e, lane, accs):
    whole = pl.ds(0, 8)
    groups = (pl.ds(0, 8), pl.ds(8, 8))
    kept = {}

    def prepare(j):
        cols = pl.ds(128 * j, 128)
        w = wl[e, whole, cols]
        out = []
        for gs in groups:
            v = vk[e, gs, cols]
            out.append((v, pltpu.roll(v, 1, 1), pltpu.roll(w * v, 127, 1)))
        kept[j] = (w, out)

    prepare(0)
    for j in range(TILES):
        cols = pl.ds(128 * j, 128)
        if j + 1 < TILES:
            prepare(j + 1)
        w, here = kept[j]
        above, below = wu[e, whole, cols], wu[e + 1, whole, cols]
        for g, gs in enumerate(groups):
            v, moved, moved_back = here[g]
            left = moved if j == 0 else jnp.where(lane == 0, kept[j - 1][1][g][1], moved)
            right = jnp.where(lane == 127, kept[j + 1][1][g][2] if j + 1 < TILES else 0.0, moved_back)
            t = above * vk[e - 1, gs, cols] + below * vk[e + 1, gs, cols]
            t = t + (w * left + right)
            if accs is not None:
                accs[0][g] = accs[0][g] + t * v
            if vn is not None:
                new = t * dinv[e, gs, cols]
                vn[e, gs, cols] = new
                if accs is not None:
                    accs[1][g] = accs[1][g] + t * new


def powers_own(v, k, wu, wl, dinv, lane):
    zero = jnp.zeros((8, 128), F32)

    def rows(i, carry):
        accs = [list(carry[0]), list(carry[1])]
        for h in range(2):
            e = RD + 2 * i + h
            apply_row(v[k], v[k + 1] if k < ITERS - 1 else None, wu, wl, dinv, e, lane, accs)
        return tuple(accs[0]), tuple(accs[1])

    got = lax.fori_loop(0, RD // 2, rows, ((zero, zero), (zero, zero)))
    return list(got[0]), list(got[1])


def powers_pair(v, k, wu, wl, dinv, lane, i):
    for e in (RD - i, 2 * RD - 1 + i):
        apply_row(v[k], v[k + 1], wu, wl, dinv, e, lane, None)


def project(fields, basis_rows, out):
    count = fields.shape[0] // (RD * CH)
    lane = lax.broadcasted_iota(jnp.int32, (CH, 256), 1) % RD
    for q in range(4):
        full = lax.dot_general(
            fields[...], basis_rows[pl.ds(256 * q, 256), :], (((1,), (1,)), ((), ())),
            preferred_element_type=F32,
        )
        for f in range(count):
            rows = full[64 * f : 64 * f + 64]
            part = rows[48:64]
            for x in range(RD - 1):
                part = jnp.where(lane == x, rows[16 * x : 16 * x + 16], part)
            for h in range(2):
                piece = part[:, 128 * h : 128 * h + 128]
                if count == 1:
                    out[2 * q + h] = piece
                else:
                    out[pl.ds(16 * (2 * q + h), 16), f, :] = piece


def over_rows(value):
    lane = lax.broadcasted_iota(jnp.int32, value.shape, 1)
    pair = value + jnp.where(lane % 2 == 0, pltpu.roll(value, 127, 1), pltpu.roll(value, 1, 1))
    return pair + jnp.where(lane % 4 < 2, pltpu.roll(pair, 126, 1), pltpu.roll(pair, 2, 1))


def in_three(value):
    high = value.astype(jnp.bfloat16)
    rest = value - high.astype(F32)
    middle = rest.astype(jnp.bfloat16)
    low = (rest - middle.astype(F32)).astype(jnp.bfloat16)
    return jnp.concatenate([high, middle, low], axis=0)


def join_three(value, count):
    return value[:count] + value[count : 2 * count] + value[2 * count : 3 * count]


def empty_side(row, end, lf, cb, sb, ob, pb, v):
    block = row // RD
    lf[pl.ds(row, RD)] = jnp.zeros((RD, CH, NY), F32)
    for at in (0, 1):
        cb[(0 if row == 0 else 3) + at] = jnp.zeros((RD, NY), F32)
    for small in (sb, ob, pb):
        small[block] = jnp.zeros((RD, NY), F32)
    for power in v[1:]:
        power[end] = jnp.zeros((CH, NY), F32)


def step_kernel(
    source, observed, precision, conductivity, log_field, noise_field, subspace_hbm, eigen_hbm, basis,
    proposal, coef_ref, info_ref,
    lf, dinv, v0, v1, v2, v3, wu, wl, ws, sx, ox, px, state, cb, sb, ob, pb, mom_a, mom_b,
    nf, bm, f2, fg, ps2, got2, sum2, ps, got, sums, wide_f, pick, em, pr,
    subspace, eigen,
    local_sem, send_sem, recv_sem, all_sem, field_sem, out_sem, ring_sem,
):
    me = lax.axis_index(AXIS)
    v = (v0, v1, v2, v3)
    own = [
        pltpu.make_async_copy(conductivity, cb.at[2], local_sem.at[1]),
        pltpu.make_async_copy(source, sb.at[1], local_sem.at[2]),
        pltpu.make_async_copy(observed, ob.at[1], local_sem.at[3]),
        pltpu.make_async_copy(precision, pb.at[1], local_sem.at[4]),
        pltpu.make_async_copy(subspace_hbm, subspace, local_sem.at[5]),
        pltpu.make_async_copy(eigen_hbm, eigen, local_sem.at[6]),
    ]
    logs = [
        pltpu.make_async_copy(log_field.at[:, x, :], lf.at[RD + x], field_sem.at[x]) for x in range(RD)
    ]
    noises = [
        pltpu.make_async_copy(noise_field.at[:, x, :], nf.at[x], field_sem.at[RD + x]) for x in range(RD)
    ]
    barrier, greeted = greet_near(me)
    for copy in own + logs:
        copy.start()

    for copy in own + logs:
        copy.wait()
    pl.semaphore_wait(barrier, greeted)
    pass_on(me, ring_sem.at[0], 8)

    count = [0]
    sent = []

    def remote(src, dst, shift):
        index = count[0]
        count[0] += 1
        copy = pltpu.make_async_remote_copy(
            src_ref=src, dst_ref=dst, send_sem=send_sem.at[index], recv_sem=recv_sem.at[index],
            device_id=(lax.rem(me + shift + N, N),), device_id_type=MESH_ID,
        )
        goes = me + shift < N if shift > 0 else me + shift >= 0
        comes = me - shift >= 0 if shift > 0 else me - shift < N

        @pl.when(goes)
        def _():
            copy.start()

        sent.append((copy, goes))
        return copy, comes

    def arrived(*pairs):
        for copy, comes in pairs:

            @pl.when(comes)
            def _():
                copy.wait_recv()

    @pl.when(me == 0)
    def _():
        empty_side(0, 0, lf, cb, sb, ob, pb, v)

    @pl.when(me == N - 1)
    def _():
        empty_side(2 * RD, EXT - 1, lf, cb, sb, ob, pb, v)

    @pl.when(me == 1)
    def _():
        cb[0] = jnp.zeros((RD, NY), F32)

    @pl.when(me == N - 2)
    def _():
        cb[4] = jnp.zeros((RD, NY), F32)

    early = []
    for block, src, centre in ((cb, 2, 2), (sb, 1, 1)):
        early.append(remote(block.at[src], block.at[centre - 1], 1))
        early.append(remote(block.at[src], block.at[centre + 1], -1))
    early.append(remote(cb.at[2], cb.at[0], 2))
    early.append(remote(cb.at[2], cb.at[4], -2))
    rows = []
    for i in range(RD):
        rows.append(
            (
                remote(lf.at[2 * RD - 1 - i], lf.at[RD - 1 - i], 1),
                remote(lf.at[RD + i], lf.at[2 * RD + i], -1),
            )
        )
    late = []
    for block in (ob, pb):
        late.append(remote(block.at[1], block.at[0], 1))
        late.append(remote(block.at[1], block.at[2], -1))

    for copy in noises:
        copy.start()

    def fetch(r, carry):
        pltpu.make_async_copy(
            basis.at[r], bm.at[pl.ds(pl.multiple_of(RD * r, RD), RD)], local_sem.at[0]
        ).start()
        return carry

    lax.fori_loop(0, basis.shape[0], fetch, 0, unroll=8)
    for x in range(RD):
        f2[pl.ds(16 * x, 16), :] = lf[RD + x].astype(jnp.bfloat16)
    for copy in noises:
        copy.wait()
    for x in range(RD):
        f2[pl.ds(64 + 16 * x, 16), :] = nf[x].astype(jnp.bfloat16)
    pltpu.make_async_copy(bm, bm, local_sem.at[0]).wait()
    project(f2, bm, ps2)
    pl.semaphore_wait(ring_sem.at[0], 3)
    pass_on(me, ring_sem.at[1], 32)

    arrived(*early)

    lane = lax.broadcasted_iota(jnp.int32, (8, 128), 1)
    first = jnp.where(me == 0, 0.0, 1.0).astype(F32)
    last = jnp.where(me == N - 1, 0.0, 1.0).astype(F32)
    col = lax.broadcasted_iota(jnp.int32, (1, NY), 1)

    def crow(e):
        return cb[e // RD + 1, pl.ds(e % RD, 1), :]

    def edge(e):
        a, b = crow(e - 1), crow(e)
        if e == RD:
            a = first * a + (1.0 - first) * b
        if e == 2 * RD:
            b = last * b + (1.0 - last) * a
        if e == 0:
            a = jnp.where(me == 1, b, a)
        if e == EXT:
            b = jnp.where(me == N - 2, a, b)
        return 0.5 * (a + b)

    for e in range(EXT + 1):
        wu[e] = jnp.broadcast_to(edge(e), (8, NY))
    for e in range(EXT):
        c = crow(e)
        before = jnp.where(col == 0, c, pltpu.roll(c, 1, 1))
        after = jnp.where(col == NY - 1, c, pltpu.roll(c, NY - 1, 1))
        left = 0.5 * (c + before)
        right = 0.5 * (c + after)
        wl[e] = jnp.broadcast_to(jnp.where(col == 0, 0.0, left), (8, NY))
        ws[e] = jnp.broadcast_to(left + right, (8, NY)) + wu[e] + wu[e + 1]
        sx[e] = jnp.broadcast_to(sb[e // RD, pl.ds(e % RD, 1), :], (8, NY))

    def start_row(e, keep):
        for g in range(2):
            gs = pl.ds(8 * g, 8)
            d = keep / (ws[e] + jnp.exp(lf[e, gs, :]))
            dinv[e, gs, :] = d
            v0[e, gs, :] = sx[e] * d

    def own_start(e, carry):
        start_row(e, jnp.float32(1.0))
        return carry

    lax.fori_loop(RD, 2 * RD, own_start, 0)

    def moments_zero(side):
        zero = jnp.zeros((8, 128), F32)

        def row(e, carry):
            out = []
            for g in range(2):
                acc = carry[g]
                for j in range(TILES):
                    sl = pl.ds(128 * j, 128)
                    acc = acc + side(e, g, sl) * v0[e, pl.ds(8 * g, 8), sl]
                out.append(acc)
            return tuple(out)

        return list(lax.fori_loop(RD, 2 * RD, row, (zero, zero)))

    accs = [moments_zero(lambda e, g, sl: sx[e, :, sl])]
    moved = []
    for i, (above, below) in enumerate(rows):
        arrived(above, below)
        start_row(RD - 1 - i, first)
        start_row(2 * RD + i, last)
        for k in range(i):
            powers_pair(v, k, wu, wl, dinv, lane, i - k)
        one, two = powers_own(v, i, wu, wl, dinv, lane)
        accs.append(one)
        if i < ITERS - 1:
            accs.append(two)
            moved.append(remote(v[i + 1].at[RD], v[i + 1].at[0], 1))
            moved.append(remote(v[i + 1].at[2 * RD - 1], v[i + 1].at[EXT - 1], -1))
    mom_a[me] = pack(accs)
    pl.semaphore_wait(ring_sem.at[1], 3)
    send_row_to_all(me, mom_a, all_sem.at[0], all_sem.at[1])

    arrived(*late)
    for e in range(EXT):
        ox[e] = jnp.broadcast_to(ob[e // RD, pl.ds(e % RD, 1), :], (8, NY))
        px[e] = jnp.broadcast_to(pb[e // RD, pl.ds(e % RD, 1), :], (8, NY))
    arrived(moved[0], moved[1])
    powers_pair(v, 1, wu, wl, dinv, lane, 3)
    arrived(moved[2], moved[3])
    powers_pair(v, 2, wu, wl, dinv, lane, 2)
    powers_pair(v, 2, wu, wl, dinv, lane, 3)
    arrived(moved[4], moved[5])

    wait_rows(mom_a, all_sem.at[1])
    y, info = krylov_weights(unpack(jnp.sum(mom_a[...], axis=0)))
    info_ref[0] = jnp.broadcast_to(info, (CH, 128))

    for copy, goes in sent:

        @pl.when(goes)
        def _():
            copy.wait_send()

    def adjoint_start(e, carry):
        out = []
        for g in range(2):
            acc = carry[g]
            gs = pl.ds(8 * g, 8)
            yg = [jnp.broadcast_to(y[k][8 * g:8 * g + 8], (8, 128)) for k in range(ITERS)]
            for j in range(TILES):
                sl = pl.ds(128 * j, 128)
                x = yg[0] * v0[e, gs, sl]
                for k in range(1, ITERS):
                    x = x + yg[k] * v[k][e, gs, sl]
                side = px[e, :, sl] * (x - ox[e, :, sl])
                new = side * dinv[e, gs, sl]
                state[e, gs, sl] = x
                v0[e, gs, sl] = new
                acc = acc + side * new
            out.append(acc)
        return tuple(out)

    zero = jnp.zeros((8, 128), F32)
    lax.fori_loop(0, RD, adjoint_start, (zero, zero))
    lax.fori_loop(2 * RD, EXT, adjoint_start, (zero, zero))
    accs = [list(lax.fori_loop(RD, 2 * RD, adjoint_start, (zero, zero)))]
    for k in range(ITERS):
        one, two = powers_own(v, k, wu, wl, dinv, lane)
        accs.append(one)
        if k < ITERS - 1:
            accs.append(two)
            for i in range(1, RD - k):
                powers_pair(v, k, wu, wl, dinv, lane, i)
    mom_b[me] = pack(accs)
    send_row_to_all(me, mom_b, all_sem.at[2], all_sem.at[3])

    def spread2(to):
        pltpu.make_async_remote_copy(
            src_ref=ps2.at[to], dst_ref=got2.at[me], send_sem=all_sem.at[4], recv_sem=all_sem.at[5],
            device_id=(to,), device_id_type=MESH_ID,
        ).start()
    for_peers(me, spread2)
    got2[me] = ps2[me]


    variance = 1.0 / (1.0 + eigen[...])
    below = 2.0 + 0.8 * variance
    factors = jnp.concatenate(
        [
            (2.0 - 0.8 * variance) / below,
            1.6 * variance / below,
            jnp.sqrt(6.4 * variance) / below,
            jnp.zeros((5, variance.shape[1]), F32),
            subspace[...],
        ],
        axis=0,
    )
    rank = factors.shape[1]
    row_id = lax.broadcasted_iota(jnp.int32, (rank, RD * rank), 0)
    lane_id = lax.broadcasted_iota(jnp.int32, (rank, RD * rank), 1)
    widen = jnp.where(lane_id // RD == row_id, 1.0, 0.0).astype(jnp.bfloat16)
    wide_f[...] = join_three(
        jnp.dot(in_three(factors), widen, preferred_element_type=F32), 8 + CH
    )
    row_id = lax.broadcasted_iota(jnp.int32, (RD * rank, rank), 0)
    lane_id = lax.broadcasted_iota(jnp.int32, (RD * rank, rank), 1)
    pick[...] = jnp.where(row_id == RD * lane_id, 1.0, 0.0).astype(jnp.bfloat16)

    wait_rows(mom_b, all_sem.at[3])
    y, info = krylov_weights(unpack(jnp.sum(mom_b[...], axis=0)))
    info_ref[1] = jnp.broadcast_to(info, (CH, 128))

    for r in range(RD):
        for h in range(4):
            sl = pl.ds(512 * h, 512)
            adj = y[0] * v0[r + RD, :, sl]
            for k in range(1, ITERS):
                adj = adj + y[k] * v[k][r + RD, :, sl]
            value = -jnp.exp(lf[r + RD, :, sl]) * adj * state[r + RD, :, sl]
            fg[pl.ds(16 * r, 16), sl] = value.astype(jnp.bfloat16)
    project(fg, bm, ps)

    def spread(to):
        pltpu.make_async_remote_copy(
            src_ref=ps.at[to // CH, pl.ds(to % CH, 1)], dst_ref=got.at[me],
            send_sem=all_sem.at[8], recv_sem=all_sem.at[9],
            device_id=(to,), device_id_type=MESH_ID,
        ).start()
    for_peers(me, spread)
    got[me] = ps[me // CH, pl.ds(me % CH, 1), :]
    wait_rows(got2, all_sem.at[5])
    sum2[me] = over_rows(jnp.sum(got2[...], axis=0))
    send_row_to_all(me, sum2, all_sem.at[6], all_sem.at[7])

    wait_rows(got, all_sem.at[9])
    sums[me] = over_rows(jnp.sum(got[...], axis=0))
    send_row_to_all(me, sums, all_sem.at[10], all_sem.at[11])
    wait_rows(sum2, all_sem.at[7])
    wait_rows(sums, all_sem.at[11])

    lane = lax.broadcasted_iota(jnp.int32, (CH, 128), 1) % RD
    pieces = []
    for b in range(8):
        rows = pl.ds(16 * b, 16)
        cols = pl.ds(128 * b, 128)
        state_coef, noise_coef = sum2[rows, 0, :], sum2[rows, 1, :]
        new = wide_f[0:1, cols] * state_coef - wide_f[1:2, cols] * sums[rows, 0, :]
        new = new + wide_f[2:3, cols] * wide_f[8 : 8 + CH, cols]
        correction = new - 0.6 * state_coef - 0.8 * noise_coef
        for x in range(RD):
            em[pl.ds(16 * x, 16), cols] = jnp.where(lane == x, correction, 0.0).astype(jnp.bfloat16)
        pieces.append(new)
    for h in range(4):
        sl = pl.ds(512 * h, 512)
        rebuilt = jnp.dot(em[...], bm[:, sl], preferred_element_type=F32)
        for x in range(RD):
            pr[x, :, sl] = 0.6 * lf[RD + x, :, sl] + 0.8 * nf[x, :, sl] + rebuilt[16 * x : 16 * x + 16]
    results = [pltpu.make_async_copy(pr.at[x], proposal.at[:, x, :], out_sem.at[x]) for x in range(RD)]
    for copy in results:
        copy.start()
    coef_ref[...] = join_three(
        jnp.dot(in_three(jnp.concatenate(pieces, axis=1)), pick[...], preferred_element_type=F32), CH
    )
    for buf, sem in ((mom_a, 0), (mom_b, 2), (got2, 4), (sum2, 6), (got, 8), (sums, 10)):
        wait_rows(buf, all_sem.at[sem])
    for copy in results:
        copy.wait()


def per_device(
    source, observed, precision, conductivity, log_field, noise_field, subspace_noise, eigenvalues, basis,
):
    any_space = pl.BlockSpec(memory_space=pltpu.HBM)
    vmem = pl.BlockSpec(memory_space=pltpu.VMEM)
    rank = eigenvalues.shape[0]
    wide = pltpu.VMEM((EXT, CH, NY), F32)
    row8 = pltpu.VMEM((EXT, 8, NY), F32)
    small = pltpu.VMEM((3, RD, NY), F32)
    one = pltpu.VMEM((N, 1, 128), F32)
    two = pltpu.VMEM((N, 2, 128), F32)
    half = jnp.bfloat16
    proposal, new_coef, info = pl.pallas_call(
        step_kernel,
        out_shape=(
            jax.ShapeDtypeStruct(log_field.shape, F32),
            jax.ShapeDtypeStruct((CH, rank), F32),
            jax.ShapeDtypeStruct((2, CH, 128), F32),
        ),
        in_specs=[any_space] * 9,
        out_specs=(any_space, vmem, vmem),
        scratch_shapes=[
            wide, wide, wide, wide, wide, wide,
            pltpu.VMEM((EXT + 1, 8, NY), F32), row8, row8, row8, row8, row8, wide,
            pltpu.VMEM((5, RD, NY), F32), small, small, small, one, one,
            pltpu.VMEM((RD, CH, NY), F32),
            pltpu.VMEM((RD * rank, NY), half),
            pltpu.VMEM((2 * RD * CH, NY), half),
            pltpu.VMEM((RD * CH, NY), half),
            two, two, two,
            pltpu.VMEM((8, CH, 128), F32), one, one,
            pltpu.VMEM((8 + CH, RD * rank), F32),
            pltpu.VMEM((RD * rank, rank), half),
            pltpu.VMEM((RD * CH, RD * rank), half),
            pltpu.VMEM((RD, CH, NY), F32),
            pltpu.VMEM((CH, rank), F32), pltpu.VMEM((1, rank), F32),
            pltpu.SemaphoreType.DMA((7,)),
            pltpu.SemaphoreType.DMA((24,)),
            pltpu.SemaphoreType.DMA((24,)),
            pltpu.SemaphoreType.DMA((12,)),
            pltpu.SemaphoreType.DMA((8,)),
            pltpu.SemaphoreType.DMA((4,)),
            pltpu.SemaphoreType.REGULAR((2,)),
        ],
        compiler_params=pltpu.CompilerParams(
            collective_id=0, has_side_effects=True, vmem_limit_bytes=66_900_000
        ),
    )(
        source, observed, precision, conductivity, log_field, noise_field,
        subspace_noise, eigenvalues.reshape(1, rank), basis,
    )
    return (proposal, new_coef)


def solution(mesh):
    return jax.shard_map(
        per_device,
        mesh=mesh,
        in_specs=(
            P(AXIS, None), P(AXIS, None), P(AXIS, None), P(AXIS, None),
            P(None, AXIS, None), P(None, AXIS, None), P(), P(), P(None, AXIS, None),
        ),
        out_specs=(P(None, AXIS, None), P()),
        check_vma=False,
    )
```

```python
import functools

import jax
import jax.numpy as jnp
from jax import lax
from jax.experimental import pallas as pl
from jax.experimental.pallas import tpu as pltpu
from jax.sharding import PartitionSpec as P

ITERS = 4
AXIS = "rows"
N = 128
RD = 4
NY = 2048
CH = 16
EXT = 12
TILES = NY // 128
MESH_ID = pl.DeviceIdType.MESH
LIMIT = 1e7
F32 = jnp.float32


def far_first(turn):
    return lax.rem(2 + 3 * turn + 3 * (turn * (turn - 1) // 2), 4)


def for_peers(me, act):
    near = []
    for z in (2, 1, 3, 0):
        for c in (1, 0):
            near.append(lax.rem(me + c, 2) + 2 * lax.rem(me // 2 + z, 4))

    def plane(turn, carry):
        y = lax.rem(me // 8 + far_first(lax.rem(turn, 4)), 4)
        x = lax.rem(me // 32 + far_first(turn // 4), 4)
        for at in near:
            act(8 * y + 32 * x + at)
        return carry

    lax.fori_loop(0, 15, plane, 0)
    for at in near[:-1]:
        act(8 * (me // 8) + at)


def ring_peers(me, stride):
    at = lax.rem(me // stride, 4)
    return [me + stride * (lax.rem(at + d, 4) - at) for d in (2, 1, 3)]


def greet_near(me):
    column = 8 * (me // 8)
    near = [column + lax.rem(me + d, 8) for d in range(1, 8)]
    near += ring_peers(me, 8) + ring_peers(me, 32)
    near += [lax.rem(me + d + N, N) for d in (-2, 2, -1, 1)]
    barrier = pltpu.get_barrier_semaphore()
    for to in near:
        pl.semaphore_signal(barrier, inc=1, device_id=(to,), device_id_type=MESH_ID)
    return barrier, len(near)


def pass_on(me, sem, stride):
    for to in ring_peers(me, stride):
        pl.semaphore_signal(sem, inc=1, device_id=(to,), device_id_type=MESH_ID)


def send_row_to_all(me, buf, send_sem, recv_sem):
    def send(to):
        pltpu.make_async_remote_copy(
            src_ref=buf.at[me], dst_ref=buf.at[me], send_sem=send_sem, recv_sem=recv_sem,
            device_id=(to,), device_id_type=MESH_ID,
        ).start()

    for_peers(me, send)


def wait_rows(buf, sem):
    part = buf.at[pl.ds(0, N - 1)]
    pltpu.make_async_copy(part, part, sem).wait()


def pack(accs):
    lane = lax.broadcasted_iota(jnp.int32, (8, 128), 1)
    sub = lax.broadcasted_iota(jnp.int32, (8, 128), 0)
    row = jnp.zeros((8, 128), F32)
    for k in range(8):
        for g in range(2):
            total = jnp.sum(accs[k][g], axis=1, keepdims=True)
            row = row + jnp.where(lane == (g * 8 + k) * 8 + sub, total, 0.0)
    return jnp.sum(row, axis=0, keepdims=True)


def unpack(row):
    lane = lax.broadcasted_iota(jnp.int32, (8, 128), 1)
    sub = lax.broadcasted_iota(jnp.int32, (8, 128), 0)
    wide = jnp.broadcast_to(row, (8, 128))
    moments = []
    for k in range(8):
        halves = [
            jnp.sum(jnp.where(lane == (g * 8 + k) * 8 + sub, wide, 0.0), axis=1, keepdims=True)
            for g in range(2)
        ]
        moments.append(jnp.concatenate(halves, axis=0))
    return moments


def square(poly):
    out = [None] * (2 * len(poly) - 1)
    for i, a in enumerate(poly):
        for j, b in enumerate(poly):
            term = a * b
            out[i + j] = term if out[i + j] is None else out[i + j] + term
    return out


def krylov_weights(m):
    one = jnp.ones_like(m[0])
    rho, pi = [one], [one]
    y = [jnp.zeros_like(one)] * ITERS
    g = m[0]
    spread = g
    gain, noise = None, None
    for step in range(ITERS):
        s = square(pi)
        c = functools.reduce(lambda a, b: a + b, [s[l] * (m[l] - m[l + 1]) for l in range(len(s))])
        size = functools.reduce(
            lambda a, b: a + b, [jnp.abs(s[l]) * (jnp.abs(m[l]) + jnp.abs(m[l + 1])) for l in range(len(s))]
        )
        alpha = g / c
        part = alpha * g
        err = part * ((size / c) * (size / c) + (spread / g) * (spread / g))
        gain = part if gain is None else gain + part
        noise = err if noise is None else noise + err
        for k in range(len(pi)):
            y[k] = y[k] + alpha * pi[k]
        if step == ITERS - 1:
            break
        new = []
        for k in range(len(pi) + 1):
            value = rho[k] if k < len(rho) else None
            if k < len(pi):
                value = value - alpha * pi[k]
            if k > 0:
                moved = alpha * pi[k - 1]
                value = moved if value is None else value + moved
            new.append(value)
        rho = new
        s = square(rho)
        following = functools.reduce(lambda a, b: a + b, [s[l] * m[l] for l in range(len(s))])
        spread = functools.reduce(lambda a, b: a + b, [jnp.abs(s[l]) * jnp.abs(m[l]) for l in range(len(s))])
        beta = following / g
        g = following
        pi = [rho[k] + beta * pi[k] if k < len(pi) else rho[k] for k in range(len(rho))]
    return y, noise / gain


def apply_row(vk, vn, wu, wl, dinv, e, lane, accs):
    whole = pl.ds(0, 8)
    groups = (pl.ds(0, 8), pl.ds(8, 8))
    kept = {}

    def prepare(j):
        cols = pl.ds(128 * j, 128)
        w = wl[e, whole, cols]
        out = []
        for gs in groups:
            v = vk[e, gs, cols]
            out.append((v, pltpu.roll(v, 1, 1), pltpu.roll(w * v, 127, 1)))
        kept[j] = (w, out)

    prepare(0)
    for j in range(TILES):
        cols = pl.ds(128 * j, 128)
        if j + 1 < TILES:
            prepare(j + 1)
        w, here = kept[j]
        above, below = wu[e, whole, cols], wu[e + 1, whole, cols]
        for g, gs in enumerate(groups):
            v, moved, moved_back = here[g]
            left = moved if j == 0 else jnp.where(lane == 0, kept[j - 1][1][g][1], moved)
            right = jnp.where(lane == 127, kept[j + 1][1][g][2] if j + 1 < TILES else 0.0, moved_back)
            t = above * vk[e - 1, gs, cols] + below * vk[e + 1, gs, cols]
            t = t + (w * left + right)
            if accs is not None:
                accs[0][g] = accs[0][g] + t * v
            if vn is not None:
                new = t * dinv[e, gs, cols]
                vn[e, gs, cols] = new
                if accs is not None:
                    accs[1][g] = accs[1][g] + t * new


def powers_own(v, k, wu, wl, dinv, lane):
    zero = jnp.zeros((8, 128), F32)

    def rows(i, carry):
        accs = [list(carry[0]), list(carry[1])]
        for h in range(2):
            e = RD + 2 * i + h
            apply_row(v[k], v[k + 1] if k < ITERS - 1 else None, wu, wl, dinv, e, lane, accs)
        return tuple(accs[0]), tuple(accs[1])

    got = lax.fori_loop(0, RD // 2, rows, ((zero, zero), (zero, zero)))
    return list(got[0]), list(got[1])


def powers_pair(v, k, wu, wl, dinv, lane, i):
    for e in (RD - i, 2 * RD - 1 + i):
        apply_row(v[k], v[k + 1], wu, wl, dinv, e, lane, None)


def project(fields, basis_rows, out):
    count = fields.shape[0] // (RD * CH)
    lane = lax.broadcasted_iota(jnp.int32, (CH, 256), 1) % RD
    for q in range(4):
        full = lax.dot_general(
            fields[...], basis_rows[pl.ds(256 * q, 256), :], (((1,), (1,)), ((), ())),
            preferred_element_type=F32,
        )
        for f in range(count):
            rows = full[64 * f : 64 * f + 64]
            part = rows[48:64]
            for x in range(RD - 1):
                part = jnp.where(lane == x, rows[16 * x : 16 * x + 16], part)
            for h in range(2):
                piece = part[:, 128 * h : 128 * h + 128]
                if count == 1:
                    out[2 * q + h] = piece
                else:
                    out[pl.ds(16 * (2 * q + h), 16), f, :] = piece


def over_rows(value):
    lane = lax.broadcasted_iota(jnp.int32, value.shape, 1)
    pair = value + jnp.where(lane % 2 == 0, pltpu.roll(value, 127, 1), pltpu.roll(value, 1, 1))
    return pair + jnp.where(lane % 4 < 2, pltpu.roll(pair, 126, 1), pltpu.roll(pair, 2, 1))


def in_three(value):
    high = value.astype(jnp.bfloat16)
    rest = value - high.astype(F32)
    middle = rest.astype(jnp.bfloat16)
    low = (rest - middle.astype(F32)).astype(jnp.bfloat16)
    return jnp.concatenate([high, middle, low], axis=0)


def join_three(value, count):
    return value[:count] + value[count : 2 * count] + value[2 * count : 3 * count]


def empty_side(row, end, lf, cb, sb, ob, pb, v):
    block = row // RD
    lf[pl.ds(row, RD)] = jnp.zeros((RD, CH, NY), F32)
    for at in (0, 1):
        cb[(0 if row == 0 else 3) + at] = jnp.zeros((RD, NY), F32)
    for small in (sb, ob, pb):
        small[block] = jnp.zeros((RD, NY), F32)
    for power in v[1:]:
        power[end] = jnp.zeros((CH, NY), F32)


def step_kernel(
    source, observed, precision, conductivity, log_field, noise_field, subspace_hbm, eigen_hbm, basis,
    proposal, coef_ref, doubt_ref,
    lf, dinv, v0, v1, v2, v3, wu, wl, ws, sx, ox, px, state, cb, sb, ob, pb, mom_a, mom_b,
    nf, bm, f2, fg, ps2, got2, sum2, ps, got, sums, wide_f, pick, em, pr,
    subspace, eigen,
    local_sem, send_sem, recv_sem, all_sem, field_sem, out_sem, ring_sem,
):
    me = lax.axis_index(AXIS)
    v = (v0, v1, v2, v3)
    own = [
        pltpu.make_async_copy(conductivity, cb.at[2], local_sem.at[1]),
        pltpu.make_async_copy(source, sb.at[1], local_sem.at[2]),
        pltpu.make_async_copy(observed, ob.at[1], local_sem.at[3]),
        pltpu.make_async_copy(precision, pb.at[1], local_sem.at[4]),
        pltpu.make_async_copy(subspace_hbm, subspace, local_sem.at[5]),
        pltpu.make_async_copy(eigen_hbm, eigen, local_sem.at[6]),
    ]
    logs = [
        pltpu.make_async_copy(log_field.at[:, x, :], lf.at[RD + x], field_sem.at[x]) for x in range(RD)
    ]
    noises = [
        pltpu.make_async_copy(noise_field.at[:, x, :], nf.at[x], field_sem.at[RD + x]) for x in range(RD)
    ]
    barrier, greeted = greet_near(me)
    for copy in own + logs:
        copy.start()

    for copy in own + logs:
        copy.wait()
    pl.semaphore_wait(barrier, greeted)
    pass_on(me, ring_sem.at[0], 8)

    count = [0]
    sent = []

    def remote(src, dst, shift):
        index = count[0]
        count[0] += 1
        copy = pltpu.make_async_remote_copy(
            src_ref=src, dst_ref=dst, send_sem=send_sem.at[index], recv_sem=recv_sem.at[index],
            device_id=(lax.rem(me + shift + N, N),), device_id_type=MESH_ID,
        )
        goes = me + shift < N if shift > 0 else me + shift >= 0
        comes = me - shift >= 0 if shift > 0 else me - shift < N

        @pl.when(goes)
        def _():
            copy.start()

        sent.append((copy, goes))
        return copy, comes

    def arrived(*pairs):
        for copy, comes in pairs:

            @pl.when(comes)
            def _():
                copy.wait_recv()

    @pl.when(me == 0)
    def _():
        empty_side(0, 0, lf, cb, sb, ob, pb, v)

    @pl.when(me == N - 1)
    def _():
        empty_side(2 * RD, EXT - 1, lf, cb, sb, ob, pb, v)

    @pl.when(me == 1)
    def _():
        cb[0] = jnp.zeros((RD, NY), F32)

    @pl.when(me == N - 2)
    def _():
        cb[4] = jnp.zeros((RD, NY), F32)

    early = []
    for block, src, centre in ((cb, 2, 2), (sb, 1, 1)):
        early.append(remote(block.at[src], block.at[centre - 1], 1))
        early.append(remote(block.at[src], block.at[centre + 1], -1))
    early.append(remote(cb.at[2], cb.at[0], 2))
    early.append(remote(cb.at[2], cb.at[4], -2))
    rows = []
    for i in range(RD):
        rows.append(
            (
                remote(lf.at[2 * RD - 1 - i], lf.at[RD - 1 - i], 1),
                remote(lf.at[RD + i], lf.at[2 * RD + i], -1),
            )
        )
    late = []
    for block in (ob, pb):
        late.append(remote(block.at[1], block.at[0], 1))
        late.append(remote(block.at[1], block.at[2], -1))

    for copy in noises:
        copy.start()

    def fetch(r, carry):
        pltpu.make_async_copy(
            basis.at[r], bm.at[pl.ds(pl.multiple_of(RD * r, RD), RD)], local_sem.at[0]
        ).start()
        return carry

    lax.fori_loop(0, basis.shape[0], fetch, 0, unroll=8)
    for x in range(RD):
        f2[pl.ds(16 * x, 16), :] = lf[RD + x].astype(jnp.bfloat16)
    for copy in noises:
        copy.wait()
    for x in range(RD):
        f2[pl.ds(64 + 16 * x, 16), :] = nf[x].astype(jnp.bfloat16)
    pltpu.make_async_copy(bm, bm, local_sem.at[0]).wait()
    project(f2, bm, ps2)
    pl.semaphore_wait(ring_sem.at[0], 3)
    pass_on(me, ring_sem.at[1], 32)

    arrived(*early)

    lane = lax.broadcasted_iota(jnp.int32, (8, 128), 1)
    first = jnp.where(me == 0, 0.0, 1.0).astype(F32)
    last = jnp.where(me == N - 1, 0.0, 1.0).astype(F32)
    col = lax.broadcasted_iota(jnp.int32, (1, NY), 1)

    def crow(e):
        return cb[e // RD + 1, pl.ds(e % RD, 1), :]

    def edge(e):
        a, b = crow(e - 1), crow(e)
        if e == RD:
            a = first * a + (1.0 - first) * b
        if e == 2 * RD:
            b = last * b + (1.0 - last) * a
        if e == 0:
            a = jnp.where(me == 1, b, a)
        if e == EXT:
            b = jnp.where(me == N - 2, a, b)
        return 0.5 * (a + b)

    for e in range(EXT + 1):
        wu[e] = jnp.broadcast_to(edge(e), (8, NY))
    for e in range(EXT):
        c = crow(e)
        before = jnp.where(col == 0, c, pltpu.roll(c, 1, 1))
        after = jnp.where(col == NY - 1, c, pltpu.roll(c, NY - 1, 1))
        left = 0.5 * (c + before)
        right = 0.5 * (c + after)
        wl[e] = jnp.broadcast_to(jnp.where(col == 0, 0.0, left), (8, NY))
        ws[e] = jnp.broadcast_to(left + right, (8, NY)) + wu[e] + wu[e + 1]
        sx[e] = jnp.broadcast_to(sb[e // RD, pl.ds(e % RD, 1), :], (8, NY))

    def start_row(e, keep):
        for g in range(2):
            gs = pl.ds(8 * g, 8)
            d = keep / (ws[e] + jnp.exp(lf[e, gs, :]))
            dinv[e, gs, :] = d
            v0[e, gs, :] = sx[e] * d

    def own_start(e, carry):
        start_row(e, jnp.float32(1.0))
        return carry

    lax.fori_loop(RD, 2 * RD, own_start, 0)

    def moments_zero(side):
        zero = jnp.zeros((8, 128), F32)

        def row(e, carry):
            out = []
            for g in range(2):
                acc = carry[g]
                for j in range(TILES):
                    sl = pl.ds(128 * j, 128)
                    acc = acc + side(e, g, sl) * v0[e, pl.ds(8 * g, 8), sl]
                out.append(acc)
            return tuple(out)

        return list(lax.fori_loop(RD, 2 * RD, row, (zero, zero)))

    accs = [moments_zero(lambda e, g, sl: sx[e, :, sl])]
    moved = []
    for i, (above, below) in enumerate(rows):
        arrived(above, below)
        start_row(RD - 1 - i, first)
        start_row(2 * RD + i, last)
        for k in range(i):
            powers_pair(v, k, wu, wl, dinv, lane, i - k)
        one, two = powers_own(v, i, wu, wl, dinv, lane)
        accs.append(one)
        if i < ITERS - 1:
            accs.append(two)
            moved.append(remote(v[i + 1].at[RD], v[i + 1].at[0], 1))
            moved.append(remote(v[i + 1].at[2 * RD - 1], v[i + 1].at[EXT - 1], -1))
    mom_a[me] = pack(accs)
    pl.semaphore_wait(ring_sem.at[1], 3)
    send_row_to_all(me, mom_a, all_sem.at[0], all_sem.at[1])

    arrived(*late)
    for e in range(EXT):
        ox[e] = jnp.broadcast_to(ob[e // RD, pl.ds(e % RD, 1), :], (8, NY))
        px[e] = jnp.broadcast_to(pb[e // RD, pl.ds(e % RD, 1), :], (8, NY))
    arrived(moved[0], moved[1])
    powers_pair(v, 1, wu, wl, dinv, lane, 3)
    arrived(moved[2], moved[3])
    powers_pair(v, 2, wu, wl, dinv, lane, 2)
    powers_pair(v, 2, wu, wl, dinv, lane, 3)
    arrived(moved[4], moved[5])

    wait_rows(mom_a, all_sem.at[1])
    y, info = krylov_weights(unpack(jnp.sum(mom_a[...], axis=0)))
    doubt = jnp.where(info < LIMIT, 0.0, 1.0)

    for copy, goes in sent:

        @pl.when(goes)
        def _():
            copy.wait_send()

    def adjoint_start(e, carry):
        out = []
        for g in range(2):
            acc = carry[g]
            gs = pl.ds(8 * g, 8)
            yg = [jnp.broadcast_to(y[k][8 * g:8 * g + 8], (8, 128)) for k in range(ITERS)]
            for j in range(TILES):
                sl = pl.ds(128 * j, 128)
                x = yg[0] * v0[e, gs, sl]
                for k in range(1, ITERS):
                    x = x + yg[k] * v[k][e, gs, sl]
                side = px[e, :, sl] * (x - ox[e, :, sl])
                new = side * dinv[e, gs, sl]
                state[e, gs, sl] = x
                v0[e, gs, sl] = new
                acc = acc + side * new
            out.append(acc)
        return tuple(out)

    zero = jnp.zeros((8, 128), F32)
    lax.fori_loop(0, RD, adjoint_start, (zero, zero))
    lax.fori_loop(2 * RD, EXT, adjoint_start, (zero, zero))
    accs = [list(lax.fori_loop(RD, 2 * RD, adjoint_start, (zero, zero)))]
    for k in range(ITERS):
        one, two = powers_own(v, k, wu, wl, dinv, lane)
        accs.append(one)
        if k < ITERS - 1:
            accs.append(two)
            for i in range(1, RD - k):
                powers_pair(v, k, wu, wl, dinv, lane, i)
    mom_b[me] = pack(accs)
    send_row_to_all(me, mom_b, all_sem.at[2], all_sem.at[3])

    def spread2(to):
        pltpu.make_async_remote_copy(
            src_ref=ps2.at[to], dst_ref=got2.at[me], send_sem=all_sem.at[4], recv_sem=all_sem.at[5],
            device_id=(to,), device_id_type=MESH_ID,
        ).start()
    for_peers(me, spread2)
    got2[me] = ps2[me]


    variance = 1.0 / (1.0 + eigen[...])
    below = 2.0 + 0.8 * variance
    factors = jnp.concatenate(
        [
            (2.0 - 0.8 * variance) / below,
            1.6 * variance / below,
            jnp.sqrt(6.4 * variance) / below,
            jnp.zeros((5, variance.shape[1]), F32),
            subspace[...],
        ],
        axis=0,
    )
    rank = factors.shape[1]
    row_id = lax.broadcasted_iota(jnp.int32, (rank, RD * rank), 0)
    lane_id = lax.broadcasted_iota(jnp.int32, (rank, RD * rank), 1)
    widen = jnp.where(lane_id // RD == row_id, 1.0, 0.0).astype(jnp.bfloat16)
    wide_f[...] = join_three(
        jnp.dot(in_three(factors), widen, preferred_element_type=F32), 8 + CH
    )
    row_id = lax.broadcasted_iota(jnp.int32, (RD * rank, rank), 0)
    lane_id = lax.broadcasted_iota(jnp.int32, (RD * rank, rank), 1)
    pick[...] = jnp.where(row_id == RD * lane_id, 1.0, 0.0).astype(jnp.bfloat16)

    wait_rows(mom_b, all_sem.at[3])
    y, info = krylov_weights(unpack(jnp.sum(mom_b[...], axis=0)))
    doubt = doubt + jnp.where(info < LIMIT, 0.0, 1.0)
    doubt_ref[0, 0] = jnp.sum(doubt)

    for r in range(RD):
        for h in range(4):
            sl = pl.ds(512 * h, 512)
            adj = y[0] * v0[r + RD, :, sl]
            for k in range(1, ITERS):
                adj = adj + y[k] * v[k][r + RD, :, sl]
            value = -jnp.exp(lf[r + RD, :, sl]) * adj * state[r + RD, :, sl]
            fg[pl.ds(16 * r, 16), sl] = value.astype(jnp.bfloat16)
    project(fg, bm, ps)

    def spread(to):
        pltpu.make_async_remote_copy(
            src_ref=ps.at[to // CH, pl.ds(to % CH, 1)], dst_ref=got.at[me],
            send_sem=all_sem.at[8], recv_sem=all_sem.at[9],
            device_id=(to,), device_id_type=MESH_ID,
        ).start()
    for_peers(me, spread)
    got[me] = ps[me // CH, pl.ds(me % CH, 1), :]
    wait_rows(got2, all_sem.at[5])
    sum2[me] = over_rows(jnp.sum(got2[...], axis=0))
    send_row_to_all(me, sum2, all_sem.at[6], all_sem.at[7])

    wait_rows(got, all_sem.at[9])
    sums[me] = over_rows(jnp.sum(got[...], axis=0))
    send_row_to_all(me, sums, all_sem.at[10], all_sem.at[11])
    wait_rows(sum2, all_sem.at[7])
    wait_rows(sums, all_sem.at[11])

    lane = lax.broadcasted_iota(jnp.int32, (CH, 128), 1) % RD
    pieces = []
    for b in range(8):
        rows = pl.ds(16 * b, 16)
        cols = pl.ds(128 * b, 128)
        state_coef, noise_coef = sum2[rows, 0, :], sum2[rows, 1, :]
        new = wide_f[0:1, cols] * state_coef - wide_f[1:2, cols] * sums[rows, 0, :]
        new = new + wide_f[2:3, cols] * wide_f[8 : 8 + CH, cols]
        correction = new - 0.6 * state_coef - 0.8 * noise_coef
        for x in range(RD):
            em[pl.ds(16 * x, 16), cols] = jnp.where(lane == x, correction, 0.0).astype(jnp.bfloat16)
        pieces.append(new)
    for h in range(4):
        sl = pl.ds(512 * h, 512)
        rebuilt = jnp.dot(em[...], bm[:, sl], preferred_element_type=F32)
        for x in range(RD):
            pr[x, :, sl] = 0.6 * lf[RD + x, :, sl] + 0.8 * nf[x, :, sl] + rebuilt[16 * x : 16 * x + 16]
    results = [pltpu.make_async_copy(pr.at[x], proposal.at[:, x, :], out_sem.at[x]) for x in range(RD)]
    for copy in results:
        copy.start()
    coef_ref[...] = join_three(
        jnp.dot(in_three(jnp.concatenate(pieces, axis=1)), pick[...], preferred_element_type=F32), CH
    )
    for buf, sem in ((mom_a, 0), (mom_b, 2), (got2, 4), (sum2, 6), (got, 8), (sums, 10)):
        wait_rows(buf, all_sem.at[sem])
    for copy in results:
        copy.wait()


def with_edges(value, dim):
    down = [(i, i + 1) for i in range(N - 1)]
    up = [(j, i) for i, j in down]
    length = value.shape[dim]
    before = lax.ppermute(lax.slice_in_dim(value, length - 1, length, axis=dim), AXIS, down)
    after = lax.ppermute(lax.slice_in_dim(value, 0, 1, axis=dim), AXIS, up)
    return jnp.concatenate([before, value, after], axis=dim)


def apply_operator(field, weights, diagonal):
    padded = jnp.pad(with_edges(field, 1), ((0, 0), (0, 0), (1, 1)))
    beside = weights[0] * padded[:, :-2, 1:-1] + weights[1] * padded[:, 2:, 1:-1]
    beside = beside + weights[2] * padded[:, 1:-1, :-2] + weights[3] * padded[:, 1:-1, 2:]
    return diagonal * field - beside


def chain_dot(left, right):
    return lax.psum(jnp.sum(left * right, axis=(1, 2)), AXIS)[:, None, None]


def solve_step_by_step(right_side, weights, diagonal):
    scaled = right_side / diagonal

    def step(_, carry):
        solution, residual, direction, current = carry
        applied = apply_operator(direction, weights, diagonal)
        length = current / chain_dot(direction, applied)
        solution = solution + length * direction
        residual = residual - length * applied
        scaled = residual / diagonal
        following = chain_dot(residual, scaled)
        return solution, residual, scaled + (following / current) * direction, following

    start = (jnp.zeros_like(scaled), right_side, scaled, chain_dot(right_side, scaled))
    return lax.fori_loop(0, ITERS, step, start)[0]


def step_by_step(
    source, observed, precision, conductivity, log_field, noise_field, subspace_noise, eigenvalues, basis,
):
    position = lax.axis_index(AXIS)
    edges = with_edges(conductivity, 0)
    upper = jnp.where(position == 0, conductivity[:1], edges[:1])
    lower = jnp.where(position == N - 1, conductivity[-1:], edges[-1:])
    padded = jnp.pad(jnp.concatenate([upper, conductivity, lower], 0), ((0, 0), (1, 1)), mode="edge")
    weights = (
        0.5 * (conductivity + padded[:-2, 1:-1]),
        0.5 * (conductivity + padded[2:, 1:-1]),
        0.5 * (conductivity + padded[1:-1, :-2]),
        0.5 * (conductivity + padded[1:-1, 2:]),
    )
    reaction = jnp.exp(log_field)
    diagonal = weights[0] + weights[1] + weights[2] + weights[3] + reaction

    def solve(_, carry):
        side, _, latest = carry
        found = solve_step_by_step(side, weights, diagonal)
        return precision * (found - observed), latest, found

    side = jnp.broadcast_to(source, log_field.shape)
    zeros = jnp.zeros_like(log_field)
    _, state, adjoint = lax.fori_loop(0, 2, solve, (side, zeros, zeros))
    gradient = -reaction * adjoint * state
    fields = jnp.concatenate([log_field, noise_field, gradient], 0).astype(jnp.bfloat16)
    coefs = lax.psum(jnp.einsum("cxy,rxy->cr", fields, basis, preferred_element_type=F32), AXIS)
    state_coef, noise_coef, grad_coef = coefs[:CH], coefs[CH : 2 * CH], coefs[2 * CH :]
    variance = 1.0 / (1.0 + eigenvalues)
    below = 2.0 + 0.8 * variance
    new_coef = (2.0 - 0.8 * variance) / below * state_coef - 1.6 * variance / below * grad_coef
    new_coef = new_coef + jnp.sqrt(6.4 * variance) / below * subspace_noise
    correction = (new_coef - 0.6 * state_coef - 0.8 * noise_coef).astype(jnp.bfloat16)
    rebuilt = jnp.einsum("cr,rxy->cxy", correction, basis, preferred_element_type=F32)
    return 0.6 * log_field + 0.8 * noise_field + rebuilt, new_coef


def per_device(
    source, observed, precision, conductivity, log_field, noise_field, subspace_noise, eigenvalues, basis,
):
    any_space = pl.BlockSpec(memory_space=pltpu.HBM)
    vmem = pl.BlockSpec(memory_space=pltpu.VMEM)
    rank = eigenvalues.shape[0]
    wide = pltpu.VMEM((EXT, CH, NY), F32)
    row8 = pltpu.VMEM((EXT, 8, NY), F32)
    small = pltpu.VMEM((3, RD, NY), F32)
    one = pltpu.VMEM((N, 1, 128), F32)
    two = pltpu.VMEM((N, 2, 128), F32)
    half = jnp.bfloat16
    proposal, new_coef, doubt = pl.pallas_call(
        step_kernel,
        out_shape=(
            jax.ShapeDtypeStruct(log_field.shape, F32),
            jax.ShapeDtypeStruct((CH, rank), F32),
            jax.ShapeDtypeStruct((1, 1), F32),
        ),
        in_specs=[any_space] * 9,
        out_specs=(any_space, vmem, pl.BlockSpec(memory_space=pltpu.SMEM)),
        scratch_shapes=[
            wide, wide, wide, wide, wide, wide,
            pltpu.VMEM((EXT + 1, 8, NY), F32), row8, row8, row8, row8, row8, wide,
            pltpu.VMEM((5, RD, NY), F32), small, small, small, one, one,
            pltpu.VMEM((RD, CH, NY), F32),
            pltpu.VMEM((RD * rank, NY), half),
            pltpu.VMEM((2 * RD * CH, NY), half),
            pltpu.VMEM((RD * CH, NY), half),
            two, two, two,
            pltpu.VMEM((8, CH, 128), F32), one, one,
            pltpu.VMEM((8 + CH, RD * rank), F32),
            pltpu.VMEM((RD * rank, rank), half),
            pltpu.VMEM((RD * CH, RD * rank), half),
            pltpu.VMEM((RD, CH, NY), F32),
            pltpu.VMEM((CH, rank), F32), pltpu.VMEM((1, rank), F32),
            pltpu.SemaphoreType.DMA((7,)),
            pltpu.SemaphoreType.DMA((24,)),
            pltpu.SemaphoreType.DMA((24,)),
            pltpu.SemaphoreType.DMA((12,)),
            pltpu.SemaphoreType.DMA((8,)),
            pltpu.SemaphoreType.DMA((4,)),
            pltpu.SemaphoreType.REGULAR((2,)),
        ],
        compiler_params=pltpu.CompilerParams(
            collective_id=0, has_side_effects=True, vmem_limit_bytes=66_900_000
        ),
    )(
        source, observed, precision, conductivity, log_field, noise_field,
        subspace_noise, eigenvalues.reshape(1, rank), basis,
    )
    return lax.cond(
        doubt[0, 0] > 0.0,
        lambda: step_by_step(
            source, observed, precision, conductivity, log_field, noise_field, subspace_noise,
            eigenvalues, basis,
        ),
        lambda: (proposal, new_coef),
    )


def solution(mesh):
    return jax.shard_map(
        per_device,
        mesh=mesh,
        in_specs=(
            P(AXIS, None), P(AXIS, None), P(AXIS, None), P(AXIS, None),
            P(None, AXIS, None), P(None, AXIS, None), P(), P(), P(None, AXIS, None),
        ),
        out_specs=(P(None, AXIS, None), P()),
        check_vma=False,
    )
```

```python
import functools

import jax
import jax.numpy as jnp
from jax import lax
from jax.experimental import pallas as pl
from jax.experimental.pallas import tpu as pltpu
from jax.sharding import PartitionSpec as P

ITERS = 4
AXIS = "rows"
N = 128
RD = 4
NY = 2048
CH = 16
EXT = 12
TILES = NY // 128
MESH_ID = pl.DeviceIdType.MESH
LIMIT = 2e6
F32 = jnp.float32


def far_first(turn):
    return lax.rem(2 + 3 * turn + 3 * (turn * (turn - 1) // 2), 4)


def for_peers(me, act):
    near = []
    for z in (2, 1, 3, 0):
        for c in (1, 0):
            near.append(lax.rem(me + c, 2) + 2 * lax.rem(me // 2 + z, 4))

    def plane(turn, carry):
        y = lax.rem(me // 8 + far_first(lax.rem(turn, 4)), 4)
        x = lax.rem(me // 32 + far_first(turn // 4), 4)
        for at in near:
            act(8 * y + 32 * x + at)
        return carry

    lax.fori_loop(0, 15, plane, 0)
    for at in near[:-1]:
        act(8 * (me // 8) + at)


def ring_peers(me, stride):
    at = lax.rem(me // stride, 4)
    return [me + stride * (lax.rem(at + d, 4) - at) for d in (2, 1, 3)]


def greet_near(me):
    column = 8 * (me // 8)
    near = [column + lax.rem(me + d, 8) for d in range(1, 8)]
    near += ring_peers(me, 8) + ring_peers(me, 32)
    near += [lax.rem(me + d + N, N) for d in (-2, 2, -1, 1)]
    barrier = pltpu.get_barrier_semaphore()
    for to in near:
        pl.semaphore_signal(barrier, inc=1, device_id=(to,), device_id_type=MESH_ID)
    return barrier, len(near)


def pass_on(me, sem, stride):
    for to in ring_peers(me, stride):
        pl.semaphore_signal(sem, inc=1, device_id=(to,), device_id_type=MESH_ID)


def send_row_to_all(me, buf, send_sem, recv_sem):
    def send(to):
        pltpu.make_async_remote_copy(
            src_ref=buf.at[me], dst_ref=buf.at[me], send_sem=send_sem, recv_sem=recv_sem,
            device_id=(to,), device_id_type=MESH_ID,
        ).start()

    for_peers(me, send)


def wait_rows(buf, sem):
    part = buf.at[pl.ds(0, N - 1)]
    pltpu.make_async_copy(part, part, sem).wait()


def pack(accs):
    lane = lax.broadcasted_iota(jnp.int32, (8, 128), 1)
    sub = lax.broadcasted_iota(jnp.int32, (8, 128), 0)
    row = jnp.zeros((8, 128), F32)
    for k in range(8):
        for g in range(2):
            total = jnp.sum(accs[k][g], axis=1, keepdims=True)
            row = row + jnp.where(lane == (g * 8 + k) * 8 + sub, total, 0.0)
    return jnp.sum(row, axis=0, keepdims=True)


def unpack(row):
    lane = lax.broadcasted_iota(jnp.int32, (8, 128), 1)
    sub = lax.broadcasted_iota(jnp.int32, (8, 128), 0)
    wide = jnp.broadcast_to(row, (8, 128))
    moments = []
    for k in range(8):
        halves = [
            jnp.sum(jnp.where(lane == (g * 8 + k) * 8 + sub, wide, 0.0), axis=1, keepdims=True)
            for g in range(2)
        ]
        moments.append(jnp.concatenate(halves, axis=0))
    return moments


def square(poly):
    out = [None] * (2 * len(poly) - 1)
    for i, a in enumerate(poly):
        for j, b in enumerate(poly):
            term = a * b
            out[i + j] = term if out[i + j] is None else out[i + j] + term
    return out


def krylov_weights(m):
    one = jnp.ones_like(m[0])
    rho, pi = [one], [one]
    y = [jnp.zeros_like(one)] * ITERS
    g = m[0]
    spread, least = g, g
    gain, noise = None, None
    for step in range(ITERS):
        s = square(pi)
        c = functools.reduce(lambda a, b: a + b, [s[l] * (m[l] - m[l + 1]) for l in range(len(s))])
        size = functools.reduce(
            lambda a, b: a + b, [jnp.abs(s[l]) * (jnp.abs(m[l]) + jnp.abs(m[l + 1])) for l in range(len(s))]
        )
        least = jnp.minimum(least, jnp.minimum(g, c))
        alpha = g / c
        part = alpha * g
        err = part * ((size / c) * (size / c) + (spread / g) * (spread / g))
        gain = part if gain is None else gain + part
        noise = err if noise is None else noise + err
        for k in range(len(pi)):
            y[k] = y[k] + alpha * pi[k]
        if step == ITERS - 1:
            break
        new = []
        for k in range(len(pi) + 1):
            value = rho[k] if k < len(rho) else None
            if k < len(pi):
                value = value - alpha * pi[k]
            if k > 0:
                moved = alpha * pi[k - 1]
                value = moved if value is None else value + moved
            new.append(value)
        rho = new
        s = square(rho)
        following = functools.reduce(lambda a, b: a + b, [s[l] * m[l] for l in range(len(s))])
        spread = functools.reduce(lambda a, b: a + b, [jnp.abs(s[l]) * jnp.abs(m[l]) for l in range(len(s))])
        beta = following / g
        g = following
        pi = [rho[k] + beta * pi[k] if k < len(pi) else rho[k] for k in range(len(rho))]
    return y, jnp.where(least > 0.0, noise / gain, 1e30)


def apply_row(vk, vn, wu, wl, dinv, e, lane, accs):
    whole = pl.ds(0, 8)
    groups = (pl.ds(0, 8), pl.ds(8, 8))
    kept = {}

    def prepare(j):
        cols = pl.ds(128 * j, 128)
        w = wl[e, whole, cols]
        out = []
        for gs in groups:
            v = vk[e, gs, cols]
            out.append((v, pltpu.roll(v, 1, 1), pltpu.roll(w * v, 127, 1)))
        kept[j] = (w, out)

    prepare(0)
    for j in range(TILES):
        cols = pl.ds(128 * j, 128)
        if j + 1 < TILES:
            prepare(j + 1)
        w, here = kept[j]
        above, below = wu[e, whole, cols], wu[e + 1, whole, cols]
        for g, gs in enumerate(groups):
            v, moved, moved_back = here[g]
            left = moved if j == 0 else jnp.where(lane == 0, kept[j - 1][1][g][1], moved)
            right = jnp.where(lane == 127, kept[j + 1][1][g][2] if j + 1 < TILES else 0.0, moved_back)
            t = above * vk[e - 1, gs, cols] + below * vk[e + 1, gs, cols]
            t = t + (w * left + right)
            if accs is not None:
                accs[0][g] = accs[0][g] + t * v
            if vn is not None:
                new = t * dinv[e, gs, cols]
                vn[e, gs, cols] = new
                if accs is not None:
                    accs[1][g] = accs[1][g] + t * new


def powers_own(v, k, wu, wl, dinv, lane):
    zero = jnp.zeros((8, 128), F32)

    def rows(i, carry):
        accs = [list(carry[0]), list(carry[1])]
        for h in range(2):
            e = RD + 2 * i + h
            apply_row(v[k], v[k + 1] if k < ITERS - 1 else None, wu, wl, dinv, e, lane, accs)
        return tuple(accs[0]), tuple(accs[1])

    got = lax.fori_loop(0, RD // 2, rows, ((zero, zero), (zero, zero)))
    return list(got[0]), list(got[1])


def powers_pair(v, k, wu, wl, dinv, lane, i):
    for e in (RD - i, 2 * RD - 1 + i):
        apply_row(v[k], v[k + 1], wu, wl, dinv, e, lane, None)


def project(fields, basis_rows, out):
    count = fields.shape[0] // (RD * CH)
    lane = lax.broadcasted_iota(jnp.int32, (CH, 256), 1) % RD
    for q in range(4):
        full = lax.dot_general(
            fields[...], basis_rows[pl.ds(256 * q, 256), :], (((1,), (1,)), ((), ())),
            preferred_element_type=F32,
        )
        for f in range(count):
            rows = full[64 * f : 64 * f + 64]
            part = rows[48:64]
            for x in range(RD - 1):
                part = jnp.where(lane == x, rows[16 * x : 16 * x + 16], part)
            for h in range(2):
                piece = part[:, 128 * h : 128 * h + 128]
                if count == 1:
                    out[2 * q + h] = piece
                else:
                    out[pl.ds(16 * (2 * q + h), 16), f, :] = piece


def over_rows(value):
    lane = lax.broadcasted_iota(jnp.int32, value.shape, 1)
    pair = value + jnp.where(lane % 2 == 0, pltpu.roll(value, 127, 1), pltpu.roll(value, 1, 1))
    return pair + jnp.where(lane % 4 < 2, pltpu.roll(pair, 126, 1), pltpu.roll(pair, 2, 1))


def in_three(value):
    high = value.astype(jnp.bfloat16)
    rest = value - high.astype(F32)
    middle = rest.astype(jnp.bfloat16)
    low = (rest - middle.astype(F32)).astype(jnp.bfloat16)
    return jnp.concatenate([high, middle, low], axis=0)


def join_three(value, count):
    return value[:count] + value[count : 2 * count] + value[2 * count : 3 * count]


def empty_side(row, end, lf, cb, sb, ob, pb, v):
    block = row // RD
    lf[pl.ds(row, RD)] = jnp.zeros((RD, CH, NY), F32)
    for at in (0, 1):
        cb[(0 if row == 0 else 3) + at] = jnp.zeros((RD, NY), F32)
    for small in (sb, ob, pb):
        small[block] = jnp.zeros((RD, NY), F32)
    for power in v[1:]:
        power[end] = jnp.zeros((CH, NY), F32)


def step_kernel(
    source, observed, precision, conductivity, log_field, noise_field, subspace_hbm, eigen_hbm, basis,
    proposal, coef_ref, doubt_ref,
    lf, dinv, v0, v1, v2, v3, wu, wl, ws, sx, ox, px, state, cb, sb, ob, pb, mom_a, mom_b,
    nf, bm, f2, fg, ps2, got2, sum2, ps, got, sums, wide_f, pick, em, pr,
    subspace, eigen,
    local_sem, send_sem, recv_sem, all_sem, field_sem, out_sem, ring_sem,
):
    me = lax.axis_index(AXIS)
    v = (v0, v1, v2, v3)
    own = [
        pltpu.make_async_copy(conductivity, cb.at[2], local_sem.at[1]),
        pltpu.make_async_copy(source, sb.at[1], local_sem.at[2]),
        pltpu.make_async_copy(observed, ob.at[1], local_sem.at[3]),
        pltpu.make_async_copy(precision, pb.at[1], local_sem.at[4]),
        pltpu.make_async_copy(subspace_hbm, subspace, local_sem.at[5]),
        pltpu.make_async_copy(eigen_hbm, eigen, local_sem.at[6]),
    ]
    logs = [
        pltpu.make_async_copy(log_field.at[:, x, :], lf.at[RD + x], field_sem.at[x]) for x in range(RD)
    ]
    noises = [
        pltpu.make_async_copy(noise_field.at[:, x, :], nf.at[x], field_sem.at[RD + x]) for x in range(RD)
    ]
    barrier, greeted = greet_near(me)
    for copy in own + logs:
        copy.start()

    for copy in own + logs:
        copy.wait()
    pl.semaphore_wait(barrier, greeted)
    pass_on(me, ring_sem.at[0], 8)

    count = [0]
    sent = []

    def remote(src, dst, shift):
        index = count[0]
        count[0] += 1
        copy = pltpu.make_async_remote_copy(
            src_ref=src, dst_ref=dst, send_sem=send_sem.at[index], recv_sem=recv_sem.at[index],
            device_id=(lax.rem(me + shift + N, N),), device_id_type=MESH_ID,
        )
        goes = me + shift < N if shift > 0 else me + shift >= 0
        comes = me - shift >= 0 if shift > 0 else me - shift < N

        @pl.when(goes)
        def _():
            copy.start()

        sent.append((copy, goes))
        return copy, comes

    def arrived(*pairs):
        for copy, comes in pairs:

            @pl.when(comes)
            def _():
                copy.wait_recv()

    @pl.when(me == 0)
    def _():
        empty_side(0, 0, lf, cb, sb, ob, pb, v)

    @pl.when(me == N - 1)
    def _():
        empty_side(2 * RD, EXT - 1, lf, cb, sb, ob, pb, v)

    @pl.when(me == 1)
    def _():
        cb[0] = jnp.zeros((RD, NY), F32)

    @pl.when(me == N - 2)
    def _():
        cb[4] = jnp.zeros((RD, NY), F32)

    early = []
    for block, src, centre in ((cb, 2, 2), (sb, 1, 1)):
        early.append(remote(block.at[src], block.at[centre - 1], 1))
        early.append(remote(block.at[src], block.at[centre + 1], -1))
    early.append(remote(cb.at[2, pl.ds(RD - 1, 1)], cb.at[0, pl.ds(RD - 1, 1)], 2))
    early.append(remote(cb.at[2, pl.ds(0, 1)], cb.at[4, pl.ds(0, 1)], -2))
    rows = []
    for i in range(RD):
        rows.append(
            (
                remote(lf.at[2 * RD - 1 - i], lf.at[RD - 1 - i], 1),
                remote(lf.at[RD + i], lf.at[2 * RD + i], -1),
            )
        )
    late = []
    for block in (ob, pb):
        late.append(remote(block.at[1], block.at[0], 1))
        late.append(remote(block.at[1], block.at[2], -1))

    for copy in noises:
        copy.start()

    def fetch(r, carry):
        pltpu.make_async_copy(
            basis.at[r], bm.at[pl.ds(pl.multiple_of(RD * r, RD), RD)], local_sem.at[0]
        ).start()
        return carry

    lax.fori_loop(0, basis.shape[0], fetch, 0, unroll=8)
    for x in range(RD):
        f2[pl.ds(16 * x, 16), :] = lf[RD + x].astype(jnp.bfloat16)
    for copy in noises:
        copy.wait()
    for x in range(RD):
        f2[pl.ds(64 + 16 * x, 16), :] = nf[x].astype(jnp.bfloat16)
    pltpu.make_async_copy(bm, bm, local_sem.at[0]).wait()
    project(f2, bm, ps2)
    pl.semaphore_wait(ring_sem.at[0], 3)
    pass_on(me, ring_sem.at[1], 32)

    arrived(*early)

    lane = lax.broadcasted_iota(jnp.int32, (8, 128), 1)
    first = jnp.where(me == 0, 0.0, 1.0).astype(F32)
    last = jnp.where(me == N - 1, 0.0, 1.0).astype(F32)
    col = lax.broadcasted_iota(jnp.int32, (1, NY), 1)

    def crow(e):
        return cb[e // RD + 1, pl.ds(e % RD, 1), :]

    def edge(e):
        a, b = crow(e - 1), crow(e)
        if e == RD:
            a = first * a + (1.0 - first) * b
        if e == 2 * RD:
            b = last * b + (1.0 - last) * a
        if e == 0:
            a = jnp.where(me == 1, b, a)
        if e == EXT:
            b = jnp.where(me == N - 2, a, b)
        return 0.5 * (a + b)

    for e in range(EXT + 1):
        wu[e] = jnp.broadcast_to(edge(e), (8, NY))
    for e in range(EXT):
        c = crow(e)
        before = jnp.where(col == 0, c, pltpu.roll(c, 1, 1))
        after = jnp.where(col == NY - 1, c, pltpu.roll(c, NY - 1, 1))
        left = 0.5 * (c + before)
        right = 0.5 * (c + after)
        wl[e] = jnp.broadcast_to(jnp.where(col == 0, 0.0, left), (8, NY))
        ws[e] = jnp.broadcast_to(left + right, (8, NY)) + wu[e] + wu[e + 1]
        sx[e] = jnp.broadcast_to(sb[e // RD, pl.ds(e % RD, 1), :], (8, NY))

    def start_row(e, keep):
        for g in range(2):
            gs = pl.ds(8 * g, 8)
            d = keep / (ws[e] + jnp.exp(lf[e, gs, :]))
            dinv[e, gs, :] = d
            v0[e, gs, :] = sx[e] * d

    def own_start(e, carry):
        start_row(e, jnp.float32(1.0))
        return carry

    lax.fori_loop(RD, 2 * RD, own_start, 0)

    def moments_zero(side):
        zero = jnp.zeros((8, 128), F32)

        def row(e, carry):
            out = []
            for g in range(2):
                acc = carry[g]
                for j in range(TILES):
                    sl = pl.ds(128 * j, 128)
                    acc = acc + side(e, g, sl) * v0[e, pl.ds(8 * g, 8), sl]
                out.append(acc)
            return tuple(out)

        return list(lax.fori_loop(RD, 2 * RD, row, (zero, zero)))

    accs = [moments_zero(lambda e, g, sl: sx[e, :, sl])]
    moved = []
    for i, (above, below) in enumerate(rows):
        arrived(above, below)
        start_row(RD - 1 - i, first)
        start_row(2 * RD + i, last)
        for k in range(i):
            powers_pair(v, k, wu, wl, dinv, lane, i - k)
        one, two = powers_own(v, i, wu, wl, dinv, lane)
        accs.append(one)
        if i < ITERS - 1:
            accs.append(two)
            moved.append(remote(v[i + 1].at[RD], v[i + 1].at[0], 1))
            moved.append(remote(v[i + 1].at[2 * RD - 1], v[i + 1].at[EXT - 1], -1))
    mom_a[me] = pack(accs)
    pl.semaphore_wait(ring_sem.at[1], 3)
    send_row_to_all(me, mom_a, all_sem.at[0], all_sem.at[1])

    arrived(*late)
    for e in range(EXT):
        ox[e] = jnp.broadcast_to(ob[e // RD, pl.ds(e % RD, 1), :], (8, NY))
        px[e] = jnp.broadcast_to(pb[e // RD, pl.ds(e % RD, 1), :], (8, NY))
    arrived(moved[0], moved[1])
    powers_pair(v, 1, wu, wl, dinv, lane, 3)
    arrived(moved[2], moved[3])
    powers_pair(v, 2, wu, wl, dinv, lane, 2)
    powers_pair(v, 2, wu, wl, dinv, lane, 3)
    arrived(moved[4], moved[5])

    wait_rows(mom_a, all_sem.at[1])
    y, info = krylov_weights(unpack(jnp.sum(mom_a[...], axis=0)))
    doubt = jnp.where(info < LIMIT, 0.0, 1.0)

    for copy, goes in sent:

        @pl.when(goes)
        def _():
            copy.wait_send()

    def adjoint_start(e, carry):
        out = []
        for g in range(2):
            acc = carry[g]
            gs = pl.ds(8 * g, 8)
            yg = [jnp.broadcast_to(y[k][8 * g:8 * g + 8], (8, 128)) for k in range(ITERS)]
            for j in range(TILES):
                sl = pl.ds(128 * j, 128)
                x = yg[0] * v0[e, gs, sl]
                for k in range(1, ITERS):
                    x = x + yg[k] * v[k][e, gs, sl]
                side = px[e, :, sl] * (x - ox[e, :, sl])
                new = side * dinv[e, gs, sl]
                state[e, gs, sl] = x
                v0[e, gs, sl] = new
                acc = acc + side * new
            out.append(acc)
        return tuple(out)

    zero = jnp.zeros((8, 128), F32)
    lax.fori_loop(0, RD, adjoint_start, (zero, zero))
    lax.fori_loop(2 * RD, EXT, adjoint_start, (zero, zero))
    accs = [list(lax.fori_loop(RD, 2 * RD, adjoint_start, (zero, zero)))]
    for k in range(ITERS):
        one, two = powers_own(v, k, wu, wl, dinv, lane)
        accs.append(one)
        if k < ITERS - 1:
            accs.append(two)
            for i in range(1, RD - k):
                powers_pair(v, k, wu, wl, dinv, lane, i)
    mom_b[me] = pack(accs)
    send_row_to_all(me, mom_b, all_sem.at[2], all_sem.at[3])

    def spread2(to):
        pltpu.make_async_remote_copy(
            src_ref=ps2.at[to], dst_ref=got2.at[me], send_sem=all_sem.at[4], recv_sem=all_sem.at[5],
            device_id=(to,), device_id_type=MESH_ID,
        ).start()
    for_peers(me, spread2)
    got2[me] = ps2[me]


    variance = 1.0 / (1.0 + eigen[...])
    below = 2.0 + 0.8 * variance
    factors = jnp.concatenate(
        [
            (2.0 - 0.8 * variance) / below,
            1.6 * variance / below,
            jnp.sqrt(6.4 * variance) / below,
            jnp.zeros((5, variance.shape[1]), F32),
            subspace[...],
        ],
        axis=0,
    )
    rank = factors.shape[1]
    row_id = lax.broadcasted_iota(jnp.int32, (rank, RD * rank), 0)
    lane_id = lax.broadcasted_iota(jnp.int32, (rank, RD * rank), 1)
    widen = jnp.where(lane_id // RD == row_id, 1.0, 0.0).astype(jnp.bfloat16)
    wide_f[...] = join_three(
        jnp.dot(in_three(factors), widen, preferred_element_type=F32), 8 + CH
    )
    row_id = lax.broadcasted_iota(jnp.int32, (RD * rank, rank), 0)
    lane_id = lax.broadcasted_iota(jnp.int32, (RD * rank, rank), 1)
    pick[...] = jnp.where(row_id == RD * lane_id, 1.0, 0.0).astype(jnp.bfloat16)

    wait_rows(mom_b, all_sem.at[3])
    y, info = krylov_weights(unpack(jnp.sum(mom_b[...], axis=0)))
    doubt = doubt + jnp.where(info < LIMIT, 0.0, 1.0)
    doubt_ref[0, 0] = jnp.sum(doubt)

    for r in range(RD):
        for h in range(4):
            sl = pl.ds(512 * h, 512)
            adj = y[0] * v0[r + RD, :, sl]
            for k in range(1, ITERS):
                adj = adj + y[k] * v[k][r + RD, :, sl]
            value = -jnp.exp(lf[r + RD, :, sl]) * adj * state[r + RD, :, sl]
            fg[pl.ds(16 * r, 16), sl] = value.astype(jnp.bfloat16)
    project(fg, bm, ps)

    def spread(to):
        pltpu.make_async_remote_copy(
            src_ref=ps.at[to // CH, pl.ds(to % CH, 1)], dst_ref=got.at[me],
            send_sem=all_sem.at[8], recv_sem=all_sem.at[9],
            device_id=(to,), device_id_type=MESH_ID,
        ).start()
    for_peers(me, spread)
    got[me] = ps[me // CH, pl.ds(me % CH, 1), :]
    wait_rows(got2, all_sem.at[5])
    sum2[me] = over_rows(jnp.sum(got2[...], axis=0))
    send_row_to_all(me, sum2, all_sem.at[6], all_sem.at[7])

    wait_rows(got, all_sem.at[9])
    sums[me] = over_rows(jnp.sum(got[...], axis=0))
    send_row_to_all(me, sums, all_sem.at[10], all_sem.at[11])
    wait_rows(sum2, all_sem.at[7])
    wait_rows(sums, all_sem.at[11])

    lane = lax.broadcasted_iota(jnp.int32, (CH, 128), 1) % RD
    pieces = []
    for b in range(8):
        rows = pl.ds(16 * b, 16)
        cols = pl.ds(128 * b, 128)
        state_coef, noise_coef = sum2[rows, 0, :], sum2[rows, 1, :]
        new = wide_f[0:1, cols] * state_coef - wide_f[1:2, cols] * sums[rows, 0, :]
        new = new + wide_f[2:3, cols] * wide_f[8 : 8 + CH, cols]
        correction = new - 0.6 * state_coef - 0.8 * noise_coef
        for x in range(RD):
            em[pl.ds(16 * x, 16), cols] = jnp.where(lane == x, correction, 0.0).astype(jnp.bfloat16)
        pieces.append(new)
    for h in range(4):
        sl = pl.ds(512 * h, 512)
        rebuilt = jnp.dot(em[...], bm[:, sl], preferred_element_type=F32)
        for x in range(RD):
            pr[x, :, sl] = 0.6 * lf[RD + x, :, sl] + 0.8 * nf[x, :, sl] + rebuilt[16 * x : 16 * x + 16]
    results = [pltpu.make_async_copy(pr.at[x], proposal.at[:, x, :], out_sem.at[x]) for x in range(RD)]
    for copy in results:
        copy.start()
    coef_ref[...] = join_three(
        jnp.dot(in_three(jnp.concatenate(pieces, axis=1)), pick[...], preferred_element_type=F32), CH
    )
    for buf, sem in ((mom_a, 0), (mom_b, 2), (got2, 4), (sum2, 6), (got, 8), (sums, 10)):
        wait_rows(buf, all_sem.at[sem])
    for copy in results:
        copy.wait()


def with_edges(value, dim):
    down = [(i, i + 1) for i in range(N - 1)]
    up = [(j, i) for i, j in down]
    length = value.shape[dim]
    before = lax.ppermute(lax.slice_in_dim(value, length - 1, length, axis=dim), AXIS, down)
    after = lax.ppermute(lax.slice_in_dim(value, 0, 1, axis=dim), AXIS, up)
    return jnp.concatenate([before, value, after], axis=dim)


def apply_operator(field, weights, diagonal):
    padded = jnp.pad(with_edges(field, 1), ((0, 0), (0, 0), (1, 1)))
    beside = weights[0] * padded[:, :-2, 1:-1] + weights[1] * padded[:, 2:, 1:-1]
    beside = beside + weights[2] * padded[:, 1:-1, :-2] + weights[3] * padded[:, 1:-1, 2:]
    return diagonal * field - beside


def chain_dot(left, right):
    return lax.psum(jnp.sum(left * right, axis=(1, 2)), AXIS)[:, None, None]


def solve_step_by_step(right_side, weights, diagonal):
    scaled = right_side / diagonal

    def step(_, carry):
        solution, residual, direction, current = carry
        applied = apply_operator(direction, weights, diagonal)
        length = current / chain_dot(direction, applied)
        solution = solution + length * direction
        residual = residual - length * applied
        scaled = residual / diagonal
        following = chain_dot(residual, scaled)
        return solution, residual, scaled + (following / current) * direction, following

    start = (jnp.zeros_like(scaled), right_side, scaled, chain_dot(right_side, scaled))
    return lax.fori_loop(0, ITERS, step, start)[0]


def step_by_step(
    source, observed, precision, conductivity, log_field, noise_field, subspace_noise, eigenvalues, basis,
):
    position = lax.axis_index(AXIS)
    edges = with_edges(conductivity, 0)
    upper = jnp.where(position == 0, conductivity[:1], edges[:1])
    lower = jnp.where(position == N - 1, conductivity[-1:], edges[-1:])
    padded = jnp.pad(jnp.concatenate([upper, conductivity, lower], 0), ((0, 0), (1, 1)), mode="edge")
    weights = (
        0.5 * (conductivity + padded[:-2, 1:-1]),
        0.5 * (conductivity + padded[2:, 1:-1]),
        0.5 * (conductivity + padded[1:-1, :-2]),
        0.5 * (conductivity + padded[1:-1, 2:]),
    )
    reaction = jnp.exp(log_field)
    diagonal = weights[0] + weights[1] + weights[2] + weights[3] + reaction

    def solve(_, carry):
        side, _, latest = carry
        found = solve_step_by_step(side, weights, diagonal)
        return precision * (found - observed), latest, found

    side = jnp.broadcast_to(source, log_field.shape)
    zeros = jnp.zeros_like(log_field)
    _, state, adjoint = lax.fori_loop(0, 2, solve, (side, zeros, zeros))
    gradient = -reaction * adjoint * state
    fields = jnp.concatenate([log_field, noise_field, gradient], 0).astype(jnp.bfloat16)
    coefs = lax.psum(jnp.einsum("cxy,rxy->cr", fields, basis, preferred_element_type=F32), AXIS)
    state_coef, noise_coef, grad_coef = coefs[:CH], coefs[CH : 2 * CH], coefs[2 * CH :]
    variance = 1.0 / (1.0 + eigenvalues)
    below = 2.0 + 0.8 * variance
    new_coef = (2.0 - 0.8 * variance) / below * state_coef - 1.6 * variance / below * grad_coef
    new_coef = new_coef + jnp.sqrt(6.4 * variance) / below * subspace_noise
    correction = (new_coef - 0.6 * state_coef - 0.8 * noise_coef).astype(jnp.bfloat16)
    rebuilt = jnp.einsum("cr,rxy->cxy", correction, basis, preferred_element_type=F32)
    return 0.6 * log_field + 0.8 * noise_field + rebuilt, new_coef


def per_device(
    source, observed, precision, conductivity, log_field, noise_field, subspace_noise, eigenvalues, basis,
):
    any_space = pl.BlockSpec(memory_space=pltpu.HBM)
    vmem = pl.BlockSpec(memory_space=pltpu.VMEM)
    rank = eigenvalues.shape[0]
    wide = pltpu.VMEM((EXT, CH, NY), F32)
    row8 = pltpu.VMEM((EXT, 8, NY), F32)
    small = pltpu.VMEM((3, RD, NY), F32)
    one = pltpu.VMEM((N, 1, 128), F32)
    two = pltpu.VMEM((N, 2, 128), F32)
    half = jnp.bfloat16
    proposal, new_coef, doubt = pl.pallas_call(
        step_kernel,
        out_shape=(
            jax.ShapeDtypeStruct(log_field.shape, F32),
            jax.ShapeDtypeStruct((CH, rank), F32),
            jax.ShapeDtypeStruct((1, 1), F32),
        ),
        in_specs=[any_space] * 9,
        out_specs=(any_space, vmem, pl.BlockSpec(memory_space=pltpu.SMEM)),
        scratch_shapes=[
            wide, wide, wide, wide, wide, wide,
            pltpu.VMEM((EXT + 1, 8, NY), F32), row8, row8, row8, row8, row8, wide,
            pltpu.VMEM((5, RD, NY), F32), small, small, small, one, one,
            pltpu.VMEM((RD, CH, NY), F32),
            pltpu.VMEM((RD * rank, NY), half),
            pltpu.VMEM((2 * RD * CH, NY), half),
            pltpu.VMEM((RD * CH, NY), half),
            two, two, two,
            pltpu.VMEM((8, CH, 128), F32), one, one,
            pltpu.VMEM((8 + CH, RD * rank), F32),
            pltpu.VMEM((RD * rank, rank), half),
            pltpu.VMEM((RD * CH, RD * rank), half),
            pltpu.VMEM((RD, CH, NY), F32),
            pltpu.VMEM((CH, rank), F32), pltpu.VMEM((1, rank), F32),
            pltpu.SemaphoreType.DMA((7,)),
            pltpu.SemaphoreType.DMA((24,)),
            pltpu.SemaphoreType.DMA((24,)),
            pltpu.SemaphoreType.DMA((12,)),
            pltpu.SemaphoreType.DMA((8,)),
            pltpu.SemaphoreType.DMA((4,)),
            pltpu.SemaphoreType.REGULAR((2,)),
        ],
        compiler_params=pltpu.CompilerParams(
            collective_id=0, has_side_effects=True, vmem_limit_bytes=66_900_000
        ),
    )(
        source, observed, precision, conductivity, log_field, noise_field,
        subspace_noise, eigenvalues.reshape(1, rank), basis,
    )
    return lax.cond(
        doubt[0, 0] > 0.0,
        lambda: step_by_step(
            source, observed, precision, conductivity, log_field, noise_field, subspace_noise,
            eigenvalues, basis,
        ),
        lambda: (proposal, new_coef),
    )


def solution(mesh):
    return jax.shard_map(
        per_device,
        mesh=mesh,
        in_specs=(
            P(AXIS, None), P(AXIS, None), P(AXIS, None), P(AXIS, None),
            P(None, AXIS, None), P(None, AXIS, None), P(), P(), P(None, AXIS, None),
        ),
        out_specs=(P(None, AXIS, None), P()),
        check_vma=False,
    )
```
